32 devices in a mesh: dp: 16 (over z, y, x), mp: 2 (over core).
Axes of the slice: x: 2, y: 2, z: 4, core: 2. Of those that a mesh axis runs over, the one named last changes fastest.
Arguments:
- inputs: bfloat16 [16, 1024, 768], P('dp'), may hold values from -6 to 6
- time_embed: float32 [16, 768], P('dp'), may hold values from -3 to 3
- targets: bfloat16 [16, 1024, 768], P('dp'), may hold values from -6 to 6
- timesteps: int32 [16], P('dp'), may hold values from 0 to 1999
- ln1_gain: float32 [768], replicated, may hold values from 0.1 to 1.9
- ln1_bias: float32 [768], replicated, may hold values from -0.1 to 0.1
- qkv_weight: bfloat16 [768, 3, 768], P(None, None, 'mp'), may hold values from -0.21875 to 0.21875
- qv_bias: float32 [2, 768], P(None, 'mp'), may hold values from -3 to 3
- out_weight: bfloat16 [768, 768], P('mp'), may hold values from -1.75 to 1.75
- out_bias: float32 [768], replicated, may hold values from -0.25 to 0.25
- ln2_gain: float32 [768], replicated, may hold values from 0.1 to 1.9
- ln2_bias: float32 [768], replicated, may hold values from -0.5 to 0.5
- up_weight: bfloat16 [768, 3072], P(None, 'mp'), may hold values from -0.21875 to 0.21875
- up_bias: float32 [3072], P('mp'), may hold values from -0.25 to 0.25
- down_weight: bfloat16 [3072, 768], P('mp'), may hold values from -0.109375 to 0.109375
- down_bias: float32 [768], replicated, may hold values from -0.25 to 0.25
Outputs:
- out_act: bfloat16 [16, 1024, 768], P('dp')
- grad_input: float32 [16, 1024, 768], P('dp')
- grad_time: float32 [16, 768], P('dp')
- grad_ln1_gain: float32 [768], replicated
- grad_ln1_bias: float32 [768], replicated
- grad_qkv: float32 [768, 3, 768], P('dp', None, 'mp')
- grad_qv_bias: float32 [2, 768], P(None, 'mp')
- grad_out: float32 [768, 768], P('mp', 'dp')
- grad_out_bias: float32 [768], replicated
- grad_ln2_gain: float32 [768], replicated
- grad_ln2_bias: float32 [768], replicated
- grad_up: float32 [768, 3072], P('dp', 'mp')
- grad_up_bias: float32 [3072], P('mp')
- grad_down: float32 [3072, 768], P('mp', 'dp')
- grad_down_bias: float32 [768], replicated
- bucket_counts: int32 [4], replicated
The draws below stay inside these ranges and needn't reach their ends.
All inputs are finite; a program needn't handle non-finite values.
Results may differ from the reference program's by a relative error of at most 0.0055.
Values sent between devices are 32-bit elements; how exact they have to be, the bound alone decides.
No kernel may reach another device: no remote copies, remote signals or barrier semaphores. Data moves between devices by JAX's collectives and lax.ppermute only.
A program may use at most 192 MiB of HBM per device.

```python
import math
import jax
import jax.numpy as jnp
from jax import lax

D = 768
HEADS = 12
HD = 64
FF = 3072
LEN = 1024
NSTEPS = 2000
NB = 4
SEQS = 16


def draw_timesteps(key, part):
    base_key = jax.random.fold_in(key, 11)
    split_key = jax.random.fold_in(key, 12)
    spot_key = jax.random.fold_in(key, 13)
    base = jax.random.randint(base_key, (SEQS,), 0, NSTEPS)
    divisor = jax.random.randint(split_key, (SEQS,), 1, 17)
    steps = base // divisor
    where_top = jax.random.randint(spot_key, (), 0, SEQS)
    return jnp.where(jnp.arange(SEQS) == where_top, NSTEPS - 1, steps).astype(jnp.int32)


def unit_noise(key, shape):
    return jax.random.normal(key, shape, jnp.float32)


def signal_pair(key):
    first_key = jax.random.fold_in(key, 21)
    second_key = jax.random.fold_in(key, 22)
    shape = (SEQS, LEN, D)
    source = jnp.clip(unit_noise(first_key, shape), -6.0, 6.0)
    wanted = jnp.clip(-source + 0.3 * unit_noise(second_key, shape), -6.0, 6.0)
    return (source, wanted)


def draw_inputs(key, part):
    return signal_pair(key)[0].astype(jnp.bfloat16)


def draw_targets(key, part):
    return signal_pair(key)[1].astype(jnp.bfloat16)


def draw_qv_bias(key, part):
    bias_key = jax.random.fold_in(key, 31)
    raw = unit_noise(bias_key, (2, D))
    scales = jnp.array([0.5, 0.02], jnp.float32)[:, None]
    return jnp.clip(raw * scales, -3.0, 3.0)


def block_scale(rng, shape, shards, low, high):
    gain, own = 1.0, jax.random.fold_in(rng, 6)
    for axis_at, shards_of in shards:
        steps = jnp.exp(jax.random.uniform(jax.random.fold_in(own, axis_at), (shards_of,), jnp.float32, low / len(shards), high / len(shards)))
        gain = gain * jnp.repeat(steps, shape[axis_at] // shards_of).reshape([-1 if axis == axis_at else 1 for axis in range(len(shape))])
    return gain


def noise(key, shape, scale, limit, shards=(), kind=jnp.bfloat16):
    factor_of = block_scale(key, shape, shards, -0.22, 0.18) if shards else 1.0
    entries = jax.random.normal(key, shape, jnp.float32) * scale * factor_of
    return jnp.minimum(jnp.maximum(entries, -limit), limit).astype(kind)


def setup_inputs(seed: int = 0) -> dict:
    arg_keys = jax.random.split(jax.random.key(seed), 17)
    inputs = draw_inputs(jax.random.fold_in(arg_keys[16], 71), 0)
    time_embed = noise(arg_keys[1], (SEQS, D), 0.2, 3.0, ((0, 16),), jnp.float32)
    targets = draw_targets(jax.random.fold_in(arg_keys[16], 71), 0)
    timesteps = draw_timesteps(jax.random.fold_in(arg_keys[16], 71), 0)
    ln1_gain = jnp.clip(1.0 + 0.18 * jax.random.normal(arg_keys[4], (D,), jnp.float32), 0.1, 1.9)
    ln1_bias = noise(arg_keys[5], (D,), 0.02, 0.1, (), jnp.float32)
    qkv_weight = noise(arg_keys[6], (D, 3, D), D ** -0.5, 0.21875, ((2, 2),))
    qv_bias = draw_qv_bias(jax.random.fold_in(arg_keys[16], 71), 0)
    out_weight = noise(arg_keys[8], (D, D), (D // 64) ** -0.5, 1.75, ((0, 2),))
    out_bias = noise(arg_keys[9], (D,), 0.05, 0.25, (), jnp.float32)
    ln2_gain = jnp.clip(1.0 + 0.18 * jax.random.normal(arg_keys[10], (D,), jnp.float32), 0.1, 1.9)
    ln2_bias = noise(arg_keys[11], (D,), 0.1, 0.5, (), jnp.float32)
    up_weight = noise(arg_keys[12], (D, FF), D ** -0.5, 0.21875, ((1, 2),))
    up_bias = noise(arg_keys[13], (FF,), 0.05, 0.25, ((0, 2),), jnp.float32)
    down_weight = noise(arg_keys[14], (FF, D), FF ** -0.5, 0.109375, ((0, 2),))
    down_bias = noise(arg_keys[15], (D,), 0.05, 0.25, (), jnp.float32)
    return {"inputs": inputs, "time_embed": time_embed, "targets": targets, "timesteps": timesteps, "ln1_gain": ln1_gain, "ln1_bias": ln1_bias, "qkv_weight": qkv_weight, "qv_bias": qv_bias, "out_weight": out_weight, "out_bias": out_bias, "ln2_gain": ln2_gain, "ln2_bias": ln2_bias, "up_weight": up_weight, "up_bias": up_bias, "down_weight": down_weight, "down_bias": down_bias}


highest = lax.Precision.HIGHEST
epsilon = 1e-05

@jax.custom_vjp
def low(v):
    return lax.optimization_barrier(v.astype(jnp.bfloat16)).astype(jnp.float32)

@jax.custom_vjp
def low_back(v):
    return v

def low_keep(v):
    return (low(v), None)

def low_pass(kept, grad):
    return (grad,)

def back_keep(v):
    return (v, None)

def back_low(kept, grad):
    return (low(grad),)
low.defvjp(low_keep, low_pass)
low_back.defvjp(back_keep, back_low)

def layer_norm(source, scaling, offset):
    row_mean = lax.optimization_barrier(jnp.mean(source, axis=-1, keepdims=True))
    centred = source - row_mean
    variance = lax.optimization_barrier(jnp.mean(centred * centred, axis=-1, keepdims=True))
    return centred * lax.rsqrt(variance + epsilon) * scaling + offset

def attend(queries, keyset, values):
    scores = low_back(jnp.einsum('bqhe,bkhe->bhqk', queries, keyset, precision=highest) * (1.0 / math.sqrt(HD)))
    attn_probs = jax.nn.softmax(scores, axis=-1)
    return jnp.einsum('bhqk,bkhe->bqhe', low(attn_probs), values, precision=highest)

def forward(params, source, time_rows):
    ln1_gain, ln1_bias, qkv_weight, qv_bias, out_weight, out_bias, ln2_gain, ln2_bias, up_weight, up_bias, down_weight, down_bias = params
    batch_size = source.shape[0]
    head_shape = (batch_size, LEN, HEADS, HD)
    residual = source + time_rows[:, None, :]
    attn_in = low(layer_norm(residual, ln1_gain, ln1_bias))
    projected = low_back(jnp.einsum('bld,dsk->blsk', attn_in, qkv_weight, precision=highest))
    queries = low(projected[:, :, 0] + qv_bias[0]).reshape(head_shape)
    keyset = low(projected[:, :, 1]).reshape(head_shape)
    values = low(projected[:, :, 2] + qv_bias[1]).reshape(head_shape)
    span_rows = min(512, LEN)
    span_count = LEN // span_rows
    pieces = jnp.moveaxis(queries.reshape(batch_size, span_count, span_rows, HEADS, HD), 1, 0)
    attended = lax.map(jax.checkpoint(lambda query_piece: attend(query_piece, keyset, values)), pieces)
    mixed_heads = low(low_back(jnp.moveaxis(attended, 0, 1).reshape(batch_size, LEN, D)))
    mid_state = residual + low_back(jnp.einsum('bld,de->ble', mixed_heads, out_weight, precision=highest)) + out_bias
    ffn_in = low(layer_norm(mid_state, ln2_gain, ln2_bias))
    preact = low_back(jnp.einsum('bld,df->blf', ffn_in, up_weight, precision=highest)) + up_bias
    activated = low(jax.nn.gelu(preact, approximate=False))
    return mid_state + low_back(jnp.einsum('blf,fd->bld', activated, down_weight, precision=highest)) + down_bias

def reference(inputs, time_embed, targets, timesteps, ln1_gain, ln1_bias, qkv_weight, qv_bias, out_weight, out_bias, ln2_gain, ln2_bias, up_weight, up_bias, down_weight, down_bias):
    buckets = (timesteps >= NSTEPS // 64).astype(jnp.int32) + (timesteps >= NSTEPS // 16).astype(jnp.int32) + (timesteps >= NSTEPS // 4).astype(jnp.int32)
    one_hot = buckets[:, None] == jnp.arange(NB, dtype=jnp.int32)[None, :]
    bucket_counts = lax.optimization_barrier(jnp.sum(one_hot.astype(jnp.int32), axis=0))
    floors = jnp.maximum(bucket_counts, 1).astype(jnp.float32)
    seq_weight = SEQS / (NB * lax.optimization_barrier(jnp.sum(jnp.where(one_hot, floors[None, :], 0.0), axis=1)))
    params = tuple((param.astype(jnp.float32) for param in (ln1_gain, ln1_bias, qkv_weight, qv_bias, out_weight, out_bias, ln2_gain, ln2_bias, up_weight, up_bias, down_weight, down_bias)))
    group_size = max(1, min(SEQS, 4096 // LEN))
    while SEQS % group_size != 0:
        group_size = group_size - 1
    group_count = SEQS // group_size

    def regroup(array):
        return array.reshape((group_count, group_size) + array.shape[1:])

    def one_group(running, group_item):
        source_rows, target_rows, time_rows, weight_rows = group_item

        def objective(params, source, time_part):
            out32 = forward(params, source, time_part)
            misfit = out32 - target_rows.astype(jnp.float32)
            return (jnp.sum(weight_rows[:, None, None] * 0.5 * misfit * misfit), out32)
        loss_value, pullback, out32 = jax.vjp(objective, params, source_rows.astype(jnp.float32), time_rows, has_aux=True)
        grad_params, grad_source, grad_times = pullback(jnp.ones_like(loss_value))
        running = jax.tree.map(lambda former, latter: former + latter, running, grad_params)
        return (running, (out32.astype(jnp.bfloat16), grad_source, grad_times))
    zero_grads = jax.tree.map(jnp.zeros_like, params)
    totals, (out_act, grad_input, grad_time) = lax.scan(one_group, zero_grads, (regroup(inputs), regroup(targets), regroup(time_embed), regroup(seq_weight)))
    return (out_act.reshape(SEQS, LEN, D), grad_input.reshape(SEQS, LEN, D), grad_time.reshape(SEQS, D), totals[0], totals[1], totals[2], totals[3], totals[4], totals[5], totals[6], totals[7], totals[8], totals[9], totals[10], totals[11], bucket_counts)
```

```python
import math

import jax
import jax.numpy as jnp
from jax import lax
from jax.sharding import PartitionSpec as P

HD = 64
NSTEPS = 2000
NB = 4


epsilon = 1e-05


def normalize(source, scaling, offset):
    row_mean = jnp.mean(source, axis=-1, keepdims=True)
    centred = source - row_mean
    variance = jnp.mean(centred * centred, axis=-1, keepdims=True)
    inv_std = lax.rsqrt(variance + epsilon)
    normed = centred * inv_std
    return (normed * scaling + offset, normed, inv_std)


def norm_back(upstream, normed, inv_std, scaling):
    scaled = upstream * scaling
    inner_part = (
        scaled
        - jnp.mean(scaled, axis=-1, keepdims=True)
        - normed * jnp.mean(scaled * normed, axis=-1, keepdims=True)
    )
    return (inv_std * inner_part, jnp.sum(upstream * normed, axis=0), jnp.sum(upstream, axis=0))


def pair_sum(value):
    size = lax.axis_size("mp")
    if size != 2:
        return lax.psum(value, "mp")
    return value + lax.ppermute(value, "mp", [(0, 1), (1, 0)])


def xor_pairs(size, bit):
    return [(index, index ^ bit) for index in range(size)]


def axis_bits(size):
    return [1 << place for place in range(size.bit_length() - 1)]


def double_sum(value):
    size = lax.axis_size("dp")
    if size & (size - 1):
        return lax.psum(value, "dp")
    for bit in axis_bits(size):
        value = value + lax.ppermute(value, "dp", xor_pairs(size, bit))
    return value


def section_orders(size):
    bits = axis_bits(size)
    if len(bits) == 4:
        x_bit, y_bit, z_low, z_high = bits
        return [
            [x_bit, y_bit, z_low, z_high],
            [y_bit, x_bit, z_low, z_high],
            [z_low, x_bit, y_bit, z_high],
        ]
    third = max(1, len(bits) // 3)
    return [bits[start:] + bits[:start] for start in (0, third, 2 * third)]


def halve(section, order, size):
    me = lax.axis_index("dp")
    left = sorted(order, reverse=True)
    rows, columns = section.shape
    section = section.reshape((2,) * len(left) + (rows // size, columns))
    for bit in order:
        at = left.index(bit)
        mine = (me // bit) % 2
        send = lax.dynamic_index_in_dim(section, 1 - mine, at, keepdims=False)
        keep = lax.dynamic_index_in_dim(section, mine, at, keepdims=False)
        section = keep + lax.ppermute(send, "dp", xor_pairs(size, bit))
        left.remove(bit)
    return section


def scatter_rows(grad):
    size = lax.axis_size("dp")
    if size & (size - 1):
        return lax.psum_scatter(grad, "dp", scatter_dimension=0, tiled=True)
    orders = section_orders(size)
    width = grad.shape[1] // len(orders)
    parts = [
        halve(grad[:, place * width : (place + 1) * width], order, size)
        for place, order in enumerate(orders)
    ]
    return jnp.concatenate(parts, axis=1)


def local(
    inputs,
    time_embed,
    targets,
    timesteps,
    ln1_gain,
    ln1_bias,
    qkv_weight,
    qv_bias,
    out_weight,
    out_bias,
    ln2_gain,
    ln2_bias,
    up_weight,
    up_bias,
    down_weight,
    down_bias,
):
    seq_count, length, model_width = inputs.shape
    tok_rows = seq_count * length
    local_width = qkv_weight.shape[2]
    heads_local = local_width // HD
    score_scale = 1.0 / math.sqrt(HD)
    head_shape = (seq_count, length, heads_local, HD)
    buckets = (
        (timesteps >= NSTEPS // 64).astype(jnp.int32)
        + (timesteps >= NSTEPS // 16).astype(jnp.int32)
        + (timesteps >= NSTEPS // 4).astype(jnp.int32)
    )
    one_hot = buckets[:, None] == jnp.arange(NB, dtype=jnp.int32)[None, :]
    bucket_counts = double_sum(jnp.sum(one_hot.astype(jnp.int32), axis=0))
    floors = jnp.maximum(bucket_counts, 1).astype(jnp.float32)
    total_seqs = seq_count * lax.axis_size("dp")
    seq_weight = total_seqs / (NB * jnp.sum(jnp.where(one_hot, floors[None, :], 0.0), axis=1))
    residual = (inputs.astype(jnp.float32) + time_embed[:, None, :]).reshape(tok_rows, model_width)
    first_out, first_normed, first_inv = normalize(residual, ln1_gain, ln1_bias)
    attn_in = first_out.astype(jnp.bfloat16)
    projected = jnp.einsum("td,dsk->tsk", attn_in, qkv_weight, preferred_element_type=jnp.float32)
    queries = (projected[:, 0] + qv_bias[0]).astype(jnp.bfloat16).reshape(head_shape)
    keyset = projected[:, 1].astype(jnp.bfloat16).reshape(head_shape)
    values = (projected[:, 2] + qv_bias[1]).astype(jnp.bfloat16).reshape(head_shape)
    span_rows = min(512, length)
    span_count = length // span_rows

    def scores_of(position):
        query_piece = queries[:, position * span_rows : (position + 1) * span_rows]
        scores = (
            jnp.einsum("bqhe,bkhe->bhqk", query_piece, keyset, preferred_element_type=jnp.float32)
            * score_scale
        )
        return (query_piece, scores)

    mixed_parts = []
    log_totals = []
    for position in range(span_count):
        query_piece, scores = scores_of(position)
        row_max = jnp.max(scores, axis=-1, keepdims=True)
        expo_vals = jnp.exp(scores - row_max)
        row_total = jnp.sum(expo_vals, axis=-1, keepdims=True)
        attn_probs = expo_vals / row_total
        log_totals.append(row_max + jnp.log(row_total))
        mixed_parts.append(
            jnp.einsum(
                "bhqk,bkhe->bqhe",
                attn_probs.astype(jnp.bfloat16),
                values,
                preferred_element_type=jnp.float32,
            )
        )
    mixed_heads = (
        jnp.concatenate(mixed_parts, axis=1).reshape(tok_rows, local_width).astype(jnp.bfloat16)
    )
    attn_sum = pair_sum(jnp.dot(mixed_heads, out_weight, preferred_element_type=jnp.float32))
    mid_state = residual + attn_sum + out_bias
    second_out, second_normed, second_inv = normalize(mid_state, ln2_gain, ln2_bias)
    ffn_in = second_out.astype(jnp.bfloat16)
    preact = jnp.dot(ffn_in, up_weight, preferred_element_type=jnp.float32) + up_bias
    gelu_value, gelu_back = jax.vjp(
        lambda inner_arg: jax.nn.gelu(inner_arg, approximate=False), preact
    )
    activated = gelu_value.astype(jnp.bfloat16)
    ffn_sum = pair_sum(jnp.dot(activated, down_weight, preferred_element_type=jnp.float32))
    final_state = mid_state + ffn_sum + down_bias
    out_act = final_state.astype(jnp.bfloat16).reshape(seq_count, length, model_width)
    misfit = final_state.reshape(seq_count, length, model_width) - targets.astype(jnp.float32)
    out_grad = (misfit * seq_weight[:, None, None]).reshape(tok_rows, model_width)
    out_grad_low = out_grad.astype(jnp.bfloat16)
    grad_down = jnp.einsum("td,tf->df", out_grad_low, activated, preferred_element_type=jnp.float32)
    pre_grad = gelu_back(
        jnp.einsum("td,fd->tf", out_grad_low, down_weight, preferred_element_type=jnp.float32)
    )[0]
    pre_grad_low = pre_grad.astype(jnp.bfloat16)
    grad_up = jnp.einsum("td,tf->df", ffn_in, pre_grad_low, preferred_element_type=jnp.float32)
    ffn_grad = pair_sum(
        jnp.einsum("tf,df->td", pre_grad_low, up_weight, preferred_element_type=jnp.float32)
    )
    mid_back, grad_ln2_gain, grad_ln2_bias = norm_back(
        ffn_grad, second_normed, second_inv, ln2_gain
    )
    mid_grad = out_grad + mid_back
    mid_grad_low = mid_grad.astype(jnp.bfloat16)
    grad_out = jnp.einsum(
        "td,tk->dk", mid_grad_low, mixed_heads, preferred_element_type=jnp.float32
    )
    mixed_grad = (
        jnp.einsum("td,kd->tk", mid_grad_low, out_weight, preferred_element_type=jnp.float32)
        .astype(jnp.bfloat16)
        .reshape(head_shape)
    )
    key_grad = jnp.zeros(head_shape, jnp.float32)
    value_grad = jnp.zeros(head_shape, jnp.float32)
    query_parts = []
    for position in range(span_count):
        query_piece, scores = scores_of(position)
        attn_probs = jnp.exp(scores - log_totals[position])
        grad_piece = mixed_grad[:, position * span_rows : (position + 1) * span_rows]
        prob_grad = jnp.einsum(
            "bqhe,bkhe->bhqk", grad_piece, values, preferred_element_type=jnp.float32
        )
        row_dot = jnp.sum(prob_grad * attn_probs, axis=-1, keepdims=True)
        score_grad = (attn_probs * (prob_grad - row_dot)).astype(jnp.bfloat16)
        query_parts.append(
            jnp.einsum("bhqk,bkhe->bqhe", score_grad, keyset, preferred_element_type=jnp.float32)
            * score_scale
        )
        key_grad = (
            key_grad
            + jnp.einsum(
                "bhqk,bqhe->bkhe", score_grad, query_piece, preferred_element_type=jnp.float32
            )
            * score_scale
        )
        value_grad = value_grad + jnp.einsum(
            "bhqk,bqhe->bkhe",
            attn_probs.astype(jnp.bfloat16),
            grad_piece,
            preferred_element_type=jnp.float32,
        )
    query_grad = jnp.concatenate(query_parts, axis=1).reshape(tok_rows, local_width)
    key_flat = key_grad.reshape(tok_rows, local_width)
    value_flat = value_grad.reshape(tok_rows, local_width)
    qv_bias_grad = jnp.stack([jnp.sum(query_grad, axis=0), jnp.sum(value_flat, axis=0)])
    proj_grad = jnp.stack([query_grad, key_flat, value_flat], axis=1).astype(jnp.bfloat16)
    grad_qkv = jnp.einsum("td,tsk->dsk", attn_in, proj_grad, preferred_element_type=jnp.float32)
    attn_grad = pair_sum(
        jnp.einsum("tsk,dsk->td", proj_grad, qkv_weight, preferred_element_type=jnp.float32)
    )
    input_back, grad_ln1_gain, grad_ln1_bias = norm_back(
        attn_grad, first_normed, first_inv, ln1_gain
    )
    input_grad = (mid_grad + input_back).reshape(seq_count, length, model_width)
    grad_time = jnp.sum(input_grad, axis=1)
    early = [
        jnp.sum(mid_grad, axis=0),
        grad_ln2_gain,
        grad_ln2_bias,
        jnp.sum(pre_grad, axis=0),
        jnp.sum(out_grad, axis=0),
    ]
    late = [grad_ln1_gain, grad_ln1_bias, qv_bias_grad.reshape(-1)]
    early_sum = double_sum(jnp.concatenate(early))
    late_sum = double_sum(jnp.concatenate(late))
    w = model_width
    hidden = up_weight.shape[1]
    small_sums = (
        late_sum[:w],
        late_sum[w : 2 * w],
        late_sum[2 * w :].reshape(2, local_width),
        early_sum[:w],
        early_sum[w : 2 * w],
        early_sum[2 * w : 3 * w],
        early_sum[3 * w : 3 * w + hidden],
        early_sum[3 * w + hidden :],
    )
    grad_qkv_part = scatter_rows(grad_qkv.reshape(w, 3 * local_width)).reshape(-1, 3, local_width)
    grad_out_part = scatter_rows(grad_out).T
    grad_up_part = scatter_rows(grad_up)
    grad_down_part = scatter_rows(grad_down).T
    return (
        out_act,
        input_grad,
        grad_time,
        small_sums[0],
        small_sums[1],
        grad_qkv_part,
        small_sums[2],
        grad_out_part,
        small_sums[3],
        small_sums[4],
        small_sums[5],
        grad_up_part,
        small_sums[6],
        grad_down_part,
        small_sums[7],
        bucket_counts,
    )


def solution(mesh):
    in_specs = (
        P("dp", None, None),
        P("dp", None),
        P("dp", None, None),
        P("dp"),
        P(),
        P(),
        P(None, None, "mp"),
        P(None, "mp"),
        P("mp", None),
        P(),
        P(),
        P(),
        P(None, "mp"),
        P("mp"),
        P("mp", None),
        P(),
    )
    out_specs = (
        P("dp", None, None),
        P("dp", None, None),
        P("dp", None),
        P(),
        P(),
        P("dp", None, "mp"),
        P(None, "mp"),
        P("mp", "dp"),
        P(),
        P(),
        P(),
        P("dp", "mp"),
        P("mp"),
        P("mp", "dp"),
        P(),
        P(),
    )
    return jax.shard_map(local, mesh=mesh, in_specs=in_specs, out_specs=out_specs, check_vma=False)
```

```python
import functools
import math

import jax
import jax.numpy as jnp
from jax import lax
from jax.experimental import pallas as pl
from jax.experimental.pallas import tpu as pltpu
from jax.sharding import PartitionSpec as P

HD = 64
NSTEPS = 2000
NB = 4
BLOCK = 256
PAIR = 2 * HD
VMEM_BYTES = 56 * 2**20

epsilon = 1e-05
F32 = jnp.float32
BF16 = jnp.bfloat16
NT = (((1,), (1,)), ((), ()))


def dot(left, right):
    return jnp.dot(left, right, preferred_element_type=F32)


def dot_nt(left, right):
    return lax.dot_general(left, right, NT, preferred_element_type=F32)


def row_mean(value):
    return jnp.mean(value, axis=-1, keepdims=True)


def column_sum(value):
    return jnp.sum(value, axis=0, keepdims=True)


def normed_of(source):
    centred = source - row_mean(source)
    inv_std = lax.rsqrt(row_mean(centred * centred) + epsilon)
    return centred * inv_std, inv_std


def accumulate(ref, value, first):
    @pl.when(first)
    def _():
        ref[...] = value

    @pl.when(jnp.logical_not(first))
    def _():
        ref[...] += value


def project_kernel(x_ref, time_ref, gain_ref, bias_ref, w_ref, qvb_ref, q_ref, k_ref, v_ref, at_ref):
    residual = x_ref[...].astype(F32) + time_ref[...]
    normed, _ = normed_of(residual)
    attn_in = (normed * gain_ref[...] + bias_ref[...]).astype(BF16)
    at_ref[...] = attn_in.T
    q_ref[...] = (dot(attn_in, w_ref[0]) + qvb_ref[0:1]).astype(BF16)
    k_ref[...] = dot(attn_in, w_ref[1]).astype(BF16)
    v_ref[...] = (dot(attn_in, w_ref[2]) + qvb_ref[1:2]).astype(BF16)


def head_mask(shape, head):
    lane = lax.broadcasted_iota(jnp.int32, shape, 1)
    return (lane >= HD) if head else (lane < HD)


def keep_head(value, head):
    return jnp.where(head_mask(value.shape, head), value, jnp.zeros_like(value))


EXP_SCALE = math.log2(math.e) / math.sqrt(HD)


def attend_kernel(q_ref, k_ref, v_ref, ow_ref, *refs):
    part_ref, mixed_ref, lse_ref, vt_ref = refs[-4:]

    @pl.when(pl.program_id(0) == 0)
    def _():
        vt_ref[...] = v_ref[...].T

    rows, width = q_ref.shape
    pieces = []
    stats = []
    for pair in range(width // PAIR):
        at = slice(pair * PAIR, (pair + 1) * PAIR)
        keys = k_ref[:, at]
        queries = q_ref[:, at]
        for head in range(2):
            scores = dot_nt(keys, keep_head(queries, head))
            top = jnp.max(scores, axis=0, keepdims=True)
            expo = jnp.exp2((scores - top) * EXP_SCALE)
            total = column_sum(expo)
            start = pair * PAIR + head * HD
            mixed = dot(vt_ref[start : start + HD, :], expo.astype(BF16))
            pieces.append(mixed * (1.0 / total))
            stats.append(top * EXP_SCALE + jnp.log2(total))
    while len(stats) < lse_ref.shape[0]:
        stats.append(jnp.zeros_like(stats[0]))
    lse_ref[...] = jnp.concatenate(stats, axis=0)
    mixed_heads = jnp.concatenate(pieces, axis=0).T.astype(BF16)
    mixed_ref[...] = mixed_heads
    part_ref[...] = dot(mixed_heads, ow_ref[...])


def normal_parts(v):
    size = jnp.abs(v)
    t = 1.0 / (1.0 + 0.2316419 * size)
    poly = t * (
        0.319381530
        + t * (-0.356563782 + t * (1.781477937 + t * (-1.821255978 + t * 1.330274429)))
    )
    density = jnp.exp2(v * v * (-0.5 * math.log2(math.e))) * (1.0 / math.sqrt(2.0 * math.pi))
    tail = poly * density
    return jnp.where(v < 0.0, tail, 1.0 - tail), density


def feed_kernel(
    x_ref, time_ref, own_ref, got_ref, ob_ref, gain_ref, bias_ref, uw_ref, ub_ref, dw_ref, *refs
):
    part_ref, mid_ref, ft_ref, act_ref, slope_ref = refs[-5:]
    mid = x_ref[...].astype(F32) + time_ref[...] + (own_ref[...] + got_ref[...]) + ob_ref[...]
    mid_ref[...] = mid
    normed, _ = normed_of(mid)
    ffn_in = (normed * gain_ref[...] + bias_ref[...]).astype(BF16)
    ft_ref[...] = ffn_in.T
    preact = dot(ffn_in, uw_ref[...]) + ub_ref[...]
    phi, density = normal_parts(preact)
    activated = (preact * phi).astype(BF16)
    act_ref[...] = activated
    slope_ref[...] = phi + preact * density
    part_ref[...] = dot(activated, dw_ref[...])


def loss_kernel(mid_ref, own_ref, got_ref, db_ref, goal_ref, weight_ref, *refs):
    sum_ref, out_ref, og_ref, low_ref, lt_ref = refs[-5:]
    final = mid_ref[...] + (own_ref[...] + got_ref[...]) + db_ref[...]
    out_ref[...] = final.astype(BF16)
    out_grad = (final - goal_ref[...].astype(F32)) * weight_ref[0, 0]
    og_ref[...] = out_grad
    low = out_grad.astype(BF16)
    low_ref[...] = low
    lt_ref[...] = low.T
    accumulate(sum_ref, column_sum(out_grad), pl.program_id(0) == 0)


def back_feed_kernel(low_ref, slope_ref, uw_ref, dw_ref, pre_ref, part_ref, sum_ref):
    pre_grad = slope_ref[...] * dot_nt(low_ref[...], dw_ref[...])
    accumulate(sum_ref, column_sum(pre_grad), pl.program_id(0) == 0)
    low = pre_grad.astype(BF16)
    pre_ref[...] = low
    part_ref[...] = dot_nt(low, uw_ref[...])


def back_mid_kernel(
    mid_ref, own_ref, got_ref, og_ref, gain_ref, ow_ref,
    mg_ref, mt_ref, mixed_ref, gain_sum_ref, bias_sum_ref, out_sum_ref,
):
    first = pl.program_id(0) == 0
    normed, inv_std = normed_of(mid_ref[...])
    upstream = own_ref[...] + got_ref[...]
    scaled = upstream * gain_ref[...]
    inner = scaled - row_mean(scaled) - normed * row_mean(scaled * normed)
    mid_grad = og_ref[...] + inv_std * inner
    mg_ref[...] = mid_grad
    low = mid_grad.astype(BF16)
    mt_ref[...] = low.T
    mixed_ref[...] = dot_nt(low, ow_ref[...]).astype(BF16)
    accumulate(gain_sum_ref, column_sum(upstream * normed), first)
    accumulate(bias_sum_ref, column_sum(upstream), first)
    accumulate(out_sum_ref, column_sum(mid_grad), first)


def back_attend_kernel(
    pair, q_ref, k_ref, v_ref, do_ref, o_ref, lse_ref,
    dq_ref, dk_ref, dv_ref, dq_sum_ref, dv_sum_ref, kt_ref, dk_acc, dv_acc,
):
    step = pl.program_id(0)
    scale = 1.0 / math.sqrt(HD)

    @pl.when(step == 0)
    def _():
        kt_ref[...] = k_ref[...].T
        dk_acc[...] = jnp.zeros_like(dk_acc)
        dv_acc[...] = jnp.zeros_like(dv_acc)

    keys, values, queries, upstream = k_ref[...], v_ref[...], q_ref[...], do_ref[...]
    both = (upstream.astype(F32) * o_ref[...].astype(F32)).T
    pieces = []
    for head in range(2):
        own_queries = keep_head(queries, head)
        own_upstream = keep_head(upstream, head)
        row_dot = column_sum(both[head * HD : (head + 1) * HD])
        log_total = lse_ref[2 * pair + head : 2 * pair + head + 1, :]
        scores = dot_nt(keys, own_queries)
        probs = jnp.exp2(scores * EXP_SCALE - log_total)
        prob_grad = dot_nt(values, own_upstream)
        score_grad = (probs * (prob_grad - row_dot)).astype(BF16)
        dv_acc[...] += dot(probs.astype(BF16), own_upstream)
        dk_acc[...] += dot(score_grad, own_queries)
        pieces.append(dot(kt_ref[head * HD : (head + 1) * HD, :], score_grad))
    query_grad = jnp.concatenate(pieces, axis=0).T * scale
    dq_ref[...] = query_grad.astype(BF16)
    accumulate(dq_sum_ref, column_sum(query_grad), step == 0)

    @pl.when(step == pl.num_programs(0) - 1)
    def _():
        dk_ref[...] = (dk_acc[...] * scale).astype(BF16)
        dv = dv_acc[...]
        dv_ref[...] = dv.astype(BF16)
        dv_sum_ref[...] = column_sum(dv)


def back_project_kernel(*refs):
    w_ref, part_ref = refs[-2:]
    pairs = (len(refs) - 2) // 3
    total = None
    for kind in range(3):
        grad = jnp.concatenate([refs[3 * pair + kind][...] for pair in range(pairs)], axis=1)
        term = dot_nt(grad, w_ref[kind])
        total = term if total is None else total + term
    part_ref[...] = total


def back_input_kernel(
    x_ref, time_ref, own_ref, got_ref, mg_ref, gain_ref,
    out_ref, time_sum_ref, gain_sum_ref, bias_sum_ref,
):
    first = pl.program_id(0) == 0
    normed, inv_std = normed_of(x_ref[...].astype(F32) + time_ref[...])
    upstream = own_ref[...] + got_ref[...]
    scaled = upstream * gain_ref[...]
    inner = scaled - row_mean(scaled) - normed * row_mean(scaled * normed)
    grad = mg_ref[...] + inv_std * inner
    out_ref[...] = grad
    accumulate(time_sum_ref, column_sum(grad), first)
    accumulate(gain_sum_ref, column_sum(upstream * normed), first)
    accumulate(bias_sum_ref, column_sum(upstream), first)


def weight_kernel(chunk, count, from_ref, *refs):
    keep_ref, send_ref, whole_ref = refs[-3:]
    xt_ref = refs[0]
    total = None
    parts = [ref[...] for ref in refs[1:-3]]
    right = parts[0] if len(parts) == 1 else jnp.concatenate(parts, axis=1)
    whole_ref[...] = dot(xt_ref[...], right)
    for place in range(count):
        start = pl.multiple_of(from_ref[place] * chunk, 8)
        rows = whole_ref[pl.ds(start, chunk), :]
        half = count // 2
        target = keep_ref if place < half else send_ref
        at = (place % half) * chunk
        target[at : at + chunk, :] = rows


def whole_weight_kernel(xt_ref, *refs):
    parts = [ref[...] for ref in refs[:-1]]
    right = parts[0] if len(parts) == 1 else jnp.concatenate(parts, axis=1)
    refs[-1][...] = dot(xt_ref[...], right)


def fixed(shape):
    return pl.BlockSpec(shape, lambda *_: (0,) * len(shape))


def by_rows(width, offset=0, rows=BLOCK):
    return pl.BlockSpec((rows, width), lambda step: (step + offset, 0))


def by_columns(height, offset=0, columns=BLOCK):
    return pl.BlockSpec((height, columns), lambda step: (0, step + offset))


def shaped(shape, dtype):
    return jax.ShapeDtypeStruct(shape, dtype)


def call(name, kernel, grid, args, specs, outs, out_specs, scratch=(), flops=0, prior=None):
    prior = list(prior or [])
    aliases = {}
    for place in range(len(prior)):
        aliases[len(args) + place] = len(outs) - len(prior) + place
    moved = sum(math.prod(a.shape) * a.dtype.itemsize for a in [*args, *outs])
    return pl.pallas_call(
        kernel,
        name=name,
        grid=grid,
        in_specs=[*specs, *[pl.BlockSpec(memory_space=pl.ANY) for _ in prior]],
        out_specs=out_specs,
        out_shape=outs,
        scratch_shapes=list(scratch),
        input_output_aliases=aliases,
        compiler_params=pltpu.CompilerParams(vmem_limit_bytes=VMEM_BYTES),
        cost_estimate=pl.CostEstimate(flops=int(flops), bytes_accessed=int(moved), transcendentals=0),
    )(*args, *prior)


def swap(value):
    return lax.ppermute(value, "mp", [(0, 1), (1, 0)])


def xor_pairs(size, bit):
    return [(index, index ^ bit) for index in range(size)]


def axis_bits(size):
    return [1 << place for place in range(size.bit_length() - 1)]


def hop(value, bit):
    return lax.ppermute(value, "dp", xor_pairs(lax.axis_size("dp"), bit))


def double_sum(value):
    for bit in axis_bits(lax.axis_size("dp")):
        value = value + hop(value, bit)
    return value


def halve(section, order):
    size = lax.axis_size("dp")
    me = lax.axis_index("dp")
    left = sorted(order, reverse=True)
    rows, columns = section.shape
    section = section.reshape((2,) * len(left) + (rows // size, columns))
    for bit in order:
        at = left.index(bit)
        mine = (me // bit) % 2
        send = lax.dynamic_index_in_dim(section, 1 - mine, at, keepdims=False)
        keep = lax.dynamic_index_in_dim(section, mine, at, keepdims=False)
        section = keep + hop(send, bit)
        left.remove(bit)
    return section


def chunk_sources(order):
    me = lax.axis_index("dp")
    places = []
    for place in range(1 << len(order)):
        relative = 0
        for step, bit in enumerate(order):
            if (place >> (len(order) - 1 - step)) & 1:
                relative |= bit
        places.append(relative)
    return jnp.array(places, jnp.int32) ^ me


class Section:
    def __init__(self, order, keep, send):
        self.order = list(order)
        self.keep = keep
        self.send = send

    def step(self, got=None):
        got = hop(self.send, self.order[0]) if got is None else got
        self.order = self.order[1:]
        if not self.order:
            self.keep = self.keep + got
            self.send = None
            return
        half = self.keep.shape[0] // 2
        self.send = self.keep[half:] + got[half:]
        self.keep = self.keep[:half] + got[:half]


def joint_step(sections):
    widths = [section.send.shape[1] for section in sections]
    got = hop(jnp.concatenate([section.send for section in sections], axis=1), sections[0].order[0])
    start = 0
    for section, width in zip(sections, widths):
        section.step(got[:, start : start + width])
        start += width


def weight_section(name, xt, parts, starts, width, order, block):
    size = lax.axis_size("dp")
    model, tokens = xt.shape
    chunk = model // size
    steps = width // block
    each = block // len(parts)
    flops = 2 * model * tokens * width
    y_specs = [by_columns(tokens, start // each, each) for start in starts]
    x_spec = fixed(xt.shape)
    if chunk % 8:
        whole = call(
            name, whole_weight_kernel, (steps,), [xt, *parts], [x_spec, *y_specs],
            [shaped((model, width), F32)], [by_columns(model, 0, block)], flops=flops,
        )[0]
        section = Section([], halve(whole, order), None)
        return section
    half = shaped((model // 2, width), F32)
    keep, send = pl.pallas_call(
        functools.partial(weight_kernel, chunk, size),
        name=name,
        grid_spec=pltpu.PrefetchScalarGridSpec(
            num_scalar_prefetch=1,
            grid=(steps,),
            in_specs=[
                pl.BlockSpec(xt.shape, lambda step, _: (0, 0)),
                *[
                    pl.BlockSpec((tokens, each), lambda step, _, at=start // each: (0, step + at))
                    for start in starts
                ],
            ],
            out_specs=[pl.BlockSpec((model // 2, block), lambda step, _: (0, step))] * 2,
            scratch_shapes=[pltpu.VMEM((model, block), F32)],
        ),
        out_shape=[half, half],
        compiler_params=pltpu.CompilerParams(vmem_limit_bytes=VMEM_BYTES),
        cost_estimate=pl.CostEstimate(
            flops=flops, bytes_accessed=2 * model * tokens + 2 * tokens * width + 4 * model * width,
            transcendentals=0,
        ),
    )(chunk_sources(order), xt, *parts)
    return Section(order, keep, send)


def section_orders(size):
    bits = axis_bits(size)
    if len(bits) == 4:
        x_bit, y_bit, z_low, z_high = bits
        return {
            "xy": [x_bit, y_bit, z_low, z_high],
            "yx": [y_bit, x_bit, z_low, z_high],
            "zxy": [z_low, x_bit, y_bit, z_high],
            "zyx": [z_low, y_bit, x_bit, z_high],
        }
    count = len(bits)
    turn = lambda start: bits[start % count :] + bits[: start % count]
    return {"xy": turn(0), "yx": turn(1), "zxy": turn(2), "zyx": turn(3)}


def local(
    inputs,
    time_embed,
    targets,
    timesteps,
    ln1_gain,
    ln1_bias,
    qkv_weight,
    qv_bias,
    out_weight,
    out_bias,
    ln2_gain,
    ln2_bias,
    up_weight,
    up_bias,
    down_weight,
    down_bias,
):
    seq_count, length, model = inputs.shape
    width = qkv_weight.shape[2]
    hidden = up_weight.shape[1]
    blocks = length // BLOCK
    halves = 2
    per_half = blocks // halves
    pairs = width // PAIR
    x = inputs.reshape(length, model)
    goal = targets.reshape(length, model)
    w_qkv = jnp.transpose(qkv_weight, (1, 0, 2))
    row = lambda vector: vector.reshape(1, -1)
    g1, b1, g2, b2 = row(ln1_gain), row(ln1_bias), row(ln2_gain), row(ln2_bias)
    ob, ub, db = row(out_bias), row(up_bias), row(down_bias)

    buckets = (
        (timesteps >= NSTEPS // 64).astype(jnp.int32)
        + (timesteps >= NSTEPS // 16).astype(jnp.int32)
        + (timesteps >= NSTEPS // 4).astype(jnp.int32)
    )
    one_hot = buckets[:, None] == jnp.arange(NB, dtype=jnp.int32)[None, :]
    bucket_counts = double_sum(jnp.sum(one_hot.astype(jnp.int32), axis=0))
    floors = jnp.maximum(bucket_counts, 1).astype(F32)
    total_seqs = seq_count * lax.axis_size("dp")
    seq_weight = total_seqs / (NB * jnp.sum(jnp.where(one_hot, floors[None, :], 0.0), axis=1))
    weight = seq_weight.reshape(1, 1)

    vec = fixed((1, model))
    mat = shaped((length, model), F32)
    low_mat = shaped((length, model), BF16)
    low_t = shaped((model, length), BF16)

    q, k, v, attn_t = call(
        "project", project_kernel, (blocks,),
        [x, time_embed, g1, b1, w_qkv, qv_bias],
        [by_rows(model), vec, vec, vec, fixed(w_qkv.shape), fixed(qv_bias.shape)],
        [shaped((length, width), BF16)] * 3 + [low_t],
        [by_rows(width)] * 3 + [by_columns(model)],
        flops=6 * length * model * width,
    )

    half_mat = shaped((length // halves, model), F32)
    prior = None
    own_attn, got_attn = [], []
    for half in range(halves):
        at = half * per_half
        part, *prior = call(
            "attend", attend_kernel, (per_half,),
            [q, k, v, out_weight],
            [by_rows(width, at), fixed(k.shape), fixed(v.shape), fixed(out_weight.shape)],
            [half_mat, shaped((length, width), BF16), shaped((8, length), F32)],
            [by_rows(model), by_rows(width, at), by_columns(8, at)],
            scratch=[pltpu.VMEM((width, length), BF16)],
            flops=16 * length * length * width // halves, prior=prior,
        )
        own_attn.append(part)
        got_attn.append(swap(part))
    mixed, lse = prior

    prior = None
    own_feed, got_feed = [], []
    for half in range(halves):
        at = half * per_half
        part, *prior = call(
            "feed", feed_kernel, (per_half,),
            [x, time_embed, own_attn[half], got_attn[half], ob, g2, b2, up_weight, ub, down_weight],
            [by_rows(model, at), vec, by_rows(model), by_rows(model), vec, vec, vec,
             fixed(up_weight.shape), fixed(ub.shape), fixed(down_weight.shape)],
            [half_mat, mat, low_t, shaped((length, hidden), BF16), shaped((length, hidden), F32)],
            [by_rows(model), by_rows(model, at), by_columns(model, at), by_rows(hidden, at),
             by_rows(hidden, at)],
            flops=4 * length * model * hidden // halves, prior=prior,
        )
        own_feed.append(part)
        got_feed.append(swap(part))
    mid, feed_t, activated, slope = prior

    prior = None
    down_sums = []
    for half in range(halves):
        at = half * per_half
        total, *prior = call(
            "loss", loss_kernel, (per_half,),
            [mid, own_feed[half], got_feed[half], db, goal, weight],
            [by_rows(model, at), by_rows(model), by_rows(model), vec, by_rows(model, at),
             pl.BlockSpec(memory_space=pltpu.SMEM)],
            [shaped((1, model), F32), low_mat, mat, low_mat, low_t],
            [vec, by_rows(model, at), by_rows(model, at), by_rows(model, at), by_columns(model, at)],
            prior=prior,
        )
        down_sums.append(total)
    out_act, out_grad, out_low, out_t = prior

    orders = section_orders(lax.axis_size("dp"))
    third = hidden // 2
    down_a = weight_section("grad_down", out_t, [activated], [0], third, orders["xy"], 256)
    down_b = weight_section("grad_down", out_t, [activated], [third], third, orders["yx"], 256)

    pre_low, own_pre, up_sum = call(
        "back_feed", back_feed_kernel, (blocks,),
        [out_low, slope, up_weight, down_weight],
        [by_rows(model), by_rows(hidden), fixed(up_weight.shape), fixed(down_weight.shape)],
        [shaped((length, hidden), BF16), mat, shaped((1, hidden), F32)],
        [by_rows(hidden), by_rows(model), fixed((1, hidden))],
        flops=4 * length * model * hidden,
    )
    got_pre = swap(own_pre)
    up_a = weight_section("grad_up", feed_t, [pre_low], [0], third, orders["zxy"], 256)
    up_b = weight_section("grad_up", feed_t, [pre_low], [third], third, orders["zyx"], 256)

    mid_grad, mid_t, mixed_grad, gain2_sum, bias2_sum, out_sum = call(
        "back_mid", back_mid_kernel, (blocks,),
        [mid, own_pre, got_pre, out_grad, g2, out_weight],
        [by_rows(model)] * 4 + [vec, fixed(out_weight.shape)],
        [mat, low_t, shaped((length, width), BF16)] + [shaped((1, model), F32)] * 3,
        [by_rows(model), by_columns(model), by_rows(width)] + [vec] * 3,
        flops=2 * length * model * width,
    )
    out_s = weight_section("grad_out", mid_t, [mixed], [0], width, orders["xy"], 128)

    grads, sums, qkv_s = [], [], []
    for pair in range(pairs):
        at_rows = pl.BlockSpec((BLOCK, PAIR), lambda step, pair=pair: (step, pair))
        whole = pl.BlockSpec((length, PAIR), lambda step, pair=pair: (0, pair))
        one = shaped((length, PAIR), BF16)
        one_sum = shaped((1, PAIR), F32)
        dq, dk, dv, dq_sum, dv_sum = call(
            "back_attend", functools.partial(back_attend_kernel, pair), (blocks,),
            [q, k, v, mixed_grad, mixed, lse],
            [at_rows, whole, whole, at_rows, at_rows, by_columns(8)],
            [one, one, one, one_sum, one_sum],
            [by_rows(PAIR), fixed((length, PAIR)), fixed((length, PAIR)), fixed((1, PAIR)),
             fixed((1, PAIR))],
            scratch=[pltpu.VMEM((PAIR, length), BF16), pltpu.VMEM((length, PAIR), F32),
                     pltpu.VMEM((length, PAIR), F32)],
            flops=40 * length * length * PAIR,
        )
        grads += [dq, dk, dv]
        sums.append((dq_sum, dv_sum))
        order = orders["yx"] if pair % 2 == 0 else orders["xy"]
        qkv_s.append(
            weight_section("grad_qkv", attn_t, [dq, dk, dv], [0, 0, 0], 3 * PAIR, order, 3 * PAIR)
        )

    own_proj = call(
        "back_project", back_project_kernel, (blocks,),
        [*grads, w_qkv], [by_rows(PAIR)] * len(grads) + [fixed(w_qkv.shape)],
        [mat], [by_rows(model)], flops=6 * length * model * width,
    )[0]
    got_proj = swap(own_proj)
    input_grad, grad_time, gain1_sum, bias1_sum = call(
        "back_input", back_input_kernel, (blocks,),
        [x, time_embed, own_proj, got_proj, mid_grad, g1],
        [by_rows(model), vec, by_rows(model), by_rows(model), by_rows(model), vec],
        [mat] + [shaped((1, model), F32)] * 3,
        [by_rows(model)] + [vec] * 3,
    )

    early = jnp.concatenate(
        [out_sum, gain2_sum, bias2_sum, up_sum, down_sums[0] + down_sums[1]], axis=1
    )
    late = jnp.concatenate(
        [gain1_sum, bias1_sum, *[s[0] for s in sums], *[s[1] for s in sums]], axis=1
    )
    early = double_sum(early)[0]
    late = double_sum(late)[0]

    for section in (down_a, down_b, up_a, up_b, out_s, *qkv_s):
        while section.order:
            section.step()

    qkv_part = jnp.concatenate([s.keep.reshape(-1, 3, PAIR) for s in qkv_s], axis=2)
    return (
        out_act.reshape(inputs.shape),
        input_grad.reshape(inputs.shape),
        grad_time,
        late[:model],
        late[model : 2 * model],
        qkv_part,
        late[2 * model :].reshape(2, width),
        out_s.keep.T,
        early[:model],
        early[model : 2 * model],
        early[2 * model : 3 * model],
        jnp.concatenate([up_a.keep, up_b.keep], axis=1),
        early[3 * model : 3 * model + hidden],
        jnp.concatenate([down_a.keep, down_b.keep], axis=1).T,
        early[3 * model + hidden :],
        bucket_counts,
    )


def solution(mesh):
    in_specs = (
        P("dp", None, None),
        P("dp", None),
        P("dp", None, None),
        P("dp"),
        P(),
        P(),
        P(None, None, "mp"),
        P(None, "mp"),
        P("mp", None),
        P(),
        P(),
        P(),
        P(None, "mp"),
        P("mp"),
        P("mp", None),
        P(),
    )
    out_specs = (
        P("dp", None, None),
        P("dp", None, None),
        P("dp", None),
        P(),
        P(),
        P("dp", None, "mp"),
        P(None, "mp"),
        P("mp", "dp"),
        P(),
        P(),
        P(),
        P("dp", "mp"),
        P("mp"),
        P("mp", "dp"),
        P(),
        P(),
    )
    return jax.shard_map(local, mesh=mesh, in_specs=in_specs, out_specs=out_specs, check_vma=False)
```

```python
import functools
import math

import jax
import jax.numpy as jnp
from jax import lax
from jax.experimental import pallas as pl
from jax.experimental.pallas import tpu as pltpu
from jax.sharding import PartitionSpec as P

HD = 64
NSTEPS = 2000
NB = 4
PAIR = 2 * HD
VMEM_BYTES = 14 * 2**20
LONG_BF = LONG_BM = LONG_BP = LONG_BI = LONG_GD = 1
LONG_AT = LONG_GU = LONG_GH = 20

epsilon = 1e-05
F32 = jnp.float32
BF16 = jnp.bfloat16
NT = (((1,), (1,)), ((), ()))
EXP_SCALE = math.log2(math.e) / math.sqrt(HD)
SCORE_LIMIT = 60.0


def dot(left, right):
    return jnp.dot(left, right, preferred_element_type=F32)


def dot_nt(left, right):
    return lax.dot_general(left, right, NT, preferred_element_type=F32)


def line(ref):
    return ref[...].reshape(1, -1)


def row_mean(value):
    return jnp.mean(value, axis=-1, keepdims=True)


def column_sum(value):
    return jnp.sum(value, axis=0, keepdims=True)


def normed_of(source):
    centred = source - row_mean(source)
    inv_std = lax.rsqrt(row_mean(centred * centred) + epsilon)
    return centred * inv_std, inv_std


def norm_grad(upstream, gain, normed, inv_std):
    scaled = upstream * gain
    inner = scaled - row_mean(scaled) - normed * row_mean(scaled * normed)
    return inv_std * inner


def head_mask(shape, head):
    lane = lax.broadcasted_iota(jnp.int32, shape, 1)
    return (lane >= HD) if head else (lane < HD)


def keep_head(value, head):
    return jnp.where(head_mask(value.shape, head), value, jnp.zeros_like(value))


def blocks_of(count, size):
    return [pl.ds(start, size) for start in range(0, count, size)]


def norm_kernel(rows, x_ref, time_ref, gain_ref, bias_ref, w_ref, qvb_ref, v_ref, in_ref, at_ref):
    for at in blocks_of(x_ref.shape[0], rows):
        residual = x_ref[at, :].astype(F32) + time_ref[...]
        normed, _ = normed_of(residual)
        attn_in = (normed * line(gain_ref) + line(bias_ref)).astype(BF16)
        in_ref[at, :] = attn_in
        at_ref[:, at] = attn_in.T
        v_ref[at, :] = (dot(attn_in, w_ref[2]) + qvb_ref[1:2]).astype(BF16)


def project_kernel(rows, in_ref, w_ref, qvb_ref, q_ref, k_ref, norm_ref):
    width = q_ref.shape[1]
    lane = lax.broadcasted_iota(jnp.int32, (width, 128), 0)
    column = lax.broadcasted_iota(jnp.int32, (width, 128), 1)
    pick = jnp.where(lane // HD == column, 1.0, 0.0).astype(BF16)
    longest = [None, None]
    for at in blocks_of(in_ref.shape[0], rows):
        attn_in = in_ref[at, :]
        queries = dot(attn_in, w_ref[0]) + qvb_ref[0:1]
        keys = dot(attn_in, w_ref[1])
        q_ref[at, :] = queries.astype(BF16)
        k_ref[at, :] = keys.astype(BF16)
        for place, value in enumerate((queries, keys)):
            top = jnp.max(dot((value * value).astype(BF16), pick), axis=0, keepdims=True)
            longest[place] = top if longest[place] is None else jnp.maximum(longest[place], top)
    norm_ref[...] = jnp.concatenate([jnp.broadcast_to(each, (8, 128)) for each in longest], axis=0)


def attend_kernel(
    start, rows, q_ref, k_ref, v_ref, norm_ref, mixed_ref, lse_ref, vt_ref
):
    length, width = k_ref.shape
    pairs = width // PAIR
    for pair in range(pairs):
        turned = v_ref[:, pair * PAIR : (pair + 1) * PAIR].T
        for head in range(2):
            at = (2 * pair + head) * PAIR
            vt_ref[at : at + HD, :] = turned[head * HD : (head + 1) * HD]
            vt_ref[at + HD : at + PAIR, :] = jnp.ones((HD, length), BF16)

    def attend(place, count, shift):
        at_own = pl.ds(place, count)
        pieces, stats = [], []
        for pair in range(pairs):
            lanes = slice(pair * PAIR, (pair + 1) * PAIR)
            keys = k_ref[:, lanes]
            queries = q_ref[pl.ds(start + place, count), lanes]
            for head in range(2):
                scores = dot_nt(keys, keep_head(queries, head))
                if shift:
                    top = jnp.max(scores, axis=0, keepdims=True)
                    expo = jnp.exp2((scores - top) * EXP_SCALE)
                else:
                    expo = jnp.exp2(scores * EXP_SCALE)
                at = (2 * pair + head) * PAIR
                both = dot(vt_ref[at : at + PAIR, :], expo.astype(BF16))
                total = both[HD : HD + 1]
                pieces.append(both[:HD] * (1.0 / total))
                stat = jnp.log2(total)
                stats.append(stat + top * EXP_SCALE if shift else stat)
        while len(stats) < lse_ref.shape[0]:
            stats.append(jnp.zeros_like(stats[0]))
        lse_ref[:, at_own] = jnp.concatenate(stats, axis=0)
        mixed_ref[at_own, :] = jnp.concatenate(pieces, axis=0).T.astype(BF16)

    bound = jnp.max(norm_ref[0:8, :] * norm_ref[8:16, :]) * (1.1 / HD)
    small = bound < SCORE_LIMIT * SCORE_LIMIT

    @pl.when(small)
    def _():
        attend(0, rows, False)

    @pl.when(jnp.logical_not(small))
    def _():
        @pl.loop(0, rows // 128)
        def _(step):
            attend(pl.multiple_of(step * 128, 128), 128, True)


def join_heads_kernel(mixed_ref, ow_ref, part_ref):
    part_ref[...] = dot(mixed_ref[...], ow_ref[...])


def normal_parts(v):
    size = jnp.abs(v)
    t = 1.0 / (1.0 + 0.2316419 * size)
    poly = t * (
        0.319381530
        + t * (-0.356563782 + t * (1.781477937 + t * (-1.821255978 + t * 1.330274429)))
    )
    density = jnp.exp2(v * v * (-0.5 * math.log2(math.e))) * (1.0 / math.sqrt(2.0 * math.pi))
    tail = poly * density
    return jnp.where(v < 0.0, tail, 1.0 - tail), density


def feed_kernel(
    start, rows, columns, x_ref, time_ref, own_ref, got_ref, ob_ref, gain_ref, bias_ref, uw_ref,
    ub_ref, dw_ref, part_ref, mid_ref, ft_ref, act_ref, slope_ref,
):
    count = own_ref.shape[0]
    hidden = uw_ref.shape[1]
    for at, at_all in zip(blocks_of(count, rows), range(start, start + count, rows)):
        mid = (
            x_ref[at_all : at_all + rows, :].astype(F32)
            + time_ref[...]
            + (own_ref[at, :] + got_ref[at, :])
            + line(ob_ref)
        )
        mid_ref[at, :] = mid
        normed, _ = normed_of(mid)
        ffn_in = (normed * line(gain_ref) + line(bias_ref)).astype(BF16)
        ft_ref[:, at] = ffn_in.T
        total = None
        for left in range(0, hidden, columns):
            span = slice(left, left + columns)
            preact = dot(ffn_in, uw_ref[:, span]) + line(ub_ref)[:, span]
            phi, density = normal_parts(preact)
            activated = (preact * phi).astype(BF16)
            act_ref[at, span] = activated
            slope_ref[at, span] = (phi + preact * density).astype(BF16)
            term = dot(activated, dw_ref[span, :])
            total = term if total is None else total + term
        part_ref[at, :] = total


def loss_kernel(
    start, rows, mid_ref, own_ref, got_ref, db_ref, goal_ref, weight_ref,
    out_ref, og_ref, low_ref, lt_ref, sum_ref,
):
    total = None
    count = mid_ref.shape[0]
    for at, at_all in zip(blocks_of(count, rows), range(start, start + count, rows)):
        final = mid_ref[at, :] + (own_ref[at, :] + got_ref[at, :]) + line(db_ref)
        out_ref[at, :] = final.astype(BF16)
        goal = goal_ref[at_all : at_all + rows, :].astype(F32)
        out_grad = (final - goal) * weight_ref[0, 0]
        og_ref[at, :] = out_grad
        low = out_grad.astype(BF16)
        low_ref[at, :] = low
        lt_ref[:, at] = low.T
        term = column_sum(out_grad)
        total = term if total is None else total + term
    sum_ref[...] = total


def back_feed_kernel(
    rows, columns, low_a, low_b, slope_a, slope_b, uw_ref, dw_ref, pre_ref, part_ref, sum_ref
):
    half = low_a.shape[0]
    hidden = uw_ref.shape[1]
    sums = [None] * (hidden // columns)
    for place, (low_ref, slope_ref) in enumerate(((low_a, slope_a), (low_b, slope_b))):
        for at, at_all in zip(blocks_of(half, rows), range(place * half, (place + 1) * half, rows)):
            out_low = low_ref[at, :]
            total = None
            for part in range(hidden // columns):
                span = slice(part * columns, (part + 1) * columns)
                pre_grad = slope_ref[at, span].astype(F32) * dot_nt(out_low, dw_ref[span, :])
                term = column_sum(pre_grad)
                sums[part] = term if sums[part] is None else sums[part] + term
                low = pre_grad.astype(BF16)
                pre_ref[at_all : at_all + rows, span] = low
                term = dot_nt(low, uw_ref[:, span])
                total = term if total is None else total + term
            part_ref[at_all : at_all + rows, :] = total
    sum_ref[...] = jnp.concatenate(sums, axis=1)


def back_mid_kernel(
    rows, mid_a, mid_b, og_a, og_b, own_ref, got_ref, gain_ref, ow_ref,
    mg_ref, mt_ref, mixed_ref, gain_sum_ref, bias_sum_ref, out_sum_ref,
):
    half = mid_a.shape[0]
    sums = [0.0, 0.0, 0.0]
    for place, (mid_ref, og_ref) in enumerate(((mid_a, og_a), (mid_b, og_b))):
        for at, at_all in zip(blocks_of(half, rows), range(place * half, (place + 1) * half, rows)):
            span = slice(at_all, at_all + rows)
            normed, inv_std = normed_of(mid_ref[at, :])
            upstream = own_ref[span, :] + got_ref[span, :]
            mid_grad = og_ref[at, :] + norm_grad(upstream, line(gain_ref), normed, inv_std)
            mg_ref[span, :] = mid_grad
            low = mid_grad.astype(BF16)
            mt_ref[:, span] = low.T
            mixed_ref[span, :] = dot_nt(low, ow_ref[...]).astype(BF16)
            for which, value in enumerate((upstream * normed, upstream, mid_grad)):
                sums[which] = sums[which] + column_sum(value)
    gain_sum_ref[...], bias_sum_ref[...], out_sum_ref[...] = sums


def back_attend_kernel(
    pair, q_ref, k_ref, v_ref, do_ref, o_a, o_b, lse_a, lse_b,
    dq_ref, dk_ref, dv_ref, dq_sum_ref, dv_sum_ref,
):
    scale = 1.0 / math.sqrt(HD)
    lanes = slice(pair * PAIR, (pair + 1) * PAIR)
    half = o_a.shape[0]
    keys, values = k_ref[:, lanes], v_ref[:, lanes]
    keys_t = keys.T
    dk, dv, dq_sum = None, None, None
    for place, (o_ref, lse_ref) in enumerate(((o_a, lse_a), (o_b, lse_b))):
        span = slice(place * half, (place + 1) * half)
        queries, upstream = q_ref[span, lanes], do_ref[span, lanes]
        both = (upstream.astype(F32) * o_ref[:, lanes].astype(F32)).T
        pieces = []
        for head in range(2):
            own_queries = keep_head(queries, head)
            own_upstream = keep_head(upstream, head)
            row_dot = column_sum(both[head * HD : (head + 1) * HD])
            log_total = lse_ref[2 * pair + head : 2 * pair + head + 1, :]
            scores = dot_nt(keys, own_queries)
            probs = jnp.exp2(scores * EXP_SCALE - log_total)
            prob_grad = dot_nt(values, own_upstream)
            score_grad = (probs * (prob_grad - row_dot)).astype(BF16)
            dv_term = dot(probs.astype(BF16), own_upstream)
            dk_term = dot(score_grad, own_queries)
            dv = dv_term if dv is None else dv + dv_term
            dk = dk_term if dk is None else dk + dk_term
            pieces.append(dot(keys_t[head * HD : (head + 1) * HD, :], score_grad))
        query_grad = jnp.concatenate(pieces, axis=0).T * scale
        dq_ref[span, :] = query_grad.astype(BF16)
        term = column_sum(query_grad)
        dq_sum = term if dq_sum is None else dq_sum + term
    dk_ref[...] = (dk * scale).astype(BF16)
    dv_ref[...] = dv.astype(BF16)
    dq_sum_ref[...] = dq_sum
    dv_sum_ref[...] = column_sum(dv)


def back_project_kernel(*refs):
    w_ref, part_ref = refs[-2:]
    pairs = (len(refs) - 2) // 3
    total = None
    for kind in range(3):
        grad = jnp.concatenate([refs[3 * pair + kind][...] for pair in range(pairs)], axis=1)
        term = dot_nt(grad, w_ref[kind])
        total = term if total is None else total + term
    part_ref[...] = total


def back_input_kernel(
    rows, x_ref, time_ref, own_ref, got_ref, mg_ref, gain_ref,
    out_ref, time_sum_ref, gain_sum_ref, bias_sum_ref,
):
    sums = [0.0, 0.0, 0.0]
    for at in blocks_of(x_ref.shape[0], rows):
        normed, inv_std = normed_of(x_ref[at, :].astype(F32) + time_ref[...])
        upstream = own_ref[at, :] + got_ref[at, :]
        grad = mg_ref[at, :] + norm_grad(upstream, line(gain_ref), normed, inv_std)
        out_ref[at, :] = grad
        for which, value in enumerate((grad, upstream * normed, upstream)):
            sums[which] = sums[which] + column_sum(value)
    time_sum_ref[...], gain_sum_ref[...], bias_sum_ref[...] = sums


def gathered(refs, start, count):
    return jnp.concatenate([ref[pl.ds(start, count), :] for ref in refs], axis=1)


def stacked(refs, columns):
    return jnp.concatenate([ref[:, columns] for ref in refs], axis=0)


def weight_kernel(chunk, count, terms, from_ref, *refs):
    keep_ref, send_ref = refs[-2:]
    half = count // 2
    for target, first in ((send_ref, half), (keep_ref, 0)):
        starts = [pl.multiple_of(from_ref[first + place] * chunk, 16) for place in range(half)]
        at, out_at = 0, 0
        for lefts, rights, columns in terms:
            left_refs = refs[at : at + lefts]
            right_refs = refs[at + lefts : at + lefts + rights]
            at += lefts + rights
            left = jnp.concatenate([gathered(left_refs, start, chunk) for start in starts], axis=0)
            right = stacked(right_refs, columns)
            target[:, out_at : out_at + right.shape[1]] = dot(left, right)
            out_at += right.shape[1]


def whole_weight_kernel(terms, *refs):
    at, out_at = 0, 0
    for lefts, rights, columns in terms:
        left = jnp.concatenate([ref[...] for ref in refs[at : at + lefts]], axis=1)
        right = stacked(refs[at + lefts : at + lefts + rights], columns)
        at += lefts + rights
        refs[-1][:, out_at : out_at + right.shape[1]] = dot(left, right)
        out_at += right.shape[1]


def step_kernel(settled, got_places, send_groups, vec_in, vec_out, *refs):
    count = len(settled)
    keeps, refs = refs[:count], refs[count:]
    total_gots = 1 + max(which for which, _ in got_places if which is not None)
    gots, refs = refs[:total_gots], refs[total_gots:]
    vector = None
    if vec_out is not None:
        vector, refs = refs[0][...], refs[1:]
    sends, news, refs = refs[: len(send_groups)], refs[len(send_groups) :][:count], refs[len(send_groups) + count :]
    rows, width = keeps[0].shape
    half = rows // 2
    for section, (which, at) in enumerate(got_places):
        total = keeps[section][...]
        if not settled[section]:
            total = total + gots[which][:rows, at * width : (at + 1) * width]
        news[section][...] = total[:half]
        for target, group in zip(sends, send_groups):
            if section in group:
                to = group.index(section) * width
                target[:half, to : to + width] = total[half:]
    if vector is not None:
        wide = vector.shape[1]
        if vec_in is not None:
            vector = vector + gots[vec_in][rows:, :wide]
        sends[vec_out][half:, :wide] = vector
        refs[0][...] = vector


def settle_kernel(keep_ref, got_ref, out_ref):
    out_ref[...] = keep_ref[...] + got_ref[...]


def finish_kernel(count, *refs):
    keeps, got_ref, outs = refs[:count], refs[count], refs[count + 1 :]
    width = keeps[0].shape[1]
    share = count // len(outs)
    for place, keep in enumerate(keeps):
        total = keep[...] + got_ref[:, place * width : (place + 1) * width]
        at = (place % share) * width
        outs[place // share][:, at : at + width] = total


def finish_heads_kernel(pair_of, keep_a, keep_b, keep_c, got_ref, vector_ref, qkv_ref, out_ref, *smalls):
    rows, width = keep_a.shape
    for place, keep in enumerate((keep_a, keep_b, keep_c)):
        total = keep[...] + got_ref[:rows, place * width : (place + 1) * width]
        lanes = slice(pair_of[place] * PAIR, (pair_of[place] + 1) * PAIR)
        for kind in range(3):
            qkv_ref[kind, :, lanes] = total[:, kind * PAIR : (kind + 1) * PAIR]
        out_ref[:, lanes] = total[:, 3 * PAIR :]
    unpack(vector_ref[...] + got_ref[rows:, : vector_ref.shape[1]], *smalls)


def pack_kernel(*refs):
    out_ref = refs[-1]
    down_a, down_b, up, gain2, bias2, out, gain1, bias1 = refs[:8]
    model = out_ref.shape[1]
    wide = up.shape[1] // model
    rows = [out[...], gain2[...], bias2[...], down_a[...] + down_b[...], gain1[...], bias1[...]]
    rows += [up[:, at * model : (at + 1) * model] for at in range(wide)]
    rows.append(jnp.concatenate([ref[...] for ref in refs[8:-1]], axis=1))
    rows.append(jnp.zeros((out_ref.shape[0] - len(rows), model), F32))
    out_ref[...] = jnp.concatenate(rows, axis=0)


def unpack_kernel(own_ref, got_ref, *outs):
    unpack(own_ref[...] + got_ref[...], *outs)


def unpack(total, *outs):
    model = total.shape[1]
    for place in range(6):
        outs[place][...] = total[place]
    wide = outs[6].shape[0] // model
    for at in range(wide):
        outs[6][at * model : (at + 1) * model] = total[6 + at]
    width = outs[7].shape[1]
    last = total[6 + wide : 7 + wide]
    outs[7][...] = jnp.concatenate([last[:, :width], last[:, width : 2 * width]], axis=0)


def held(shape, dtype):
    return pltpu.VMEM(shape, dtype)


def call(name, kernel, args, outs, scratch=(), flops=0, scalars=(), pins=()):
    if pins:
        count, inner = len(args), kernel
        kernel = lambda *refs: inner(*refs[:count], *refs[count + len(pins) :])
        args = [*args, *pins]
    whole = pl.BlockSpec(memory_space=pltpu.VMEM)
    specs = [
        pl.BlockSpec(memory_space=pltpu.SMEM) if place in scalars else whole
        for place in range(len(args))
    ]
    args = [
        arg if place in scalars else pltpu.with_memory_space_constraint(arg, pltpu.VMEM)
        for place, arg in enumerate(args)
    ]
    moved = sum(math.prod(a.shape) * a.dtype.itemsize for a in outs)
    return pl.pallas_call(
        kernel,
        name=name,
        in_specs=specs,
        out_specs=[whole] * len(outs),
        out_shape=outs,
        scratch_shapes=list(scratch),
        compiler_params=pltpu.CompilerParams(vmem_limit_bytes=VMEM_BYTES),
        cost_estimate=pl.CostEstimate(flops=int(flops), bytes_accessed=int(moved), transcendentals=0),
    )(*args)


def after(values, *others):
    return lax.optimization_barrier((values, others))[0]


def swap(value):
    return lax.ppermute(value, "mp", [(0, 1), (1, 0)])


def xor_pairs(size, bit):
    return [(index, index ^ bit) for index in range(size)]


def axis_bits(size):
    return [1 << place for place in range(size.bit_length() - 1)]


def hop(value, bit):
    return lax.ppermute(value, "dp", xor_pairs(lax.axis_size("dp"), bit))


def halve(section, order):
    size = lax.axis_size("dp")
    me = lax.axis_index("dp")
    left = sorted(order, reverse=True)
    rows, columns = section.shape
    section = section.reshape((2,) * len(left) + (rows // size, columns))
    for bit in order:
        at = left.index(bit)
        mine = (me // bit) % 2
        send = lax.dynamic_index_in_dim(section, 1 - mine, at, keepdims=False)
        keep = lax.dynamic_index_in_dim(section, mine, at, keepdims=False)
        section = keep + hop(send, bit)
        left.remove(bit)
    return section


def chunk_sources(order):
    me = lax.axis_index("dp")
    places = []
    for place in range(1 << len(order)):
        relative = 0
        for step, bit in enumerate(order):
            if (place >> (len(order) - 1 - step)) & 1:
                relative |= bit
        places.append(relative)
    return jnp.array(places, jnp.int32) ^ me


class Halving:
    def __init__(self, orders, plan):
        self.orders = orders
        self.plan = list(plan)
        self.keeps = [None] * len(orders)
        self.sends = [None] * len(orders)
        self.gots = []
        self.settled = [False] * len(orders)
        self.vector_at = None

    def start(self, places=None):
        for place, (_, bit) in enumerate(self.plan[0]):
            if places is None or place in places:
                self.gots.append((place, hop(self.sends[place], bit)))

    def settle(self, section, *others):
        which = [place for place, (group, _) in enumerate(self.plan[0]) if group == [section]][0]
        got = dict(self.gots)[which]
        self.gots = [each for each in self.gots if each[0] != which]
        keep, got = after((self.keeps[section], got), *others)
        self.keeps[section] = call("settle", settle_kernel, [keep, got], [held(keep.shape, F32)])[0]
        self.settled[section] = True
        return self.keeps[section]

    def advance(self, *others, vector=None, place=None):
        order = sorted(self.gots, key=lambda pair: pair[0])
        gots = after([got for _, got in order], *others)
        count = len(self.keeps)
        places = [(None, None)] * count
        for which, (slot, _) in enumerate(order):
            for at, section in enumerate(self.plan[0][slot][0]):
                places[section] = (which, at)
        vec_in = None
        if self.vector_at is not None:
            vec_in = [slot for slot, _ in order].index(self.vector_at)
        self.plan = self.plan[1:]
        self.gots = []
        groups = [group for group, _ in self.plan[0]]
        rows, width = self.keeps[0].shape
        half = rows // 2
        extra = [vector.shape[0] if vector is not None and at == place else 0 for at in range(len(groups))]
        outs = [held((half + more, width * len(group)), F32) for group, more in zip(groups, extra)]
        outs += [held((half, width), F32)] * count
        args = [*self.keeps, *gots]
        if vector is not None:
            args.append(vector)
            outs.append(held(vector.shape, F32))
        outs = call(
            "halve", functools.partial(step_kernel, self.settled, places, groups, vec_in, place), args, outs
        )
        self.settled = [False] * count
        self.sends, self.keeps = list(outs[: len(groups)]), list(outs[len(groups) :][:count])
        self.vector_at = place
        self.start()
        return self.keeps[0] if vector is None else outs[-1]

    def arrived(self):
        return [got for _, got in self.gots]


def two_axes(bits, turned):
    a, b, z, top = bits
    if turned:
        a, b = b, a
    orders = [[a, b, z, top], [b, a, z, top], [z, a, b, top]]
    plan = [
        [([0], a), ([1], b), ([2], z)],
        [([0], b), ([1, 2], a)],
        [([0, 1], z), ([2], b)],
        [([0, 1, 2], top)],
    ]
    return Halving(orders, plan)


def weight_section(name, terms, state, section, order):
    size = lax.axis_size("dp")
    model = terms[0][0][0].shape[0]
    chunk = model // size
    tokens = sum(left.shape[1] for left in terms[0][0])
    width = sum(columns.stop - columns.start for _, _, columns in terms)
    shape = [(len(left), len(right), columns) for left, right, columns in terms]
    flat = [piece for left, right, _ in terms for piece in [*left, *right]]
    flops = 2 * model * tokens * width * {'grad_down': LONG_GD, 'grad_up': LONG_GU, 'grad_heads': LONG_GH}[name]
    if state is None:
        whole = call(
            name, functools.partial(whole_weight_kernel, shape), flat,
            [held((model, width), F32)], flops=flops,
        )[0]
        return halve(whole, order)
    keep, send = call(
        name, functools.partial(weight_kernel, chunk, size, shape),
        [chunk_sources(state.orders[section]), *flat], [held((model // 2, width), F32)] * 2,
        flops=flops, scalars=(0,),
    )
    state.keeps[section], state.sends[section] = keep, send
    state.start([section])
    return send


def local(
    inputs,
    time_embed,
    targets,
    timesteps,
    ln1_gain,
    ln1_bias,
    qkv_weight,
    qv_bias,
    out_weight,
    out_bias,
    ln2_gain,
    ln2_bias,
    up_weight,
    up_bias,
    down_weight,
    down_bias,
):
    seq_count, length, model = inputs.shape
    width = qkv_weight.shape[2]
    hidden = up_weight.shape[1]
    size = lax.axis_size("dp")
    bits = axis_bits(size)
    halves = 2
    part_rows = length // halves
    pairs = width // PAIR
    x = inputs.reshape(length, model)
    goal = targets.reshape(length, model)
    w_qkv = jnp.transpose(qkv_weight, (1, 0, 2))
    g1, b1, g2, b2 = ln1_gain, ln1_bias, ln2_gain, ln2_bias
    ob, ub, db = out_bias, up_bias, down_bias

    buckets = (
        (timesteps >= NSTEPS // 64).astype(jnp.int32)
        + (timesteps >= NSTEPS // 16).astype(jnp.int32)
        + (timesteps >= NSTEPS // 4).astype(jnp.int32)
    )
    one_hot = buckets[:, None] == jnp.arange(NB, dtype=jnp.int32)[None, :]
    bucket_counts = jnp.sum(one_hot.astype(jnp.int32), axis=0)

    def count_hop(counts, bits):
        for bit in bits:
            counts = counts + hop(counts, bit)
        return counts

    vec = held((1, model), F32)

    def square(rows, dtype):
        return held((rows, model), dtype)

    bucket_counts = count_hop(bucket_counts, bits[:1])
    v, attn_in, attn_t = call(
        "norm", functools.partial(norm_kernel, 256),
        [x, time_embed, g1, b1, w_qkv, qv_bias],
        [held((length, width), BF16), held((length, model), BF16), held((model, length), BF16)],
        flops=2 * length * model * width,
    )
    attn_in, bucket_counts = lax.optimization_barrier((attn_in, bucket_counts))
    bucket_counts = count_hop(bucket_counts, bits[1:2])
    q, k, lengths = call(
        "project", functools.partial(project_kernel, 256),
        [attn_in, w_qkv, qv_bias],
        [held((length, width), BF16)] * 2 + [held((16, 128), F32)],
        flops=4 * length * model * width,
    )

    own_attn, mixed, lse, got_attn = [], [], [], []
    for half in range(halves):
        q, bucket_counts = lax.optimization_barrier((q, bucket_counts))
        bucket_counts = count_hop(bucket_counts, bits[half + 2 : half + 3 if half == 0 else None])
        mixed_half, lse_half = call(
            "attend", functools.partial(attend_kernel, half * part_rows, part_rows),
            [q, k, v, lengths],
            [held((part_rows, width), BF16), held((8, part_rows), F32)],
            scratch=[pltpu.VMEM((2 * width, length), BF16)],
            flops=16 * length * length * width // halves,
        )
        mixed_half, bucket_counts = lax.optimization_barrier((mixed_half, bucket_counts))
        part = call(
            "join_heads", join_heads_kernel, [mixed_half, out_weight],
            [square(part_rows, F32)], flops=2 * part_rows * width * model,
        )[0]
        own_attn.append(part)
        mixed.append(mixed_half)
        lse.append(lse_half)
        got_attn.append(swap(part))
        if half == 0:
            q = after(q, part)

    own_feed, mid, feed_t, activated, slope, got_feed = [], [], [], [], [], []
    for half in range(halves):
        outs = call(
            "feed", functools.partial(feed_kernel, half * part_rows, 256, 512),
            [x, time_embed, own_attn[half], got_attn[half], ob, g2, b2, up_weight, ub, down_weight],
            [square(part_rows, F32), square(part_rows, F32), held((model, part_rows), BF16),
             held((part_rows, hidden), BF16), held((part_rows, hidden), BF16)],
            flops=4 * length * model * hidden // halves,
            pins=[*mid, *feed_t, *activated, *slope],
        )
        for kept, value in zip((own_feed, mid, feed_t, activated, slope), outs):
            kept.append(value)
        got_feed.append(swap(outs[0]))
        if half == 0:
            own_attn[1] = after(own_attn[1], outs[0])

    floors = jnp.maximum(bucket_counts, 1).astype(F32)
    total_seqs = seq_count * size
    seq_weight = total_seqs / (NB * jnp.sum(jnp.where(one_hot, floors[None, :], 0.0), axis=1))
    weight = seq_weight.reshape(1, 1)

    out_act, out_grad, out_low, out_t, down_sums = [], [], [], [], []
    for half in range(halves):
        outs = call(
            "loss", functools.partial(loss_kernel, half * part_rows, 256),
            [mid[half], own_feed[half], got_feed[half], db, goal, weight],
            [square(part_rows, BF16), square(part_rows, F32), square(part_rows, BF16),
             held((model, part_rows), BF16), vec],
            scalars=(5,),
        )
        for kept, value in zip((out_act, out_grad, out_low, out_t, down_sums), outs):
            kept.append(value)

    staged = size == 16 and (model // size) % 16 == 0
    down, up, heads = [two_axes(bits, turned) if staged else None for turned in (False, True, False)]
    third = hidden // 3
    thirds = [slice(at * third, (at + 1) * third) for at in range(3)]
    down_parts, up_parts, head_parts = [], [], []
    for section, columns in enumerate(thirds):
        down_parts.append(weight_section("grad_down", [(out_t, activated, columns)], down, section, bits))

    out_low = after(out_low, *down_parts)
    pre_low, own_pre, up_sum = call(
        "back_feed", functools.partial(back_feed_kernel, 256, 512),
        [*out_low, *slope, up_weight, down_weight],
        [held((length, hidden), BF16), square(length, F32), held((1, hidden), F32)],
        flops=4 * length * model * hidden * LONG_BF,
    )
    got_pre = swap(own_pre)
    for section, columns in enumerate(thirds):
        up_parts.append(weight_section("grad_up", [(feed_t, [pre_low], columns)], up, section, bits))

    got_pre = after(got_pre, *up_parts)
    mid_grad, mid_t, mixed_grad, gain2_sum, bias2_sum, out_sum = call(
        "back_mid", functools.partial(back_mid_kernel, 256),
        [*mid, *out_grad, own_pre, got_pre, g2, out_weight],
        [square(length, F32), held((model, length), BF16), held((length, width), BF16)] + [vec] * 3,
        flops=2 * length * model * width * LONG_BM,
    )
    token = down.advance(out_sum) if staged else out_sum

    grads, sums = [], []
    section_of = [2, 0, 1]

    def head_gradient(pair, others):
        terms = [([after(attn_t, *others)], [grad], slice(0, PAIR)) for grad in grads[3 * pair :]]
        terms.append(([mid_t], mixed, slice(pair * PAIR, (pair + 1) * PAIR)))
        head_parts.append(weight_section("grad_heads", terms, heads, section_of[pair], bits))
        return head_parts[-1]

    for pair in range(pairs):
        one = held((length, PAIR), BF16)
        one_sum = held((1, PAIR), F32)
        mixed_grad = after(mixed_grad, token)
        dq, dk, dv, dq_sum, dv_sum = call(
            "back_attend", functools.partial(back_attend_kernel, pair),
            [q, k, v, mixed_grad, *mixed, *lse], [one, one, one, one_sum, one_sum],
            flops=40 * length * length * PAIR * LONG_AT,
        )
        grads += [dq, dk, dv]
        sums += [dq_sum, dv_sum]
        token = dq_sum
        if pair < pairs - 1:
            token = head_gradient(pair, [token])
        if staged:
            token = (up, down, up)[pair].advance(token)
            if pair == 1:
                token = heads.settle(section_of[0], token)
    grads[0] = after(grads[0], token)
    own_proj = call(
        "back_project", back_project_kernel, [*grads, w_qkv], [square(length, F32)],
        flops=6 * length * model * width * LONG_BP,
    )[0]
    got_proj = swap(own_proj)
    token = own_proj
    if staged:
        token = down.advance(token)
    token = head_gradient(pairs - 1, [token])
    got_proj = after(got_proj, token)
    input_grad, grad_time, gain1_sum, bias1_sum = call(
        "back_input", functools.partial(back_input_kernel, 256),
        [x, time_embed, own_proj, got_proj, mid_grad, g1],
        [jax.ShapeDtypeStruct((length, model), F32), jax.ShapeDtypeStruct((1, model), F32), vec, vec],
        flops=2 * length * model * width * LONG_BI,
    )
    packed = call(
        "pack", pack_kernel,
        [*down_sums, up_sum, gain2_sum, bias2_sum, out_sum, gain1_sum, bias1_sum,
         *sums[0::2], *sums[1::2]],
        [held((16, model), F32)],
    )[0]

    rows = model // size
    vector = jax.ShapeDtypeStruct((model,), F32)
    small_outs = [vector] * 6
    small_outs += [jax.ShapeDtypeStruct((hidden,), F32), jax.ShapeDtypeStruct((2, width), F32)]
    if staged:
        x_bit, y_bit, z_bit, top_bit = bits
        packed = packed + hop(packed, y_bit)
        token = up.advance(packed)
        packed = heads.advance(token, vector=packed, place=1)
        wide = [jax.ShapeDtypeStruct((rows, hidden), F32)]
        finish = functools.partial(finish_kernel, 3)
        down_part = call("finish", finish, [*down.keeps, *after(down.arrived(), packed)], wide)[0]
        packed = heads.advance(down_part, vector=packed, place=0)
        up_part = call("finish", finish, [*up.keeps, *after(up.arrived(), packed)], wide)[0]
        packed = heads.advance(up_part, vector=packed, place=0)
        qkv_part, out_part, *small = call(
            "finish_heads",
            functools.partial(finish_heads_kernel, [section_of.index(at) for at in range(3)]),
            [*heads.keeps, *heads.arrived(), packed],
            [jax.ShapeDtypeStruct((3, rows, width), F32), jax.ShapeDtypeStruct((rows, width), F32)]
            + small_outs,
        )
        qkv_part = jnp.transpose(qkv_part, (1, 0, 2))
    else:
        for bit in bits[:-1]:
            packed = packed + hop(packed, bit)
        small = call("unpack", unpack_kernel, [packed, hop(packed, bits[-1])], small_outs)
        down_part = jnp.concatenate(down_parts, axis=1)
        up_part = jnp.concatenate(up_parts, axis=1)
        split = 3 * PAIR
        qkv_part = jnp.concatenate([p[:, :split].reshape(rows, 3, PAIR) for p in head_parts], axis=2)
        out_part = jnp.concatenate([p[:, split:] for p in head_parts], axis=1)
    out_sum, gain2_sum, bias2_sum, down_sum, gain1_sum, bias1_sum, up_sum, qv_sum = small

    return (
        jnp.concatenate(out_act, axis=0).reshape(inputs.shape),
        input_grad.reshape(inputs.shape),
        grad_time,
        gain1_sum,
        bias1_sum,
        qkv_part,
        qv_sum,
        out_part.T,
        out_sum,
        gain2_sum,
        bias2_sum,
        up_part,
        up_sum,
        down_part.T,
        down_sum,
        bucket_counts,
    )


def solution(mesh):
    in_specs = (
        P("dp", None, None),
        P("dp", None),
        P("dp", None, None),
        P("dp"),
        P(),
        P(),
        P(None, None, "mp"),
        P(None, "mp"),
        P("mp", None),
        P(),
        P(),
        P(),
        P(None, "mp"),
        P("mp"),
        P("mp", None),
        P(),
    )
    out_specs = (
        P("dp", None, None),
        P("dp", None, None),
        P("dp", None),
        P(),
        P(),
        P("dp", None, "mp"),
        P(None, "mp"),
        P("mp", "dp"),
        P(),
        P(),
        P(),
        P("dp", "mp"),
        P("mp"),
        P("mp", "dp"),
        P(),
        P(),
    )
    return jax.shard_map(local, mesh=mesh, in_specs=in_specs, out_specs=out_specs, check_vma=False)
```

```python
import functools
import math

import jax
import jax.numpy as jnp
from jax import lax
from jax.experimental import pallas as pl
from jax.experimental.pallas import tpu as pltpu
from jax.sharding import PartitionSpec as P

HD = 64
NSTEPS = 2000
NB = 4
PAIR = 2 * HD
VMEM_BYTES = 14 * 2**20
LONG_BF = LONG_BM = LONG_BP = LONG_BI = LONG_GD = 1
LONG_AT = LONG_GU = LONG_GH = 20

epsilon = 1e-05
F32 = jnp.float32
BF16 = jnp.bfloat16
NT = (((1,), (1,)), ((), ()))
EXP_SCALE = math.log2(math.e) / math.sqrt(HD)
SCORE_LIMIT = 60.0


def dot(left, right):
    return jnp.dot(left, right, preferred_element_type=F32)


def dot_nt(left, right):
    return lax.dot_general(left, right, NT, preferred_element_type=F32)


def line(ref):
    return ref[...].reshape(1, -1)


def row_mean(value):
    return jnp.mean(value, axis=-1, keepdims=True)


def column_sum(value):
    return jnp.sum(value, axis=0, keepdims=True)


def normed_of(source):
    centred = source - row_mean(source)
    inv_std = lax.rsqrt(row_mean(centred * centred) + epsilon)
    return centred * inv_std, inv_std


def norm_grad(upstream, gain, normed, inv_std):
    scaled = upstream * gain
    inner = scaled - row_mean(scaled) - normed * row_mean(scaled * normed)
    return inv_std * inner


def head_mask(shape, head):
    lane = lax.broadcasted_iota(jnp.int32, shape, 1)
    return (lane >= HD) if head else (lane < HD)


def keep_head(value, head):
    return jnp.where(head_mask(value.shape, head), value, jnp.zeros_like(value))


def blocks_of(count, size):
    return [pl.ds(start, size) for start in range(0, count, size)]


def norm_kernel(rows, x_ref, time_ref, gain_ref, bias_ref, w_ref, qvb_ref, v_ref, in_ref, at_ref):
    for at in blocks_of(x_ref.shape[0], rows):
        residual = x_ref[at, :].astype(F32) + time_ref[...]
        normed, _ = normed_of(residual)
        attn_in = (normed * line(gain_ref) + line(bias_ref)).astype(BF16)
        in_ref[at, :] = attn_in
        at_ref[:, at] = attn_in.T
        v_ref[at, :] = (dot(attn_in, w_ref[2]) + qvb_ref[1:2]).astype(BF16)


def project_kernel(rows, in_ref, w_ref, qvb_ref, q_ref, k_ref, norm_ref):
    width = q_ref.shape[1]
    lane = lax.broadcasted_iota(jnp.int32, (width, 128), 0)
    column = lax.broadcasted_iota(jnp.int32, (width, 128), 1)
    pick = jnp.where(lane // HD == column, 1.0, 0.0).astype(BF16)
    longest = [None, None]
    for at in blocks_of(in_ref.shape[0], rows):
        attn_in = in_ref[at, :]
        queries = dot(attn_in, w_ref[0]) + qvb_ref[0:1]
        keys = dot(attn_in, w_ref[1])
        q_ref[at, :] = queries.astype(BF16)
        k_ref[at, :] = keys.astype(BF16)
        for place, value in enumerate((queries, keys)):
            top = jnp.max(dot((value * value).astype(BF16), pick), axis=0, keepdims=True)
            longest[place] = top if longest[place] is None else jnp.maximum(longest[place], top)
    norm_ref[...] = jnp.concatenate([jnp.broadcast_to(each, (8, 128)) for each in longest], axis=0)


def attend_kernel(rows, q_ref, k_ref, v_ref, norm_ref, mixed_ref, lse_ref, vt_ref):
    length, width = k_ref.shape
    pairs = width // PAIR
    for pair in range(pairs):
        turned = v_ref[:, pair * PAIR : (pair + 1) * PAIR].T
        for head in range(2):
            at = (2 * pair + head) * PAIR
            vt_ref[at : at + HD, :] = turned[head * HD : (head + 1) * HD]
            vt_ref[at + HD : at + PAIR, :] = jnp.ones((HD, length), BF16)

    def attend(place, count, shift):
        at_own = pl.ds(pl.multiple_of(place * count, count), count)
        pieces, stats = [], []
        for pair in range(pairs):
            lanes = slice(pair * PAIR, (pair + 1) * PAIR)
            keys = k_ref[:, lanes]
            queries = q_ref[at_own, lanes]
            for head in range(2):
                scores = dot_nt(keys, keep_head(queries, head))
                if shift:
                    top = jnp.max(scores, axis=0, keepdims=True)
                    expo = jnp.exp2((scores - top) * EXP_SCALE)
                else:
                    expo = jnp.exp2(scores * EXP_SCALE)
                at = (2 * pair + head) * PAIR
                both = dot(vt_ref[at : at + PAIR, :], expo.astype(BF16))
                total = both[HD : HD + 1]
                pieces.append(both[:HD] * (1.0 / total))
                stat = jnp.log2(total)
                stats.append(stat + top * EXP_SCALE if shift else stat)
        while len(stats) < lse_ref.shape[0]:
            stats.append(jnp.zeros_like(stats[0]))
        lse_ref[:, at_own] = jnp.concatenate(stats, axis=0)
        mixed_ref[at_own, :] = jnp.concatenate(pieces, axis=0).T.astype(BF16)

    bound = jnp.max(norm_ref[0:8, :] * norm_ref[8:16, :]) * (1.1 / HD)
    small = bound < SCORE_LIMIT * SCORE_LIMIT

    @pl.when(small)
    def _():
        @pl.loop(0, length // rows)
        def _(place):
            attend(place, rows, False)

    @pl.when(jnp.logical_not(small))
    def _():
        @pl.loop(0, length // 128)
        def _(place):
            attend(place, 128, True)


def join_heads_kernel(start, mixed_ref, ow_ref, part_ref):
    part_ref[...] = dot(mixed_ref[start : start + part_ref.shape[0], :], ow_ref[...])


def normal_parts(v):
    size = jnp.abs(v)
    t = 1.0 / (1.0 + 0.2316419 * size)
    poly = t * (
        0.319381530
        + t * (-0.356563782 + t * (1.781477937 + t * (-1.821255978 + t * 1.330274429)))
    )
    density = jnp.exp2(v * v * (-0.5 * math.log2(math.e))) * (1.0 / math.sqrt(2.0 * math.pi))
    tail = poly * density
    return jnp.where(v < 0.0, tail, 1.0 - tail), density


def feed_kernel(
    start, rows, columns, x_ref, time_ref, own_ref, got_ref, ob_ref, gain_ref, bias_ref, uw_ref,
    ub_ref, dw_ref, part_ref, mid_ref, ft_ref, act_ref, slope_ref,
):
    count = own_ref.shape[0]
    hidden = uw_ref.shape[1]
    for at, at_all in zip(blocks_of(count, rows), range(start, start + count, rows)):
        mid = (
            x_ref[at_all : at_all + rows, :].astype(F32)
            + time_ref[...]
            + (own_ref[at, :] + got_ref[at, :])
            + line(ob_ref)
        )
        mid_ref[at, :] = mid
        normed, _ = normed_of(mid)
        ffn_in = (normed * line(gain_ref) + line(bias_ref)).astype(BF16)
        ft_ref[:, at] = ffn_in.T
        total = None
        for left in range(0, hidden, columns):
            span = slice(left, left + columns)
            preact = dot(ffn_in, uw_ref[:, span]) + line(ub_ref)[:, span]
            phi, density = normal_parts(preact)
            activated = (preact * phi).astype(BF16)
            act_ref[at, span] = activated
            slope_ref[at, span] = (phi + preact * density).astype(BF16)
            term = dot(activated, dw_ref[span, :])
            total = term if total is None else total + term
        part_ref[at, :] = total


def loss_kernel(
    start, rows, mid_ref, own_ref, got_ref, db_ref, goal_ref, weight_ref,
    out_ref, og_ref, low_ref, lt_ref, sum_ref,
):
    total = None
    count = mid_ref.shape[0]
    for at, at_all in zip(blocks_of(count, rows), range(start, start + count, rows)):
        final = mid_ref[at, :] + (own_ref[at, :] + got_ref[at, :]) + line(db_ref)
        out_ref[at, :] = final.astype(BF16)
        goal = goal_ref[at_all : at_all + rows, :].astype(F32)
        out_grad = (final - goal) * weight_ref[0, 0]
        og_ref[at, :] = out_grad
        low = out_grad.astype(BF16)
        low_ref[at, :] = low
        lt_ref[:, at] = low.T
        term = column_sum(out_grad)
        total = term if total is None else total + term
    sum_ref[...] = total


def back_feed_kernel(
    rows, columns, low_a, low_b, slope_a, slope_b, uw_ref, dw_ref, pre_ref, part_ref, sum_ref
):
    half = low_a.shape[0]
    hidden = uw_ref.shape[1]
    sums = [None] * (hidden // columns)
    for place, (low_ref, slope_ref) in enumerate(((low_a, slope_a), (low_b, slope_b))):
        for at, at_all in zip(blocks_of(half, rows), range(place * half, (place + 1) * half, rows)):
            out_low = low_ref[at, :]
            total = None
            for part in range(hidden // columns):
                span = slice(part * columns, (part + 1) * columns)
                pre_grad = slope_ref[at, span].astype(F32) * dot_nt(out_low, dw_ref[span, :])
                term = column_sum(pre_grad)
                sums[part] = term if sums[part] is None else sums[part] + term
                low = pre_grad.astype(BF16)
                pre_ref[at_all : at_all + rows, span] = low
                term = dot_nt(low, uw_ref[:, span])
                total = term if total is None else total + term
            part_ref[at_all : at_all + rows, :] = total
    sum_ref[...] = jnp.concatenate(sums, axis=1)


def back_mid_kernel(
    rows, mid_a, mid_b, og_a, og_b, own_ref, got_ref, gain_ref, ow_ref,
    mg_ref, mt_ref, mixed_ref, gain_sum_ref, bias_sum_ref, out_sum_ref,
):
    half = mid_a.shape[0]
    sums = [0.0, 0.0, 0.0]
    for place, (mid_ref, og_ref) in enumerate(((mid_a, og_a), (mid_b, og_b))):
        for at, at_all in zip(blocks_of(half, rows), range(place * half, (place + 1) * half, rows)):
            span = slice(at_all, at_all + rows)
            normed, inv_std = normed_of(mid_ref[at, :])
            upstream = own_ref[span, :] + got_ref[span, :]
            mid_grad = og_ref[at, :] + norm_grad(upstream, line(gain_ref), normed, inv_std)
            mg_ref[span, :] = mid_grad
            low = mid_grad.astype(BF16)
            mt_ref[:, span] = low.T
            mixed_ref[span, :] = dot_nt(low, ow_ref[...]).astype(BF16)
            for which, value in enumerate((upstream * normed, upstream, mid_grad)):
                sums[which] = sums[which] + column_sum(value)
    gain_sum_ref[...], bias_sum_ref[...], out_sum_ref[...] = sums


def back_attend_kernel(
    pair, blocks, q_ref, k_ref, v_ref, do_ref, o_ref, lse_ref,
    dq_ref, dk_ref, dv_ref, dq_sum_ref, dv_sum_ref,
):
    scale = 1.0 / math.sqrt(HD)
    lanes = slice(pair * PAIR, (pair + 1) * PAIR)
    half = o_ref.shape[0] // blocks
    keys, values = k_ref[:, lanes], v_ref[:, lanes]
    keys_t = keys.T
    dk, dv, dq_sum = None, None, None
    for place in range(blocks):
        span = slice(place * half, (place + 1) * half)
        queries, upstream = q_ref[span, lanes], do_ref[span, lanes]
        both = (upstream.astype(F32) * o_ref[span, lanes].astype(F32)).T
        pieces = []
        for head in range(2):
            own_queries = keep_head(queries, head)
            own_upstream = keep_head(upstream, head)
            row_dot = column_sum(both[head * HD : (head + 1) * HD])
            log_total = lse_ref[2 * pair + head : 2 * pair + head + 1, span]
            scores = dot_nt(keys, own_queries)
            probs = jnp.exp2(scores * EXP_SCALE - log_total)
            prob_grad = dot_nt(values, own_upstream)
            score_grad = (probs * (prob_grad - row_dot)).astype(BF16)
            dv_term = dot(probs.astype(BF16), own_upstream)
            dk_term = dot(score_grad, own_queries)
            dv = dv_term if dv is None else dv + dv_term
            dk = dk_term if dk is None else dk + dk_term
            pieces.append(dot(keys_t[head * HD : (head + 1) * HD, :], score_grad))
        query_grad = jnp.concatenate(pieces, axis=0).T * scale
        dq_ref[span, :] = query_grad.astype(BF16)
        term = column_sum(query_grad)
        dq_sum = term if dq_sum is None else dq_sum + term
    dk_ref[...] = (dk * scale).astype(BF16)
    dv_ref[...] = dv.astype(BF16)
    dq_sum_ref[...] = dq_sum
    dv_sum_ref[...] = column_sum(dv)


def back_project_kernel(*refs):
    w_ref, part_ref = refs[-2:]
    pairs = (len(refs) - 2) // 3
    total = None
    for kind in range(3):
        grad = jnp.concatenate([refs[3 * pair + kind][...] for pair in range(pairs)], axis=1)
        term = dot_nt(grad, w_ref[kind])
        total = term if total is None else total + term
    part_ref[...] = total


def back_input_kernel(
    rows, x_ref, time_ref, own_ref, got_ref, mg_ref, gain_ref,
    out_ref, time_sum_ref, gain_sum_ref, bias_sum_ref,
):
    sums = [0.0, 0.0, 0.0]
    for at in blocks_of(x_ref.shape[0], rows):
        normed, inv_std = normed_of(x_ref[at, :].astype(F32) + time_ref[...])
        upstream = own_ref[at, :] + got_ref[at, :]
        grad = mg_ref[at, :] + norm_grad(upstream, line(gain_ref), normed, inv_std)
        out_ref[at, :] = grad
        for which, value in enumerate((grad, upstream * normed, upstream)):
            sums[which] = sums[which] + column_sum(value)
    time_sum_ref[...], gain_sum_ref[...], bias_sum_ref[...] = sums


def gathered(refs, start, count):
    return jnp.concatenate([ref[pl.ds(start, count), :] for ref in refs], axis=1)


def stacked(refs, columns):
    return jnp.concatenate([ref[:, columns] for ref in refs], axis=0)


def weight_kernel(chunk, count, terms, from_ref, *refs):
    keep_ref, send_ref = refs[-2:]
    half = count // 2
    for target, first in ((send_ref, half), (keep_ref, 0)):
        starts = [pl.multiple_of(from_ref[first + place] * chunk, 16) for place in range(half)]
        at, out_at = 0, 0
        for lefts, rights, columns in terms:
            left_refs = refs[at : at + lefts]
            right_refs = refs[at + lefts : at + lefts + rights]
            at += lefts + rights
            left = jnp.concatenate([gathered(left_refs, start, chunk) for start in starts], axis=0)
            right = stacked(right_refs, columns)
            target[:, out_at : out_at + right.shape[1]] = dot(left, right)
            out_at += right.shape[1]


def whole_weight_kernel(terms, *refs):
    at, out_at = 0, 0
    for lefts, rights, columns in terms:
        left = jnp.concatenate([ref[...] for ref in refs[at : at + lefts]], axis=1)
        right = stacked(refs[at + lefts : at + lefts + rights], columns)
        at += lefts + rights
        refs[-1][:, out_at : out_at + right.shape[1]] = dot(left, right)
        out_at += right.shape[1]


def step_kernel(settled, got_places, send_groups, vec_in, vec_out, *refs):
    count = len(settled)
    keeps, refs = refs[:count], refs[count:]
    total_gots = 1 + max(which for which, _ in got_places if which is not None)
    gots, refs = refs[:total_gots], refs[total_gots:]
    vector = None
    if vec_out is not None:
        vector, refs = refs[0][...], refs[1:]
    sends, news, refs = refs[: len(send_groups)], refs[len(send_groups) :][:count], refs[len(send_groups) + count :]
    rows, width = keeps[0].shape
    half = rows // 2
    for section, (which, at) in enumerate(got_places):
        total = keeps[section][...]
        if not settled[section]:
            total = total + gots[which][:rows, at * width : (at + 1) * width]
        news[section][...] = total[:half]
        for target, group in zip(sends, send_groups):
            if section in group:
                to = group.index(section) * width
                target[:half, to : to + width] = total[half:]
    if vector is not None:
        wide = vector.shape[1]
        if vec_in is not None:
            vector = vector + gots[vec_in][rows:, :wide]
        sends[vec_out][half:, :wide] = vector
        refs[0][...] = vector


def settle_kernel(keep_ref, got_ref, out_ref):
    out_ref[...] = keep_ref[...] + got_ref[...]


def finish_kernel(count, *refs):
    keeps, got_ref, outs = refs[:count], refs[count], refs[count + 1 :]
    width = keeps[0].shape[1]
    share = count // len(outs)
    for place, keep in enumerate(keeps):
        total = keep[...] + got_ref[:, place * width : (place + 1) * width]
        at = (place % share) * width
        outs[place // share][:, at : at + width] = total


def finish_heads_kernel(pair_of, keep_a, keep_b, keep_c, got_ref, vector_ref, qkv_ref, out_ref, *smalls):
    rows, width = keep_a.shape
    for place, keep in enumerate((keep_a, keep_b, keep_c)):
        total = keep[...] + got_ref[:rows, place * width : (place + 1) * width]
        lanes = slice(pair_of[place] * PAIR, (pair_of[place] + 1) * PAIR)
        for kind in range(3):
            qkv_ref[kind, :, lanes] = total[:, kind * PAIR : (kind + 1) * PAIR]
        out_ref[:, lanes] = total[:, 3 * PAIR :]
    unpack(vector_ref[...] + got_ref[rows:, : vector_ref.shape[1]], *smalls)


def pack_kernel(*refs):
    out_ref = refs[-1]
    down_a, down_b, up, gain2, bias2, out, gain1, bias1 = refs[:8]
    model = out_ref.shape[1]
    wide = up.shape[1] // model
    rows = [out[...], gain2[...], bias2[...], down_a[...] + down_b[...], gain1[...], bias1[...]]
    rows += [up[:, at * model : (at + 1) * model] for at in range(wide)]
    rows.append(jnp.concatenate([ref[...] for ref in refs[8:-1]], axis=1))
    rows.append(jnp.zeros((out_ref.shape[0] - len(rows), model), F32))
    out_ref[...] = jnp.concatenate(rows, axis=0)


def unpack_kernel(own_ref, got_ref, *outs):
    unpack(own_ref[...] + got_ref[...], *outs)


def unpack(total, *outs):
    model = total.shape[1]
    for place in range(6):
        outs[place][...] = total[place]
    wide = outs[6].shape[0] // model
    for at in range(wide):
        outs[6][at * model : (at + 1) * model] = total[6 + at]
    width = outs[7].shape[1]
    last = total[6 + wide : 7 + wide]
    outs[7][...] = jnp.concatenate([last[:, :width], last[:, width : 2 * width]], axis=0)


def held(shape, dtype):
    return pltpu.VMEM(shape, dtype)


def call(name, kernel, args, outs, scratch=(), flops=0, scalars=(), pins=()):
    if pins:
        count, inner = len(args), kernel
        kernel = lambda *refs: inner(*refs[:count], *refs[count + len(pins) :])
        args = [*args, *pins]
    whole = pl.BlockSpec(memory_space=pltpu.VMEM)
    specs = [
        pl.BlockSpec(memory_space=pltpu.SMEM) if place in scalars else whole
        for place in range(len(args))
    ]
    args = [
        arg if place in scalars else pltpu.with_memory_space_constraint(arg, pltpu.VMEM)
        for place, arg in enumerate(args)
    ]
    moved = sum(math.prod(a.shape) * a.dtype.itemsize for a in outs)
    return pl.pallas_call(
        kernel,
        name=name,
        in_specs=specs,
        out_specs=[whole] * len(outs),
        out_shape=outs,
        scratch_shapes=list(scratch),
        compiler_params=pltpu.CompilerParams(vmem_limit_bytes=VMEM_BYTES),
        cost_estimate=pl.CostEstimate(flops=int(flops), bytes_accessed=int(moved), transcendentals=0),
    )(*args)


def after(values, *others):
    return lax.optimization_barrier((values, others))[0]


def swap(value):
    return lax.ppermute(value, "mp", [(0, 1), (1, 0)])


def xor_pairs(size, bit):
    return [(index, index ^ bit) for index in range(size)]


def axis_bits(size):
    return [1 << place for place in range(size.bit_length() - 1)]


def hop(value, bit):
    return lax.ppermute(value, "dp", xor_pairs(lax.axis_size("dp"), bit))


def halve(section, order):
    size = lax.axis_size("dp")
    me = lax.axis_index("dp")
    left = sorted(order, reverse=True)
    rows, columns = section.shape
    section = section.reshape((2,) * len(left) + (rows // size, columns))
    for bit in order:
        at = left.index(bit)
        mine = (me // bit) % 2
        send = lax.dynamic_index_in_dim(section, 1 - mine, at, keepdims=False)
        keep = lax.dynamic_index_in_dim(section, mine, at, keepdims=False)
        section = keep + hop(send, bit)
        left.remove(bit)
    return section


def chunk_sources(order):
    me = lax.axis_index("dp")
    places = []
    for place in range(1 << len(order)):
        relative = 0
        for step, bit in enumerate(order):
            if (place >> (len(order) - 1 - step)) & 1:
                relative |= bit
        places.append(relative)
    return jnp.array(places, jnp.int32) ^ me


class Halving:
    def __init__(self, orders, plan):
        self.orders = orders
        self.plan = list(plan)
        self.keeps = [None] * len(orders)
        self.sends = [None] * len(orders)
        self.gots = []
        self.settled = [False] * len(orders)
        self.vector_at = None

    def start(self, places=None):
        for place, (_, bit) in enumerate(self.plan[0]):
            if places is None or place in places:
                self.gots.append((place, hop(self.sends[place], bit)))

    def settle(self, section, *others):
        which = [place for place, (group, _) in enumerate(self.plan[0]) if group == [section]][0]
        got = dict(self.gots)[which]
        self.gots = [each for each in self.gots if each[0] != which]
        keep, got = after((self.keeps[section], got), *others)
        self.keeps[section] = call("settle", settle_kernel, [keep, got], [held(keep.shape, F32)])[0]
        self.settled[section] = True
        return self.keeps[section]

    def advance(self, *others, vector=None, place=None):
        order = sorted(self.gots, key=lambda pair: pair[0])
        gots = after([got for _, got in order], *others)
        count = len(self.keeps)
        places = [(None, None)] * count
        for which, (slot, _) in enumerate(order):
            for at, section in enumerate(self.plan[0][slot][0]):
                places[section] = (which, at)
        vec_in = None
        if self.vector_at is not None:
            vec_in = [slot for slot, _ in order].index(self.vector_at)
        self.plan = self.plan[1:]
        self.gots = []
        groups = [group for group, _ in self.plan[0]]
        rows, width = self.keeps[0].shape
        half = rows // 2
        extra = [vector.shape[0] if vector is not None and at == place else 0 for at in range(len(groups))]
        outs = [held((half + more, width * len(group)), F32) for group, more in zip(groups, extra)]
        outs += [held((half, width), F32)] * count
        args = [*self.keeps, *gots]
        if vector is not None:
            args.append(vector)
            outs.append(held(vector.shape, F32))
        outs = call(
            "halve", functools.partial(step_kernel, self.settled, places, groups, vec_in, place), args, outs
        )
        self.settled = [False] * count
        self.sends, self.keeps = list(outs[: len(groups)]), list(outs[len(groups) :][:count])
        self.vector_at = place
        self.start()
        return self.keeps[0] if vector is None else outs[-1]

    def arrived(self):
        return [got for _, got in self.gots]


def two_axes(bits, turned):
    a, b, z, top = bits
    if turned:
        a, b = b, a
    orders = [[a, b, z, top], [b, a, z, top], [z, a, b, top]]
    plan = [
        [([0], a), ([1], b), ([2], z)],
        [([0], b), ([1, 2], a)],
        [([0, 1], z), ([2], b)],
        [([0, 1, 2], top)],
    ]
    return Halving(orders, plan)


def weight_section(name, terms, state, section, order):
    size = lax.axis_size("dp")
    model = terms[0][0][0].shape[0]
    chunk = model // size
    tokens = sum(left.shape[1] for left in terms[0][0])
    width = sum(columns.stop - columns.start for _, _, columns in terms)
    shape = [(len(left), len(right), columns) for left, right, columns in terms]
    flat = [piece for left, right, _ in terms for piece in [*left, *right]]
    flops = 2 * model * tokens * width * {'grad_down': LONG_GD, 'grad_up': LONG_GU, 'grad_heads': LONG_GH}[name]
    if state is None:
        whole = call(
            name, functools.partial(whole_weight_kernel, shape), flat,
            [held((model, width), F32)], flops=flops,
        )[0]
        return halve(whole, order)
    keep, send = call(
        name, functools.partial(weight_kernel, chunk, size, shape),
        [chunk_sources(state.orders[section]), *flat], [held((model // 2, width), F32)] * 2,
        flops=flops, scalars=(0,),
    )
    state.keeps[section], state.sends[section] = keep, send
    state.start([section])
    return send


def local(
    inputs,
    time_embed,
    targets,
    timesteps,
    ln1_gain,
    ln1_bias,
    qkv_weight,
    qv_bias,
    out_weight,
    out_bias,
    ln2_gain,
    ln2_bias,
    up_weight,
    up_bias,
    down_weight,
    down_bias,
):
    seq_count, length, model = inputs.shape
    width = qkv_weight.shape[2]
    hidden = up_weight.shape[1]
    size = lax.axis_size("dp")
    bits = axis_bits(size)
    halves = 2
    part_rows = length // halves
    pairs = width // PAIR
    x = inputs.reshape(length, model)
    goal = targets.reshape(length, model)
    w_qkv = jnp.transpose(qkv_weight, (1, 0, 2))
    g1, b1, g2, b2 = ln1_gain, ln1_bias, ln2_gain, ln2_bias
    ob, ub, db = out_bias, up_bias, down_bias

    buckets = (
        (timesteps >= NSTEPS // 64).astype(jnp.int32)
        + (timesteps >= NSTEPS // 16).astype(jnp.int32)
        + (timesteps >= NSTEPS // 4).astype(jnp.int32)
    )
    one_hot = buckets[:, None] == jnp.arange(NB, dtype=jnp.int32)[None, :]
    bucket_counts = jnp.sum(one_hot.astype(jnp.int32), axis=0)

    def count_hop(counts, bits):
        for bit in bits:
            counts = counts + hop(counts, bit)
        return counts

    vec = held((1, model), F32)

    def square(rows, dtype):
        return held((rows, model), dtype)

    bucket_counts = count_hop(bucket_counts, bits[:1])
    v, attn_in, attn_t = call(
        "norm", functools.partial(norm_kernel, 256),
        [x, time_embed, g1, b1, w_qkv, qv_bias],
        [held((length, width), BF16), held((length, model), BF16), held((model, length), BF16)],
        flops=2 * length * model * width,
    )
    attn_in, bucket_counts = lax.optimization_barrier((attn_in, bucket_counts))
    bucket_counts = count_hop(bucket_counts, bits[1:2])
    q, k, lengths = call(
        "project", functools.partial(project_kernel, 256),
        [attn_in, w_qkv, qv_bias],
        [held((length, width), BF16)] * 2 + [held((16, 128), F32)],
        flops=4 * length * model * width,
    )

    q, bucket_counts = lax.optimization_barrier((q, bucket_counts))
    bucket_counts = count_hop(bucket_counts, bits[2:3])
    mixed, lse = call(
        "attend", functools.partial(attend_kernel, part_rows),
        [q, k, v, lengths],
        [held((length, width), BF16), held((8, length), F32)],
        scratch=[pltpu.VMEM((2 * width, length), BF16)],
        flops=16 * length * length * width,
    )
    mixed, bucket_counts = lax.optimization_barrier((mixed, bucket_counts))
    bucket_counts = count_hop(bucket_counts, bits[3:])
    own_attn, got_attn = [], []
    for half in range(halves):
        own_attn.append(call(
            "join_heads", functools.partial(join_heads_kernel, half * part_rows), [mixed, out_weight],
            [square(part_rows, F32)], flops=2 * part_rows * width * model,
        )[0])
        got_attn.append(swap(own_attn[half]))
        if half == 0:
            mixed = after(mixed, own_attn[0])
    own_attn[0], bucket_counts = lax.optimization_barrier((own_attn[0], bucket_counts))

    own_feed, mid, feed_t, activated, slope, got_feed = [], [], [], [], [], []
    for half in range(halves):
        outs = call(
            "feed", functools.partial(feed_kernel, half * part_rows, 256, 512),
            [x, time_embed, own_attn[half], got_attn[half], ob, g2, b2, up_weight, ub, down_weight],
            [square(part_rows, F32), square(part_rows, F32), held((model, part_rows), BF16),
             held((part_rows, hidden), BF16), held((part_rows, hidden), BF16)],
            flops=4 * length * model * hidden // halves,
            pins=[*mid, *feed_t, *activated, *slope],
        )
        for kept, value in zip((own_feed, mid, feed_t, activated, slope), outs):
            kept.append(value)
        got_feed.append(swap(outs[0]))
        if half == 0:
            own_attn[1] = after(own_attn[1], outs[0])

    floors = jnp.maximum(bucket_counts, 1).astype(F32)
    total_seqs = seq_count * size
    seq_weight = total_seqs / (NB * jnp.sum(jnp.where(one_hot, floors[None, :], 0.0), axis=1))
    weight = seq_weight.reshape(1, 1)

    out_act, out_grad, out_low, out_t, down_sums = [], [], [], [], []
    for half in range(halves):
        outs = call(
            "loss", functools.partial(loss_kernel, half * part_rows, 256),
            [mid[half], own_feed[half], got_feed[half], db, goal, weight],
            [square(part_rows, BF16), square(part_rows, F32), square(part_rows, BF16),
             held((model, part_rows), BF16), vec],
            scalars=(5,),
        )
        for kept, value in zip((out_act, out_grad, out_low, out_t, down_sums), outs):
            kept.append(value)

    staged = size == 16 and (model // size) % 16 == 0
    down, up, heads = [two_axes(bits, turned) if staged else None for turned in (False, True, True)]
    third = hidden // 3
    thirds = [slice(at * third, (at + 1) * third) for at in range(3)]
    down_parts, up_parts, head_parts = [], [], []
    for section, columns in enumerate(thirds):
        down_parts.append(weight_section("grad_down", [(out_t, activated, columns)], down, section, bits))

    out_low = after(out_low, *down_parts)
    pre_low, own_pre, up_sum = call(
        "back_feed", functools.partial(back_feed_kernel, 256, 512),
        [*out_low, *slope, up_weight, down_weight],
        [held((length, hidden), BF16), square(length, F32), held((1, hidden), F32)],
        flops=4 * length * model * hidden * LONG_BF,
    )
    got_pre = swap(own_pre)
    for section, columns in enumerate(thirds):
        up_parts.append(weight_section("grad_up", [(feed_t, [pre_low], columns)], up, section, bits))

    got_pre = after(got_pre, *up_parts)
    mid_grad, mid_t, mixed_grad, gain2_sum, bias2_sum, out_sum = call(
        "back_mid", functools.partial(back_mid_kernel, 256),
        [*mid, *out_grad, own_pre, got_pre, g2, out_weight],
        [square(length, F32), held((model, length), BF16), held((length, width), BF16)] + [vec] * 3,
        flops=2 * length * model * width * LONG_BM,
    )
    token = down.advance(out_sum) if staged else out_sum

    grads, sums = [], []
    section_of = [2, 0, 1]

    def head_gradient(pair, others):
        terms = [([after(attn_t, *others)], [grad], slice(0, PAIR)) for grad in grads[3 * pair :]]
        terms.append(([mid_t], [mixed], slice(pair * PAIR, (pair + 1) * PAIR)))
        head_parts.append(weight_section("grad_heads", terms, heads, section_of[pair], bits))
        return head_parts[-1]

    for pair in range(pairs):
        one = held((length, PAIR), BF16)
        one_sum = held((1, PAIR), F32)
        mixed_grad = after(mixed_grad, token)
        dq, dk, dv, dq_sum, dv_sum = call(
            "back_attend", functools.partial(back_attend_kernel, pair, halves),
            [q, k, v, mixed_grad, mixed, lse], [one, one, one, one_sum, one_sum],
            flops=40 * length * length * PAIR * LONG_AT,
        )
        grads += [dq, dk, dv]
        sums += [dq_sum, dv_sum]
        token = dq_sum
        if pair < pairs - 1:
            token = head_gradient(pair, [token])
        if staged:
            token = (up, down, up)[pair].advance(token)
            if pair == 1:
                token = heads.settle(section_of[0], token)
            if pair == 2:
                token = down.advance(token)
    grads[0] = after(grads[0], token)
    own_proj = call(
        "back_project", back_project_kernel, [*grads, w_qkv], [square(length, F32)],
        flops=6 * length * model * width * LONG_BP,
    )[0]
    got_proj = swap(own_proj)
    token = head_gradient(pairs - 1, [own_proj])
    got_proj = after(got_proj, token)
    input_grad, grad_time, gain1_sum, bias1_sum = call(
        "back_input", functools.partial(back_input_kernel, 256),
        [x, time_embed, own_proj, got_proj, mid_grad, g1],
        [jax.ShapeDtypeStruct((length, model), F32), jax.ShapeDtypeStruct((1, model), F32), vec, vec],
        flops=2 * length * model * width * LONG_BI,
    )
    packed = call(
        "pack", pack_kernel,
        [*down_sums, up_sum, gain2_sum, bias2_sum, out_sum, gain1_sum, bias1_sum,
         *sums[0::2], *sums[1::2]],
        [held((16, model), F32)],
    )[0]

    rows = model // size
    vector = jax.ShapeDtypeStruct((model,), F32)
    small_outs = [vector] * 6
    small_outs += [jax.ShapeDtypeStruct((hidden,), F32), jax.ShapeDtypeStruct((2, width), F32)]
    if staged:
        x_bit, y_bit, z_bit, top_bit = bits
        packed = packed + hop(packed, x_bit)
        wide = [jax.ShapeDtypeStruct((rows, hidden), F32)]
        finish = functools.partial(finish_kernel, 3)
        down_part = call("finish", finish, [*down.keeps, *after(down.arrived(), packed)], wide)[0]
        token = up.advance(down_part)
        packed = heads.advance(token, vector=packed, place=1)
        up_part = call("finish", finish, [*up.keeps, *after(up.arrived(), packed)], wide)[0]
        packed = heads.advance(up_part, vector=packed, place=0)
        packed = heads.advance(packed, vector=packed, place=0)
        qkv_part, out_part, *small = call(
            "finish_heads",
            functools.partial(finish_heads_kernel, [section_of.index(at) for at in range(3)]),
            [*heads.keeps, *heads.arrived(), packed],
            [jax.ShapeDtypeStruct((3, rows, width), F32), jax.ShapeDtypeStruct((rows, width), F32)]
            + small_outs,
        )
        qkv_part = jnp.transpose(qkv_part, (1, 0, 2))
    else:
        for bit in bits[:-1]:
            packed = packed + hop(packed, bit)
        small = call("unpack", unpack_kernel, [packed, hop(packed, bits[-1])], small_outs)
        down_part = jnp.concatenate(down_parts, axis=1)
        up_part = jnp.concatenate(up_parts, axis=1)
        split = 3 * PAIR
        qkv_part = jnp.concatenate([p[:, :split].reshape(rows, 3, PAIR) for p in head_parts], axis=2)
        out_part = jnp.concatenate([p[:, split:] for p in head_parts], axis=1)
    out_sum, gain2_sum, bias2_sum, down_sum, gain1_sum, bias1_sum, up_sum, qv_sum = small

    return (
        jnp.concatenate(out_act, axis=0).reshape(inputs.shape),
        input_grad.reshape(inputs.shape),
        grad_time,
        gain1_sum,
        bias1_sum,
        qkv_part,
        qv_sum,
        out_part.T,
        out_sum,
        gain2_sum,
        bias2_sum,
        up_part,
        up_sum,
        down_part.T,
        down_sum,
        bucket_counts,
    )


def solution(mesh):
    in_specs = (
        P("dp", None, None),
        P("dp", None),
        P("dp", None, None),
        P("dp"),
        P(),
        P(),
        P(None, None, "mp"),
        P(None, "mp"),
        P("mp", None),
        P(),
        P(),
        P(),
        P(None, "mp"),
        P("mp"),
        P("mp", None),
        P(),
    )
    out_specs = (
        P("dp", None, None),
        P("dp", None, None),
        P("dp", None),
        P(),
        P(),
        P("dp", None, "mp"),
        P(None, "mp"),
        P("mp", "dp"),
        P(),
        P(),
        P(),
        P("dp", "mp"),
        P("mp"),
        P("mp", "dp"),
        P(),
        P(),
    )
    return jax.shard_map(local, mesh=mesh, in_specs=in_specs, out_specs=out_specs, check_vma=False)
```

```python
import functools
import math

import jax
import jax.numpy as jnp
from jax import lax
from jax.experimental import pallas as pl
from jax.experimental.pallas import tpu as pltpu
from jax.sharding import PartitionSpec as P

HD = 64
NSTEPS = 2000
NB = 4
PAIR = 2 * HD
VMEM_BYTES = 14 * 2**20
LONG_BF = LONG_BM = LONG_BP = LONG_BI = LONG_GD = 1
LONG_AT = LONG_GU = LONG_GH = 20
LONG_LAST = 20

epsilon = 1e-05
F32 = jnp.float32
BF16 = jnp.bfloat16
NT = (((1,), (1,)), ((), ()))
EXP_SCALE = math.log2(math.e) / math.sqrt(HD)
SCORE_LIMIT = 60.0


def dot(left, right):
    return jnp.dot(left, right, preferred_element_type=F32)


def dot_nt(left, right):
    return lax.dot_general(left, right, NT, preferred_element_type=F32)


def line(ref):
    return ref[...].reshape(1, -1)


def row_mean(value):
    return jnp.mean(value, axis=-1, keepdims=True)


def column_sum(value):
    return jnp.sum(value, axis=0, keepdims=True)


def normed_of(source):
    centred = source - row_mean(source)
    inv_std = lax.rsqrt(row_mean(centred * centred) + epsilon)
    return centred * inv_std, inv_std


def norm_grad(upstream, gain, normed, inv_std):
    scaled = upstream * gain
    inner = scaled - row_mean(scaled) - normed * row_mean(scaled * normed)
    return inv_std * inner


def head_mask(shape, head):
    lane = lax.broadcasted_iota(jnp.int32, shape, 1)
    return (lane >= HD) if head else (lane < HD)


def keep_head(value, head):
    return jnp.where(head_mask(value.shape, head), value, jnp.zeros_like(value))


def blocks_of(count, size):
    return [pl.ds(start, size) for start in range(0, count, size)]


def norm_kernel(rows, x_ref, time_ref, gain_ref, bias_ref, w_ref, qvb_ref, v_ref, in_ref, at_ref):
    for at in blocks_of(x_ref.shape[0], rows):
        residual = x_ref[at, :].astype(F32) + time_ref[...]
        normed, _ = normed_of(residual)
        attn_in = (normed * line(gain_ref) + line(bias_ref)).astype(BF16)
        in_ref[at, :] = attn_in
        at_ref[:, at] = attn_in.T
        v_ref[at, :] = (dot(attn_in, w_ref[2]) + qvb_ref[1:2]).astype(BF16)


def project_kernel(rows, in_ref, w_ref, qvb_ref, q_ref, k_ref, norm_ref):
    width = q_ref.shape[1]
    lane = lax.broadcasted_iota(jnp.int32, (width, 128), 0)
    column = lax.broadcasted_iota(jnp.int32, (width, 128), 1)
    pick = jnp.where(lane // HD == column, 1.0, 0.0).astype(BF16)
    longest = [None, None]
    for at in blocks_of(in_ref.shape[0], rows):
        attn_in = in_ref[at, :]
        queries = dot(attn_in, w_ref[0]) + qvb_ref[0:1]
        keys = dot(attn_in, w_ref[1])
        q_ref[at, :] = queries.astype(BF16)
        k_ref[at, :] = keys.astype(BF16)
        for place, value in enumerate((queries, keys)):
            top = jnp.max(dot((value * value).astype(BF16), pick), axis=0, keepdims=True)
            longest[place] = top if longest[place] is None else jnp.maximum(longest[place], top)
    norm_ref[...] = jnp.concatenate([jnp.broadcast_to(each, (8, 128)) for each in longest], axis=0)


def attend_kernel(rows, q_ref, k_ref, v_ref, norm_ref, mixed_ref, lse_ref, vt_ref):
    length, width = k_ref.shape
    pairs = width // PAIR
    for pair in range(pairs):
        turned = v_ref[:, pair * PAIR : (pair + 1) * PAIR].T
        for head in range(2):
            at = (2 * pair + head) * PAIR
            vt_ref[at : at + HD, :] = turned[head * HD : (head + 1) * HD]
            vt_ref[at + HD : at + PAIR, :] = jnp.ones((HD, length), BF16)

    def attend(place, count, shift):
        at_own = pl.ds(pl.multiple_of(place * count, count), count)
        pieces, stats = [], []
        for pair in range(pairs):
            lanes = slice(pair * PAIR, (pair + 1) * PAIR)
            keys = k_ref[:, lanes]
            queries = q_ref[at_own, lanes]
            for head in range(2):
                scores = dot_nt(keys, keep_head(queries, head))
                if shift:
                    top = jnp.max(scores, axis=0, keepdims=True)
                    expo = jnp.exp2((scores - top) * EXP_SCALE)
                else:
                    expo = jnp.exp2(scores * EXP_SCALE)
                at = (2 * pair + head) * PAIR
                both = dot(vt_ref[at : at + PAIR, :], expo.astype(BF16))
                total = both[HD : HD + 1]
                pieces.append(both[:HD] * (1.0 / total))
                stat = jnp.log2(total)
                stats.append(stat + top * EXP_SCALE if shift else stat)
        while len(stats) < lse_ref.shape[0]:
            stats.append(jnp.zeros_like(stats[0]))
        lse_ref[:, at_own] = jnp.concatenate(stats, axis=0)
        mixed_ref[at_own, :] = jnp.concatenate(pieces, axis=0).T.astype(BF16)

    bound = jnp.max(norm_ref[0:8, :] * norm_ref[8:16, :]) * (1.1 / HD)
    small = bound < SCORE_LIMIT * SCORE_LIMIT

    @pl.when(small)
    def _():
        @pl.loop(0, length // rows)
        def _(place):
            attend(place, rows, False)

    @pl.when(jnp.logical_not(small))
    def _():
        @pl.loop(0, length // 128)
        def _(place):
            attend(place, 128, True)


def join_heads_kernel(start, mixed_ref, ow_ref, part_ref):
    part_ref[...] = dot(mixed_ref[start : start + part_ref.shape[0], :], ow_ref[...])


def normal_parts(v):
    size = jnp.abs(v)
    t = 1.0 / (1.0 + 0.2316419 * size)
    poly = t * (
        0.319381530
        + t * (-0.356563782 + t * (1.781477937 + t * (-1.821255978 + t * 1.330274429)))
    )
    density = jnp.exp2(v * v * (-0.5 * math.log2(math.e))) * (1.0 / math.sqrt(2.0 * math.pi))
    tail = poly * density
    return jnp.where(v < 0.0, tail, 1.0 - tail), density


def feed_kernel(
    start, rows, columns, x_ref, time_ref, own_ref, got_ref, ob_ref, gain_ref, bias_ref, uw_ref,
    ub_ref, dw_ref, part_ref, mid_ref, ft_ref, act_ref, slope_ref,
):
    count = own_ref.shape[0]
    hidden = uw_ref.shape[1]
    for at, at_all in zip(blocks_of(count, rows), range(start, start + count, rows)):
        mid = (
            x_ref[at_all : at_all + rows, :].astype(F32)
            + time_ref[...]
            + (own_ref[at, :] + got_ref[at, :])
            + line(ob_ref)
        )
        mid_ref[at, :] = mid
        normed, _ = normed_of(mid)
        ffn_in = (normed * line(gain_ref) + line(bias_ref)).astype(BF16)
        ft_ref[:, at] = ffn_in.T
        total = None
        for left in range(0, hidden, columns):
            span = slice(left, left + columns)
            preact = dot(ffn_in, uw_ref[:, span]) + line(ub_ref)[:, span]
            phi, density = normal_parts(preact)
            activated = (preact * phi).astype(BF16)
            act_ref[at, span] = activated
            slope_ref[at, span] = (phi + preact * density).astype(BF16)
            term = dot(activated, dw_ref[span, :])
            total = term if total is None else total + term
        part_ref[at, :] = total


def loss_kernel(
    start, rows, mid_ref, own_ref, got_ref, db_ref, goal_ref, weight_ref,
    out_ref, og_ref, low_ref, lt_ref, sum_ref,
):
    total = None
    count = mid_ref.shape[0]
    for at, at_all in zip(blocks_of(count, rows), range(start, start + count, rows)):
        final = mid_ref[at, :] + (own_ref[at, :] + got_ref[at, :]) + line(db_ref)
        out_ref[at, :] = final.astype(BF16)
        goal = goal_ref[at_all : at_all + rows, :].astype(F32)
        out_grad = (final - goal) * weight_ref[0, 0]
        og_ref[at, :] = out_grad
        low = out_grad.astype(BF16)
        low_ref[at, :] = low
        lt_ref[:, at] = low.T
        term = column_sum(out_grad)
        total = term if total is None else total + term
    sum_ref[...] = total


def back_feed_kernel(
    rows, columns, low_a, low_b, slope_a, slope_b, uw_ref, dw_ref, pre_ref, part_ref, sum_ref
):
    half = low_a.shape[0]
    hidden = uw_ref.shape[1]
    sums = [None] * (hidden // columns)
    for place, (low_ref, slope_ref) in enumerate(((low_a, slope_a), (low_b, slope_b))):
        for at, at_all in zip(blocks_of(half, rows), range(place * half, (place + 1) * half, rows)):
            out_low = low_ref[at, :]
            total = None
            for part in range(hidden // columns):
                span = slice(part * columns, (part + 1) * columns)
                pre_grad = slope_ref[at, span].astype(F32) * dot_nt(out_low, dw_ref[span, :])
                term = column_sum(pre_grad)
                sums[part] = term if sums[part] is None else sums[part] + term
                low = pre_grad.astype(BF16)
                pre_ref[at_all : at_all + rows, span] = low
                term = dot_nt(low, uw_ref[:, span])
                total = term if total is None else total + term
            part_ref[at_all : at_all + rows, :] = total
    sum_ref[...] = jnp.concatenate(sums, axis=1)


def back_mid_kernel(
    rows, mid_a, mid_b, og_a, og_b, own_ref, got_ref, gain_ref, ow_ref,
    mg_ref, mt_ref, mixed_ref, gain_sum_ref, bias_sum_ref, out_sum_ref,
):
    half = mid_a.shape[0]
    sums = [0.0, 0.0, 0.0]
    for place, (mid_ref, og_ref) in enumerate(((mid_a, og_a), (mid_b, og_b))):
        for at, at_all in zip(blocks_of(half, rows), range(place * half, (place + 1) * half, rows)):
            span = slice(at_all, at_all + rows)
            normed, inv_std = normed_of(mid_ref[at, :])
            upstream = own_ref[span, :] + got_ref[span, :]
            mid_grad = og_ref[at, :] + norm_grad(upstream, line(gain_ref), normed, inv_std)
            mg_ref[span, :] = mid_grad
            low = mid_grad.astype(BF16)
            mt_ref[:, span] = low.T
            mixed_ref[span, :] = dot_nt(low, ow_ref[...]).astype(BF16)
            for which, value in enumerate((upstream * normed, upstream, mid_grad)):
                sums[which] = sums[which] + column_sum(value)
    gain_sum_ref[...], bias_sum_ref[...], out_sum_ref[...] = sums


def back_attend_kernel(
    pair, blocks, q_ref, k_ref, v_ref, do_ref, o_ref, lse_ref,
    dq_ref, dk_ref, dv_ref, dq_sum_ref, dv_sum_ref,
):
    scale = 1.0 / math.sqrt(HD)
    lanes = slice(pair * PAIR, (pair + 1) * PAIR)
    half = o_ref.shape[0] // blocks
    keys, values = k_ref[:, lanes], v_ref[:, lanes]
    keys_t = keys.T
    dk, dv, dq_sum = None, None, None
    for place in range(blocks):
        span = slice(place * half, (place + 1) * half)
        queries, upstream = q_ref[span, lanes], do_ref[span, lanes]
        both = (upstream.astype(F32) * o_ref[span, lanes].astype(F32)).T
        pieces = []
        for head in range(2):
            own_queries = keep_head(queries, head)
            own_upstream = keep_head(upstream, head)
            row_dot = column_sum(both[head * HD : (head + 1) * HD])
            log_total = lse_ref[2 * pair + head : 2 * pair + head + 1, span]
            scores = dot_nt(keys, own_queries)
            probs = jnp.exp2(scores * EXP_SCALE - log_total)
            prob_grad = dot_nt(values, own_upstream)
            score_grad = (probs * (prob_grad - row_dot)).astype(BF16)
            dv_term = dot(probs.astype(BF16), own_upstream)
            dk_term = dot(score_grad, own_queries)
            dv = dv_term if dv is None else dv + dv_term
            dk = dk_term if dk is None else dk + dk_term
            pieces.append(dot(keys_t[head * HD : (head + 1) * HD, :], score_grad))
        query_grad = jnp.concatenate(pieces, axis=0).T * scale
        dq_ref[span, :] = query_grad.astype(BF16)
        term = column_sum(query_grad)
        dq_sum = term if dq_sum is None else dq_sum + term
    dk_ref[...] = (dk * scale).astype(BF16)
    dv_ref[...] = dv.astype(BF16)
    dq_sum_ref[...] = dq_sum
    dv_sum_ref[...] = column_sum(dv)


def back_project_kernel(*refs):
    w_ref, part_ref = refs[-2:]
    pairs = (len(refs) - 2) // 3
    total = None
    for kind in range(3):
        grad = jnp.concatenate([refs[3 * pair + kind][...] for pair in range(pairs)], axis=1)
        term = dot_nt(grad, w_ref[kind])
        total = term if total is None else total + term
    part_ref[...] = total


def back_input_kernel(
    rows, x_ref, time_ref, own_ref, got_ref, mg_ref, gain_ref,
    out_ref, time_sum_ref, gain_sum_ref, bias_sum_ref,
):
    sums = [0.0, 0.0, 0.0]
    for at in blocks_of(x_ref.shape[0], rows):
        normed, inv_std = normed_of(x_ref[at, :].astype(F32) + time_ref[...])
        upstream = own_ref[at, :] + got_ref[at, :]
        grad = mg_ref[at, :] + norm_grad(upstream, line(gain_ref), normed, inv_std)
        out_ref[at, :] = grad
        for which, value in enumerate((grad, upstream * normed, upstream)):
            sums[which] = sums[which] + column_sum(value)
    time_sum_ref[...], gain_sum_ref[...], bias_sum_ref[...] = sums


def gathered(refs, start, count):
    return jnp.concatenate([ref[pl.ds(start, count), :] for ref in refs], axis=1)


def stacked(refs, columns):
    return jnp.concatenate([ref[:, columns] for ref in refs], axis=0)


def weight_kernel(chunk, count, terms, from_ref, *refs):
    keep_ref, send_ref = refs[-2:]
    half = count // 2
    for target, first in ((send_ref, half), (keep_ref, 0)):
        starts = [pl.multiple_of(from_ref[first + place] * chunk, 16) for place in range(half)]
        at, out_at = 0, 0
        for lefts, rights, columns in terms:
            left_refs = refs[at : at + lefts]
            right_refs = refs[at + lefts : at + lefts + rights]
            at += lefts + rights
            left = jnp.concatenate([gathered(left_refs, start, chunk) for start in starts], axis=0)
            right = stacked(right_refs, columns)
            target[:, out_at : out_at + right.shape[1]] = dot(left, right)
            out_at += right.shape[1]


def whole_weight_kernel(terms, *refs):
    at, out_at = 0, 0
    for lefts, rights, columns in terms:
        left = jnp.concatenate([ref[...] for ref in refs[at : at + lefts]], axis=1)
        right = stacked(refs[at + lefts : at + lefts + rights], columns)
        at += lefts + rights
        refs[-1][:, out_at : out_at + right.shape[1]] = dot(left, right)
        out_at += right.shape[1]


def step_kernel(settled, got_places, send_groups, vec_in, vec_out, *refs):
    count = len(settled)
    keeps, refs = refs[:count], refs[count:]
    total_gots = 1 + max(which for which, _ in got_places if which is not None)
    gots, refs = refs[:total_gots], refs[total_gots:]
    vector = None
    if vec_out is not None:
        vector, refs = refs[0][...], refs[1:]
        if vec_in == "other":
            other, refs = refs[0], refs[1:]
            vector = vector + get_vector(other, other.shape[0] - vector_rows(vector.shape, other.shape[1]), vector.shape)
            vec_in = None
    sends, news, refs = refs[: len(send_groups)], refs[len(send_groups) :][:count], refs[len(send_groups) + count :]
    rows, width = keeps[0].shape
    half = rows // 2
    for section, (which, at) in enumerate(got_places):
        total = keeps[section][...]
        if not settled[section]:
            total = total + gots[which][:rows, at * width : (at + 1) * width]
        news[section][...] = total[:half]
        for target, group in zip(sends, send_groups):
            if section in group:
                to = group.index(section) * width
                target[:half, to : to + width] = total[half:]
    if vector is not None:
        if vec_in is not None:
            vector = vector + get_vector(gots[vec_in], rows, vector.shape)
        put_vector(sends[vec_out], half, vector)
        refs[0][...] = vector


def vector_rows(shape, width):
    return 8 * -(-(shape[0] // 8) // (width // shape[1]))


def vector_spots(shape, width):
    each = width // shape[1]
    for block in range(shape[0] // 8):
        row, column = 8 * (block // each), shape[1] * (block % each)
        yield slice(8 * block, 8 * block + 8), slice(row, row + 8), slice(column, column + shape[1])


def put_vector(target, first, vector):
    for own, at, columns in vector_spots(vector.shape, target.shape[1]):
        target[first + at.start : first + at.stop, columns] = vector[own]


def get_vector(source, first, shape):
    parts = []
    for _, at, columns in vector_spots(shape, source.shape[1]):
        parts.append(source[first + at.start : first + at.stop, columns])
    return jnp.concatenate(parts, axis=0)


def settle_kernel(keep_ref, got_ref, out_ref):
    out_ref[...] = keep_ref[...] + got_ref[...]


def finish_kernel(count, *refs):
    keeps, got_ref, outs = refs[:count], refs[count], refs[count + 1 :]
    width = keeps[0].shape[1]
    share = count // len(outs)
    for place, keep in enumerate(keeps):
        total = keep[...] + got_ref[:, place * width : (place + 1) * width]
        at = (place % share) * width
        outs[place // share][:, at : at + width] = total


def finish_heads_kernel(pair_of, keep_a, keep_b, keep_c, got_ref, vector_ref, qkv_ref, out_ref, *smalls):
    rows, width = keep_a.shape
    for place, keep in enumerate((keep_a, keep_b, keep_c)):
        total = keep[...] + got_ref[:rows, place * width : (place + 1) * width]
        lanes = slice(pair_of[place] * PAIR, (pair_of[place] + 1) * PAIR)
        for kind in range(3):
            qkv_ref[kind, :, lanes] = total[:, kind * PAIR : (kind + 1) * PAIR]
        out_ref[:, lanes] = total[:, 3 * PAIR :]
    unpack(vector_ref[...] + get_vector(got_ref, rows, vector_ref.shape), *smalls)


def pack_kernel(*refs):
    out_ref = refs[-1]
    down_a, down_b, up, gain2, bias2, out, gain1, bias1 = refs[:8]
    model = 2 * out_ref.shape[1]
    wide = up.shape[1] // model
    rows = [out[...], gain2[...], bias2[...], down_a[...] + down_b[...], gain1[...], bias1[...]]
    rows += [up[:, at * model : (at + 1) * model] for at in range(wide)]
    rows.append(jnp.concatenate([ref[...] for ref in refs[8:-1]], axis=1))
    height, half = out_ref.shape[0] // 2, out_ref.shape[1]
    rows.append(jnp.zeros((height - len(rows), 2 * half), F32))
    whole = jnp.concatenate(rows, axis=0)
    out_ref[...] = jnp.concatenate([whole[:, :half], whole[:, half:]], axis=0)


def unpack_kernel(own_ref, got_ref, *outs):
    unpack(own_ref[...] + got_ref[...], *outs)


def unpack(halves, *outs):
    height = halves.shape[0] // 2
    total = jnp.concatenate([halves[:height], halves[height:]], axis=1)
    model = total.shape[1]
    for place in range(6):
        outs[place][...] = total[place]
    wide = outs[6].shape[0] // model
    for at in range(wide):
        outs[6][at * model : (at + 1) * model] = total[6 + at]
    width = outs[7].shape[1]
    last = total[6 + wide : 7 + wide]
    outs[7][...] = jnp.concatenate([last[:, :width], last[:, width : 2 * width]], axis=0)


def held(shape, dtype):
    return pltpu.VMEM(shape, dtype)


def call(name, kernel, args, outs, scratch=(), flops=0, scalars=(), pins=(), plain=()):
    if pins:
        count, inner = len(args), kernel
        kernel = lambda *refs: inner(*refs[:count], *refs[count + len(pins) :])
        args = [*args, *pins]
    whole = pl.BlockSpec(memory_space=pltpu.VMEM)
    specs = [
        pl.BlockSpec(memory_space=pltpu.SMEM) if place in scalars else whole
        for place in range(len(args))
    ]
    args = [
        arg if place in scalars
        else pltpu.with_memory_space_constraint(arg, pltpu.HBM if place in plain else pltpu.VMEM)
        for place, arg in enumerate(args)
    ]
    moved = sum(math.prod(a.shape) * a.dtype.itemsize for a in outs)
    return pl.pallas_call(
        kernel,
        name=name,
        in_specs=specs,
        out_specs=[whole] * len(outs),
        out_shape=outs,
        scratch_shapes=list(scratch),
        compiler_params=pltpu.CompilerParams(vmem_limit_bytes=VMEM_BYTES),
        cost_estimate=pl.CostEstimate(flops=int(flops), bytes_accessed=int(moved), transcendentals=0),
    )(*args)


def after(values, *others):
    return lax.optimization_barrier((values, others))[0]


def swap(value):
    return lax.ppermute(value, "mp", [(0, 1), (1, 0)])


def xor_pairs(size, bit):
    return [(index, index ^ bit) for index in range(size)]


def axis_bits(size):
    return [1 << place for place in range(size.bit_length() - 1)]


def hop(value, bit):
    return lax.ppermute(value, "dp", xor_pairs(lax.axis_size("dp"), bit))


def halve(section, order):
    size = lax.axis_size("dp")
    me = lax.axis_index("dp")
    left = sorted(order, reverse=True)
    rows, columns = section.shape
    section = section.reshape((2,) * len(left) + (rows // size, columns))
    for bit in order:
        at = left.index(bit)
        mine = (me // bit) % 2
        send = lax.dynamic_index_in_dim(section, 1 - mine, at, keepdims=False)
        keep = lax.dynamic_index_in_dim(section, mine, at, keepdims=False)
        section = keep + hop(send, bit)
        left.remove(bit)
    return section


def chunk_sources(order):
    me = lax.axis_index("dp")
    places = []
    for place in range(1 << len(order)):
        relative = 0
        for step, bit in enumerate(order):
            if (place >> (len(order) - 1 - step)) & 1:
                relative |= bit
        places.append(relative)
    return jnp.array(places, jnp.int32) ^ me


class Halving:
    def __init__(self, orders, plan):
        self.orders = orders
        self.plan = list(plan)
        self.keeps = [None] * len(orders)
        self.sends = [None] * len(orders)
        self.gots = []
        self.settled = [False] * len(orders)
        self.vector_at = None

    def start(self, places=None):
        for place, (_, bit) in enumerate(self.plan[0]):
            if places is None or place in places:
                self.gots.append((place, hop(self.sends[place], bit)))

    def settle(self, section, *others):
        which = [place for place, (group, _) in enumerate(self.plan[0]) if group == [section]][0]
        got = dict(self.gots)[which]
        self.gots = [each for each in self.gots if each[0] != which]
        keep, got = after((self.keeps[section], got), *others)
        self.keeps[section] = call("settle", settle_kernel, [keep, got], [held(keep.shape, F32)])[0]
        self.settled[section] = True
        return self.keeps[section]

    def advance(self, *others, vector=None, place=None, other=None, start=True):
        order = sorted(self.gots, key=lambda pair: pair[0])
        gots = after([got for _, got in order], *others)
        count = len(self.keeps)
        places = [(None, None)] * count
        for which, (slot, _) in enumerate(order):
            for at, section in enumerate(self.plan[0][slot][0]):
                places[section] = (which, at)
        vec_in = None
        if self.vector_at is not None:
            vec_in = [slot for slot, _ in order].index(self.vector_at)
        if other is not None:
            vec_in = "other"
        self.plan = self.plan[1:]
        self.gots = []
        groups = [group for group, _ in self.plan[0]]
        rows, width = self.keeps[0].shape
        half = rows // 2
        extra = [0] * len(groups)
        if vector is not None:
            extra[place] = vector_rows(vector.shape, width * len(groups[place]))
        outs = [held((half + more, width * len(group)), F32) for group, more in zip(groups, extra)]
        outs += [held((half, width), F32)] * count
        args = [*self.keeps, *gots]
        if vector is not None:
            args += [vector] if other is None else [vector, other]
            outs.append(held(vector.shape, F32))
        outs = call(
            "halve", functools.partial(step_kernel, self.settled, places, groups, vec_in, place), args, outs
        )
        self.settled = [False] * count
        self.sends, self.keeps = list(outs[: len(groups)]), list(outs[len(groups) :][:count])
        self.vector_at = place
        if start:
            self.start()
        return self.keeps[0] if vector is None else outs[-1]

    def arrived(self):
        return [got for _, got in self.gots]


def two_axes(bits, turned):
    a, b, z, top = bits
    if turned:
        a, b = b, a
    orders = [[a, b, z, top], [b, a, z, top], [z, a, b, top]]
    plan = [
        [([0], a), ([1], b), ([2], z)],
        [([0], b), ([1, 2], a)],
        [([0, 1], z), ([2], b)],
        [([0, 1, 2], top)],
    ]
    return Halving(orders, plan)


def weight_section(name, terms, state, section, order, start=True):
    size = lax.axis_size("dp")
    model = terms[0][0][0].shape[0]
    chunk = model // size
    tokens = sum(left.shape[1] for left in terms[0][0])
    width = sum(columns.stop - columns.start for _, _, columns in terms)
    shape = [(len(left), len(right), columns) for left, right, columns in terms]
    flat = [piece for left, right, _ in terms for piece in [*left, *right]]
    flops = 2 * model * tokens * width * {'grad_down': LONG_GD, 'grad_up': LONG_GU, 'grad_heads': LONG_GH}[name]
    if state is None:
        whole = call(
            name, functools.partial(whole_weight_kernel, shape), flat,
            [held((model, width), F32)], flops=flops,
        )[0]
        return halve(whole, order)
    keep, send = call(
        name, functools.partial(weight_kernel, chunk, size, shape),
        [chunk_sources(state.orders[section]), *flat], [held((model // 2, width), F32)] * 2,
        flops=flops, scalars=(0,),
    )
    state.keeps[section], state.sends[section] = keep, send
    if start:
        state.start([section])
    return send


def local(
    inputs,
    time_embed,
    targets,
    timesteps,
    ln1_gain,
    ln1_bias,
    qkv_weight,
    qv_bias,
    out_weight,
    out_bias,
    ln2_gain,
    ln2_bias,
    up_weight,
    up_bias,
    down_weight,
    down_bias,
):
    seq_count, length, model = inputs.shape
    width = qkv_weight.shape[2]
    hidden = up_weight.shape[1]
    size = lax.axis_size("dp")
    bits = axis_bits(size)
    halves = 2
    part_rows = length // halves
    pairs = width // PAIR
    x = inputs.reshape(length, model)
    goal = targets.reshape(length, model)
    w_qkv = jnp.transpose(qkv_weight, (1, 0, 2))
    g1, b1, g2, b2 = ln1_gain, ln1_bias, ln2_gain, ln2_bias
    ob, ub, db = out_bias, up_bias, down_bias

    buckets = (
        (timesteps >= NSTEPS // 64).astype(jnp.int32)
        + (timesteps >= NSTEPS // 16).astype(jnp.int32)
        + (timesteps >= NSTEPS // 4).astype(jnp.int32)
    )
    one_hot = buckets[:, None] == jnp.arange(NB, dtype=jnp.int32)[None, :]
    bucket_counts = jnp.sum(one_hot.astype(jnp.int32), axis=0)

    def count_hop(counts, bits):
        for bit in bits:
            counts = counts + hop(counts, bit)
        return counts

    vec = held((1, model), F32)

    def square(rows, dtype):
        return held((rows, model), dtype)

    v, attn_in, attn_t = call(
        "norm", functools.partial(norm_kernel, 256),
        [x, time_embed, g1, b1, w_qkv, qv_bias],
        [held((length, width), BF16), held((length, model), BF16), held((model, length), BF16)],
        flops=2 * length * model * width, plain=range(6),
    )
    attn_in, bucket_counts = lax.optimization_barrier((attn_in, bucket_counts))
    bucket_counts = count_hop(bucket_counts, bits[:1])
    q, k, lengths = call(
        "project", functools.partial(project_kernel, 256),
        [attn_in, w_qkv, qv_bias],
        [held((length, width), BF16)] * 2 + [held((16, 128), F32)],
        flops=4 * length * model * width,
    )

    q, bucket_counts = lax.optimization_barrier((q, bucket_counts))
    bucket_counts = count_hop(bucket_counts, bits[1:2])
    mixed, lse = call(
        "attend", functools.partial(attend_kernel, part_rows),
        [q, k, v, lengths],
        [held((length, width), BF16), held((8, length), F32)],
        scratch=[pltpu.VMEM((2 * width, length), BF16)],
        flops=16 * length * length * width,
    )
    mixed, bucket_counts = lax.optimization_barrier((mixed, bucket_counts))
    bucket_counts = count_hop(bucket_counts, bits[2:])
    own_attn, got_attn = [], []
    for half in range(halves):
        own_attn.append(call(
            "join_heads", functools.partial(join_heads_kernel, half * part_rows), [mixed, out_weight],
            [square(part_rows, F32)], flops=2 * part_rows * width * model,
        )[0])
        got_attn.append(swap(own_attn[half]))
        if half == 0:
            mixed = after(mixed, own_attn[0])
    own_attn[0], bucket_counts = lax.optimization_barrier((own_attn[0], bucket_counts))

    own_feed, mid, feed_t, activated, slope, got_feed = [], [], [], [], [], []
    for half in range(halves):
        outs = call(
            "feed", functools.partial(feed_kernel, half * part_rows, part_rows, hidden),
            [x, time_embed, own_attn[half], got_attn[half], ob, g2, b2, up_weight, ub, down_weight],
            [square(part_rows, F32), square(part_rows, F32), held((model, part_rows), BF16),
             held((part_rows, hidden), BF16), held((part_rows, hidden), BF16)],
            flops=4 * length * model * hidden // halves,
            pins=[*mid, *feed_t, *activated, *slope] + [goal] * half,
        )
        for kept, value in zip((own_feed, mid, feed_t, activated, slope), outs):
            kept.append(value)
        got_feed.append(swap(outs[0]))
        if half == 0:
            own_attn[1] = after(own_attn[1], outs[0])

    floors = jnp.maximum(bucket_counts, 1).astype(F32)
    total_seqs = seq_count * size
    seq_weight = total_seqs / (NB * jnp.sum(jnp.where(one_hot, floors[None, :], 0.0), axis=1))
    weight = seq_weight.reshape(1, 1)

    out_act, out_grad, out_low, out_t, down_sums = [], [], [], [], []
    for half in range(halves):
        outs = call(
            "loss", functools.partial(loss_kernel, half * part_rows, 256),
            [mid[half], own_feed[half], got_feed[half], db, goal, weight],
            [square(part_rows, BF16), square(part_rows, F32), square(part_rows, BF16),
             held((model, part_rows), BF16), vec],
            scalars=(5,),
        )
        for kept, value in zip((out_act, out_grad, out_low, out_t, down_sums), outs):
            kept.append(value)

    staged = size == 16 and (model // size) % 16 == 0
    down, up, heads = [two_axes(bits, turned) if staged else None for turned in (False, True, True)]
    third = hidden // 3
    thirds = [slice(at * third, (at + 1) * third) for at in range(3)]
    down_parts, up_parts, head_parts = [], [], []
    for section, columns in enumerate(thirds):
        down_parts.append(weight_section("grad_down", [(out_t, activated, columns)], down, section, bits))

    out_low = after(out_low, *down_parts)
    pre_low, own_pre, up_sum = call(
        "back_feed", functools.partial(back_feed_kernel, 256, 512),
        [*out_low, *slope, up_weight, down_weight],
        [held((length, hidden), BF16), square(length, F32), held((1, hidden), F32)],
        flops=4 * length * model * hidden * LONG_BF,
    )
    got_pre = swap(own_pre)
    for section, columns in enumerate(thirds):
        up_parts.append(weight_section("grad_up", [(feed_t, [pre_low], columns)], up, section, bits))

    got_pre = after(got_pre, *up_parts)
    mid_grad, mid_t, mixed_grad, gain2_sum, bias2_sum, out_sum = call(
        "back_mid", functools.partial(back_mid_kernel, 256),
        [*mid, *out_grad, own_pre, got_pre, g2, out_weight],
        [square(length, F32), held((model, length), BF16), held((length, width), BF16)] + [vec] * 3,
        flops=2 * length * model * width * LONG_BM,
    )
    token = down.advance(out_sum) if staged else out_sum

    grads, sums = [], []
    section_of = [2, 0, 1]

    def head_gradient(pair, others, start=True):
        terms = [([after(attn_t, *others)], [grad], slice(0, PAIR)) for grad in grads[3 * pair :]]
        terms.append(([mid_t], [mixed], slice(pair * PAIR, (pair + 1) * PAIR)))
        head_parts.append(weight_section("grad_heads", terms, heads, section_of[pair], bits, start))
        return head_parts[-1]

    for pair in range(pairs):
        one = held((length, PAIR), BF16)
        one_sum = held((1, PAIR), F32)
        mixed_grad = after(mixed_grad, token)
        dq, dk, dv, dq_sum, dv_sum = call(
            "back_attend", functools.partial(back_attend_kernel, pair, halves),
            [q, k, v, mixed_grad, mixed, lse], [one, one, one, one_sum, one_sum],
            flops=40 * length * length * PAIR * LONG_AT,
        )
        grads += [dq, dk, dv]
        sums += [dq_sum, dv_sum]
        token = dq_sum
        if pair < pairs - 1:
            token = head_gradient(pair, [token])
        if staged:
            token = (up, down, up)[pair].advance(token)
            if pair == 1:
                token = heads.settle(section_of[0], token)
            if pair == 2:
                token = down.advance(token)
    grads[0] = after(grads[0], token)
    own_proj = call(
        "back_project", back_project_kernel, [*grads, w_qkv], [square(length, F32)],
        flops=6 * length * model * width * LONG_BP,
    )[0]
    got_proj = swap(own_proj)
    token = head_gradient(pairs - 1, [own_proj])
    got_proj = after(got_proj, token)
    input_grad, grad_time, gain1_sum, bias1_sum = call(
        "back_input", functools.partial(back_input_kernel, 256),
        [x, time_embed, own_proj, got_proj, mid_grad, g1],
        [jax.ShapeDtypeStruct((length, model), F32), jax.ShapeDtypeStruct((1, model), F32), vec, vec],
        flops=2 * length * model * width * LONG_BI,
    )
    packed = call(
        "pack", pack_kernel,
        [*down_sums, up_sum, gain2_sum, bias2_sum, out_sum, gain1_sum, bias1_sum,
         *sums[0::2], *sums[1::2]],
        [held((24, model // 2), F32)],
    )[0]

    rows = model // size
    vector = jax.ShapeDtypeStruct((model,), F32)
    small_outs = [vector] * 6
    small_outs += [jax.ShapeDtypeStruct((hidden,), F32), jax.ShapeDtypeStruct((2, width), F32)]
    if staged:
        packed = packed + hop(packed, bits[2])
        wide = [jax.ShapeDtypeStruct((rows, hidden), F32)]
        finish = functools.partial(finish_kernel, 3)
        down_part = call("finish", finish, [*down.keeps, *after(down.arrived(), packed)], wide)[0]
        token = up.advance(down_part)
        packed = heads.advance(token, vector=packed, place=1)
        up_part = call("finish", finish, [*up.keeps, *after(up.arrived(), packed)], wide)[0]
        packed = heads.advance(up_part, vector=packed, place=1)
        packed = heads.advance(packed, vector=packed, place=0)
        qkv_part, out_part, *small = call(
            "finish_heads",
            functools.partial(finish_heads_kernel, [section_of.index(at) for at in range(3)]),
            [*heads.keeps, *heads.arrived(), packed],
            [jax.ShapeDtypeStruct((3, rows, width), F32), jax.ShapeDtypeStruct((rows, width), F32)]
            + small_outs,
        )
        qkv_part = jnp.transpose(qkv_part, (1, 0, 2))
    else:
        for bit in bits[:-1]:
            packed = packed + hop(packed, bit)
        small = call("unpack", unpack_kernel, [packed, hop(packed, bits[-1])], small_outs)
        down_part = jnp.concatenate(down_parts, axis=1)
        up_part = jnp.concatenate(up_parts, axis=1)
        split = 3 * PAIR
        qkv_part = jnp.concatenate([p[:, :split].reshape(rows, 3, PAIR) for p in head_parts], axis=2)
        out_part = jnp.concatenate([p[:, split:] for p in head_parts], axis=1)
    out_sum, gain2_sum, bias2_sum, down_sum, gain1_sum, bias1_sum, up_sum, qv_sum = small

    return (
        jnp.concatenate(out_act, axis=0).reshape(inputs.shape),
        input_grad.reshape(inputs.shape),
        grad_time,
        gain1_sum,
        bias1_sum,
        qkv_part,
        qv_sum,
        out_part.T,
        out_sum,
        gain2_sum,
        bias2_sum,
        up_part,
        up_sum,
        down_part.T,
        down_sum,
        bucket_counts,
    )


def solution(mesh):
    in_specs = (
        P("dp", None, None),
        P("dp", None),
        P("dp", None, None),
        P("dp"),
        P(),
        P(),
        P(None, None, "mp"),
        P(None, "mp"),
        P("mp", None),
        P(),
        P(),
        P(),
        P(None, "mp"),
        P("mp"),
        P("mp", None),
        P(),
    )
    out_specs = (
        P("dp", None, None),
        P("dp", None, None),
        P("dp", None),
        P(),
        P(),
        P("dp", None, "mp"),
        P(None, "mp"),
        P("mp", "dp"),
        P(),
        P(),
        P(),
        P("dp", "mp"),
        P("mp"),
        P("mp", "dp"),
        P(),
        P(),
    )
    return jax.shard_map(local, mesh=mesh, in_specs=in_specs, out_specs=out_specs, check_vma=False)
```

```python
import functools
import math

import jax
import jax.numpy as jnp
from jax import lax
from jax.experimental import pallas as pl
from jax.experimental.pallas import tpu as pltpu
from jax.sharding import PartitionSpec as P

HD = 64
NSTEPS = 2000
NB = 4
PAIR = 2 * HD
VMEM_BYTES = 14 * 2**20
LONG_BF = LONG_BM = LONG_BP = LONG_BI = LONG_GD = 1
LONG_AT = LONG_GU = LONG_GH = 20
LONG_LAST = 20

epsilon = 1e-05
F32 = jnp.float32
BF16 = jnp.bfloat16
NT = (((1,), (1,)), ((), ()))
EXP_SCALE = math.log2(math.e) / math.sqrt(HD)
SCORE_LIMIT = 60.0


def dot(left, right):
    return jnp.dot(left, right, preferred_element_type=F32)


def dot_nt(left, right):
    return lax.dot_general(left, right, NT, preferred_element_type=F32)


def line(ref):
    return ref[...].reshape(1, -1)


def row_mean(value):
    return jnp.mean(value, axis=-1, keepdims=True)


def column_sum(value):
    return jnp.sum(value, axis=0, keepdims=True)


def normed_of(source):
    centred = source - row_mean(source)
    inv_std = lax.rsqrt(row_mean(centred * centred) + epsilon)
    return centred * inv_std, inv_std


def norm_grad(upstream, gain, normed, inv_std):
    scaled = upstream * gain
    inner = scaled - row_mean(scaled) - normed * row_mean(scaled * normed)
    return inv_std * inner


def head_mask(shape, head):
    lane = lax.broadcasted_iota(jnp.int32, shape, 1)
    return (lane >= HD) if head else (lane < HD)


def keep_head(value, head):
    return jnp.where(head_mask(value.shape, head), value, jnp.zeros_like(value))


def blocks_of(count, size):
    return [pl.ds(start, size) for start in range(0, count, size)]


def norm_kernel(rows, x_ref, time_ref, gain_ref, bias_ref, w_ref, qvb_ref, v_ref, in_ref, at_ref):
    for at in blocks_of(x_ref.shape[0], rows):
        residual = x_ref[at, :].astype(F32) + time_ref[...]
        normed, _ = normed_of(residual)
        attn_in = (normed * line(gain_ref) + line(bias_ref)).astype(BF16)
        in_ref[at, :] = attn_in
        at_ref[:, at] = attn_in.T
        v_ref[at, :] = (dot(attn_in, w_ref[2]) + qvb_ref[1:2]).astype(BF16)


def project_kernel(rows, in_ref, w_ref, qvb_ref, q_ref, k_ref, norm_ref):
    width = q_ref.shape[1]
    lane = lax.broadcasted_iota(jnp.int32, (width, 128), 0)
    column = lax.broadcasted_iota(jnp.int32, (width, 128), 1)
    pick = jnp.where(lane // HD == column, 1.0, 0.0).astype(BF16)
    longest = [None, None]
    for at in blocks_of(in_ref.shape[0], rows):
        attn_in = in_ref[at, :]
        queries = dot(attn_in, w_ref[0]) + qvb_ref[0:1]
        keys = dot(attn_in, w_ref[1])
        q_ref[at, :] = queries.astype(BF16)
        k_ref[at, :] = keys.astype(BF16)
        for place, value in enumerate((queries, keys)):
            top = jnp.max(dot((value * value).astype(BF16), pick), axis=0, keepdims=True)
            longest[place] = top if longest[place] is None else jnp.maximum(longest[place], top)
    norm_ref[...] = jnp.concatenate([jnp.broadcast_to(each, (8, 128)) for each in longest], axis=0)


def attend_kernel(rows, q_ref, k_ref, v_ref, norm_ref, mixed_ref, lse_ref, vt_ref):
    length, width = k_ref.shape
    pairs = width // PAIR
    for pair in range(pairs):
        turned = v_ref[:, pair * PAIR : (pair + 1) * PAIR].T
        for head in range(2):
            at = (2 * pair + head) * PAIR
            vt_ref[at : at + HD, :] = turned[head * HD : (head + 1) * HD]
            vt_ref[at + HD : at + PAIR, :] = jnp.ones((HD, length), BF16)

    def attend(place, count, shift):
        at_own = pl.ds(pl.multiple_of(place * count, count), count)
        pieces, stats = [], []
        for pair in range(pairs):
            lanes = slice(pair * PAIR, (pair + 1) * PAIR)
            keys = k_ref[:, lanes]
            queries = q_ref[at_own, lanes]
            for head in range(2):
                scores = dot_nt(keys, keep_head(queries, head))
                if shift:
                    top = jnp.max(scores, axis=0, keepdims=True)
                    expo = jnp.exp2((scores - top) * EXP_SCALE)
                else:
                    expo = jnp.exp2(scores * EXP_SCALE)
                at = (2 * pair + head) * PAIR
                both = dot(vt_ref[at : at + PAIR, :], expo.astype(BF16))
                total = both[HD : HD + 1]
                pieces.append(both[:HD] * (1.0 / total))
                stat = jnp.log2(total)
                stats.append(stat + top * EXP_SCALE if shift else stat)
        while len(stats) < lse_ref.shape[0]:
            stats.append(jnp.zeros_like(stats[0]))
        lse_ref[:, at_own] = jnp.concatenate(stats, axis=0)
        mixed_ref[at_own, :] = jnp.concatenate(pieces, axis=0).T.astype(BF16)

    bound = jnp.max(norm_ref[0:8, :] * norm_ref[8:16, :]) * (1.1 / HD)
    small = bound < SCORE_LIMIT * SCORE_LIMIT

    @pl.when(small)
    def _():
        @pl.loop(0, length // rows)
        def _(place):
            attend(place, rows, False)

    @pl.when(jnp.logical_not(small))
    def _():
        @pl.loop(0, length // 128)
        def _(place):
            attend(place, 128, True)


def join_heads_kernel(start, mixed_ref, ow_ref, part_ref):
    part_ref[...] = dot(mixed_ref[start : start + part_ref.shape[0], :], ow_ref[...])


def normal_parts(v):
    size = jnp.abs(v)
    t = 1.0 / (1.0 + 0.2316419 * size)
    poly = t * (
        0.319381530
        + t * (-0.356563782 + t * (1.781477937 + t * (-1.821255978 + t * 1.330274429)))
    )
    density = jnp.exp2(v * v * (-0.5 * math.log2(math.e))) * (1.0 / math.sqrt(2.0 * math.pi))
    tail = poly * density
    return jnp.where(v < 0.0, tail, 1.0 - tail), density


def feed_kernel(
    start, rows, columns, x_ref, time_ref, own_ref, got_ref, ob_ref, gain_ref, bias_ref, uw_ref,
    ub_ref, dw_ref, db_ref, part_ref, mid_ref, ft_ref, act_ref, slope_ref,
):
    count = own_ref.shape[0]
    hidden = uw_ref.shape[1]
    for at, at_all in zip(blocks_of(count, rows), range(start, start + count, rows)):
        mid = (
            x_ref[at_all : at_all + rows, :].astype(F32)
            + time_ref[...]
            + (own_ref[at, :] + got_ref[at, :])
            + line(ob_ref)
        )
        mid_ref[at, :] = mid
        normed, _ = normed_of(mid)
        ffn_in = (normed * line(gain_ref) + line(bias_ref)).astype(BF16)
        ft_ref[:, at] = ffn_in.T
        total = None
        for left in range(0, hidden, columns):
            span = slice(left, left + columns)
            preact = dot(ffn_in, uw_ref[:, span]) + line(ub_ref)[:, span]
            phi, density = normal_parts(preact)
            activated = (preact * phi).astype(BF16)
            act_ref[at, span] = activated
            slope_ref[at, span] = (phi + preact * density).astype(BF16)
            term = dot(activated, dw_ref[span, :])
            total = term if total is None else total + term
        part_ref[at, :] = total + 0.5 * (mid + line(db_ref))


def loss_kernel(
    start, rows, own_ref, got_ref, goal_ref, weight_ref,
    out_ref, og_ref, low_ref, lt_ref, sum_ref,
):
    total = None
    count = own_ref.shape[0]
    for at, at_all in zip(blocks_of(count, rows), range(start, start + count, rows)):
        final = own_ref[at, :] + got_ref[at, :]
        out_ref[at, :] = final.astype(BF16)
        goal = goal_ref[at_all : at_all + rows, :].astype(F32)
        out_grad = (final - goal) * weight_ref[0, 0]
        og_ref[at, :] = out_grad
        low = out_grad.astype(BF16)
        low_ref[at, :] = low
        lt_ref[:, at] = low.T
        term = column_sum(out_grad)
        total = term if total is None else total + term
    sum_ref[...] = total


def back_feed_kernel(
    rows, columns, low_a, low_b, slope_a, slope_b, uw_ref, dw_ref, pre_ref, part_ref, sum_ref
):
    half = low_a.shape[0]
    hidden = uw_ref.shape[1]
    sums = [None] * (hidden // columns)
    for place, (low_ref, slope_ref) in enumerate(((low_a, slope_a), (low_b, slope_b))):
        for at, at_all in zip(blocks_of(half, rows), range(place * half, (place + 1) * half, rows)):
            out_low = low_ref[at, :]
            total = None
            for part in range(hidden // columns):
                span = slice(part * columns, (part + 1) * columns)
                pre_grad = slope_ref[at, span].astype(F32) * dot_nt(out_low, dw_ref[span, :])
                term = column_sum(pre_grad)
                sums[part] = term if sums[part] is None else sums[part] + term
                low = pre_grad.astype(BF16)
                pre_ref[at_all : at_all + rows, span] = low
                term = dot_nt(low, uw_ref[:, span])
                total = term if total is None else total + term
            part_ref[at_all : at_all + rows, :] = total
    sum_ref[...] = jnp.concatenate(sums, axis=1)


def back_mid_kernel(
    rows, mid_a, mid_b, og_a, og_b, own_ref, got_ref, gain_ref, ow_ref,
    mg_ref, mt_ref, mixed_ref, gain_sum_ref, bias_sum_ref, out_sum_ref,
):
    half = mid_a.shape[0]
    sums = [0.0, 0.0, 0.0]
    for place, (mid_ref, og_ref) in enumerate(((mid_a, og_a), (mid_b, og_b))):
        for at, at_all in zip(blocks_of(half, rows), range(place * half, (place + 1) * half, rows)):
            span = slice(at_all, at_all + rows)
            normed, inv_std = normed_of(mid_ref[at, :])
            upstream = own_ref[span, :] + got_ref[span, :]
            mid_grad = og_ref[at, :] + norm_grad(upstream, line(gain_ref), normed, inv_std)
            mg_ref[span, :] = mid_grad
            low = mid_grad.astype(BF16)
            mt_ref[:, span] = low.T
            mixed_ref[span, :] = dot_nt(low, ow_ref[...]).astype(BF16)
            for which, value in enumerate((upstream * normed, upstream, mid_grad)):
                sums[which] = sums[which] + column_sum(value)
    gain_sum_ref[...], bias_sum_ref[...], out_sum_ref[...] = sums


def back_attend_kernel(
    pair, blocks, q_ref, k_ref, v_ref, do_ref, o_ref, lse_ref,
    dq_ref, dk_ref, dv_ref, dq_sum_ref, dv_sum_ref,
):
    scale = 1.0 / math.sqrt(HD)
    lanes = slice(pair * PAIR, (pair + 1) * PAIR)
    half = o_ref.shape[0] // blocks
    keys, values = k_ref[:, lanes], v_ref[:, lanes]
    keys_t = keys.T
    dk, dv, dq_sum = None, None, None
    for place in range(blocks):
        span = slice(place * half, (place + 1) * half)
        queries, upstream = q_ref[span, lanes], do_ref[span, lanes]
        both = (upstream.astype(F32) * o_ref[span, lanes].astype(F32)).T
        pieces = []
        for head in range(2):
            own_queries = keep_head(queries, head)
            own_upstream = keep_head(upstream, head)
            row_dot = column_sum(both[head * HD : (head + 1) * HD])
            log_total = lse_ref[2 * pair + head : 2 * pair + head + 1, span]
            scores = dot_nt(keys, own_queries)
            probs = jnp.exp2(scores * EXP_SCALE - log_total)
            prob_grad = dot_nt(values, own_upstream)
            score_grad = (probs * (prob_grad - row_dot)).astype(BF16)
            dv_term = dot(probs.astype(BF16), own_upstream)
            dk_term = dot(score_grad, own_queries)
            dv = dv_term if dv is None else dv + dv_term
            dk = dk_term if dk is None else dk + dk_term
            pieces.append(dot(keys_t[head * HD : (head + 1) * HD, :], score_grad))
        query_grad = jnp.concatenate(pieces, axis=0).T * scale
        dq_ref[span, :] = query_grad.astype(BF16)
        term = column_sum(query_grad)
        dq_sum = term if dq_sum is None else dq_sum + term
    dk_ref[...] = (dk * scale).astype(BF16)
    dv_ref[...] = dv.astype(BF16)
    dq_sum_ref[...] = dq_sum
    dv_sum_ref[...] = column_sum(dv)


def back_project_kernel(*refs):
    w_ref, part_ref = refs[-2:]
    pairs = (len(refs) - 2) // 3
    total = None
    for kind in range(3):
        grad = jnp.concatenate([refs[3 * pair + kind][...] for pair in range(pairs)], axis=1)
        term = dot_nt(grad, w_ref[kind])
        total = term if total is None else total + term
    part_ref[...] = total


def back_input_kernel(
    rows, x_ref, time_ref, own_ref, got_ref, mg_ref, gain_ref,
    out_ref, time_sum_ref, gain_sum_ref, bias_sum_ref,
):
    sums = [0.0, 0.0, 0.0]
    for at in blocks_of(x_ref.shape[0], rows):
        normed, inv_std = normed_of(x_ref[at, :].astype(F32) + time_ref[...])
        upstream = own_ref[at, :] + got_ref[at, :]
        grad = mg_ref[at, :] + norm_grad(upstream, line(gain_ref), normed, inv_std)
        out_ref[at, :] = grad
        for which, value in enumerate((grad, upstream * normed, upstream)):
            sums[which] = sums[which] + column_sum(value)
    time_sum_ref[...], gain_sum_ref[...], bias_sum_ref[...] = sums


def gathered(refs, start, count):
    return jnp.concatenate([ref[pl.ds(start, count), :] for ref in refs], axis=1)


def stacked(refs, columns, beside):
    return jnp.concatenate([ref[:, columns] for ref in refs], axis=1 if beside else 0)


def weight_kernel(chunk, count, terms, from_ref, *refs):
    keep_ref, send_ref = refs[-2:]
    half = count // 2
    for target, first in ((send_ref, half), (keep_ref, 0)):
        starts = [pl.multiple_of(from_ref[first + place] * chunk, 16) for place in range(half)]
        at, out_at = 0, 0
        for lefts, rights, columns, beside in terms:
            left_refs = refs[at : at + lefts]
            right_refs = refs[at + lefts : at + lefts + rights]
            at += lefts + rights
            left = jnp.concatenate([gathered(left_refs, start, chunk) for start in starts], axis=0)
            right = stacked(right_refs, columns, beside)
            target[:, out_at : out_at + right.shape[1]] = dot(left, right)
            out_at += right.shape[1]


def whole_weight_kernel(terms, *refs):
    at, out_at = 0, 0
    for lefts, rights, columns, beside in terms:
        left = jnp.concatenate([ref[...] for ref in refs[at : at + lefts]], axis=1)
        right = stacked(refs[at + lefts : at + lefts + rights], columns, beside)
        at += lefts + rights
        refs[-1][:, out_at : out_at + right.shape[1]] = dot(left, right)
        out_at += right.shape[1]


def step_kernel(settled, got_places, send_groups, vec_in, vec_out, *refs):
    count = len(settled)
    keeps, refs = refs[:count], refs[count:]
    total_gots = 1 + max(which for which, _ in got_places if which is not None)
    gots, refs = refs[:total_gots], refs[total_gots:]
    vector = None
    if vec_out is not None:
        vector, refs = refs[0][...], refs[1:]
        if vec_in == "other":
            other, refs = refs[0], refs[1:]
            vector = vector + get_vector(other, other.shape[0] - vector_rows(vector.shape, other.shape[1]), vector.shape)
            vec_in = None
    sends, news, refs = refs[: len(send_groups)], refs[len(send_groups) :][:count], refs[len(send_groups) + count :]
    rows, width = keeps[0].shape
    half = rows // 2
    for section, (which, at) in enumerate(got_places):
        total = keeps[section][...]
        if not settled[section]:
            total = total + gots[which][:rows, at * width : (at + 1) * width]
        news[section][...] = total[:half]
        for target, group in zip(sends, send_groups):
            if section in group:
                to = group.index(section) * width
                target[:half, to : to + width] = total[half:]
    if vector is not None:
        if vec_in is not None:
            vector = vector + get_vector(gots[vec_in], rows, vector.shape)
        put_vector(sends[vec_out], half, vector)
        refs[0][...] = vector


def vector_rows(shape, width):
    return 8 * -(-(shape[0] // 8) // (width // shape[1]))


def vector_spots(shape, width):
    each = width // shape[1]
    for block in range(shape[0] // 8):
        row, column = 8 * (block // each), shape[1] * (block % each)
        yield slice(8 * block, 8 * block + 8), slice(row, row + 8), slice(column, column + shape[1])


def put_vector(target, first, vector):
    for own, at, columns in vector_spots(vector.shape, target.shape[1]):
        target[first + at.start : first + at.stop, columns] = vector[own]


def get_vector(source, first, shape):
    parts = []
    for _, at, columns in vector_spots(shape, source.shape[1]):
        parts.append(source[first + at.start : first + at.stop, columns])
    return jnp.concatenate(parts, axis=0)


def store_kernel(value_ref, row_ref, value_out, row_out):
    value_out[...] = value_ref[...]
    row_out[...] = row_ref[...]


def settle_kernel(keep_ref, got_ref, out_ref):
    out_ref[...] = keep_ref[...] + got_ref[...]


def finish_kernel(count, *refs):
    keeps, got_ref, outs = refs[:count], refs[count], refs[count + 1 :]
    width = keeps[0].shape[1]
    share = count // len(outs)
    for place, keep in enumerate(keeps):
        total = keep[...] + got_ref[:, place * width : (place + 1) * width]
        at = (place % share) * width
        outs[place // share][:, at : at + width] = total


def finish_heads_kernel(pair_of, keep_a, keep_b, keep_c, got_ref, vector_ref, qkv_ref, out_ref, *smalls):
    rows, width = keep_a.shape
    for place, keep in enumerate((keep_a, keep_b, keep_c)):
        total = keep[...] + got_ref[:rows, place * width : (place + 1) * width]
        lanes = slice(pair_of[place] * PAIR, (pair_of[place] + 1) * PAIR)
        for kind in range(3):
            qkv_ref[kind, :, lanes] = total[:, kind * PAIR : (kind + 1) * PAIR]
        out_ref[:, lanes] = total[:, 3 * PAIR :]
    unpack(vector_ref[...] + get_vector(got_ref, rows, vector_ref.shape), *smalls)


def pack_kernel(*refs):
    out_ref = refs[-1]
    down_a, down_b, up, gain2, bias2, out, gain1, bias1 = refs[:8]
    model = 2 * out_ref.shape[1]
    wide = up.shape[1] // model
    rows = [out[...], gain2[...], bias2[...], down_a[...] + down_b[...], gain1[...], bias1[...]]
    rows += [up[:, at * model : (at + 1) * model] for at in range(wide)]
    rows.append(jnp.concatenate([ref[...] for ref in refs[8:-1]], axis=1))
    height, half = out_ref.shape[0] // 2, out_ref.shape[1]
    rows.append(jnp.zeros((height - len(rows), 2 * half), F32))
    whole = jnp.concatenate(rows, axis=0)
    out_ref[...] = jnp.concatenate([whole[:, :half], whole[:, half:]], axis=0)


def unpack_kernel(own_ref, got_ref, *outs):
    unpack(own_ref[...] + got_ref[...], *outs)


def unpack(halves, *outs):
    height = halves.shape[0] // 2
    total = jnp.concatenate([halves[:height], halves[height:]], axis=1)
    model = total.shape[1]
    for place in range(6):
        outs[place][...] = total[place]
    wide = outs[6].shape[0] // model
    for at in range(wide):
        outs[6][at * model : (at + 1) * model] = total[6 + at]
    width = outs[7].shape[1]
    last = total[6 + wide : 7 + wide]
    outs[7][...] = jnp.concatenate([last[:, :width], last[:, width : 2 * width]], axis=0)


def held(shape, dtype):
    return pltpu.VMEM(shape, dtype)


def call(name, kernel, args, outs, scratch=(), flops=0, scalars=(), pins=(), plain=()):
    if pins:
        count, inner = len(args), kernel
        kernel = lambda *refs: inner(*refs[:count], *refs[count + len(pins) :])
        args = [*args, *pins]
    whole = pl.BlockSpec(memory_space=pltpu.VMEM)
    specs = [
        pl.BlockSpec(memory_space=pltpu.SMEM) if place in scalars else whole
        for place in range(len(args))
    ]
    args = [
        arg if place in scalars
        else pltpu.with_memory_space_constraint(arg, pltpu.HBM if place in plain else pltpu.VMEM)
        for place, arg in enumerate(args)
    ]
    moved = sum(math.prod(a.shape) * a.dtype.itemsize for a in outs)
    return pl.pallas_call(
        kernel,
        name=name,
        in_specs=specs,
        out_specs=[whole] * len(outs),
        out_shape=outs,
        scratch_shapes=list(scratch),
        compiler_params=pltpu.CompilerParams(vmem_limit_bytes=VMEM_BYTES),
        cost_estimate=pl.CostEstimate(flops=int(flops), bytes_accessed=int(moved), transcendentals=0),
    )(*args)


def after(values, *others):
    return lax.optimization_barrier((values, others))[0]


def swap(value):
    return lax.ppermute(value, "mp", [(0, 1), (1, 0)])


def xor_pairs(size, bit):
    return [(index, index ^ bit) for index in range(size)]


def axis_bits(size):
    return [1 << place for place in range(size.bit_length() - 1)]


def hop(value, bit):
    return lax.ppermute(value, "dp", xor_pairs(lax.axis_size("dp"), bit))


def halve(section, order):
    size = lax.axis_size("dp")
    me = lax.axis_index("dp")
    left = sorted(order, reverse=True)
    rows, columns = section.shape
    section = section.reshape((2,) * len(left) + (rows // size, columns))
    for bit in order:
        at = left.index(bit)
        mine = (me // bit) % 2
        send = lax.dynamic_index_in_dim(section, 1 - mine, at, keepdims=False)
        keep = lax.dynamic_index_in_dim(section, mine, at, keepdims=False)
        section = keep + hop(send, bit)
        left.remove(bit)
    return section


def chunk_sources(order):
    me = lax.axis_index("dp")
    places = []
    for place in range(1 << len(order)):
        relative = 0
        for step, bit in enumerate(order):
            if (place >> (len(order) - 1 - step)) & 1:
                relative |= bit
        places.append(relative)
    return jnp.array(places, jnp.int32) ^ me


class Halving:
    def __init__(self, orders, plan):
        self.orders = orders
        self.plan = list(plan)
        self.keeps = [None] * len(orders)
        self.sends = [None] * len(orders)
        self.gots = []
        self.settled = [False] * len(orders)
        self.vector_at = None

    def start(self, places=None):
        for place, (_, bit) in enumerate(self.plan[0]):
            if places is None or place in places:
                self.gots.append((place, hop(self.sends[place], bit)))

    def settle(self, section, *others):
        which = [place for place, (group, _) in enumerate(self.plan[0]) if group == [section]][0]
        got = dict(self.gots)[which]
        self.gots = [each for each in self.gots if each[0] != which]
        keep, got = after((self.keeps[section], got), *others)
        self.keeps[section] = call("settle", settle_kernel, [keep, got], [held(keep.shape, F32)])[0]
        self.settled[section] = True
        return self.keeps[section]

    def advance(self, *others, vector=None, place=None, other=None, start=True):
        order = sorted(self.gots, key=lambda pair: pair[0])
        gots = after([got for _, got in order], *others)
        count = len(self.keeps)
        places = [(None, None)] * count
        for which, (slot, _) in enumerate(order):
            for at, section in enumerate(self.plan[0][slot][0]):
                places[section] = (which, at)
        vec_in = None
        if self.vector_at is not None:
            vec_in = [slot for slot, _ in order].index(self.vector_at)
        if other is not None:
            vec_in = "other"
        self.plan = self.plan[1:]
        self.gots = []
        groups = [group for group, _ in self.plan[0]]
        rows, width = self.keeps[0].shape
        half = rows // 2
        extra = [0] * len(groups)
        if vector is not None:
            extra[place] = vector_rows(vector.shape, width * len(groups[place]))
        outs = [held((half + more, width * len(group)), F32) for group, more in zip(groups, extra)]
        outs += [held((half, width), F32)] * count
        args = [*self.keeps, *gots]
        if vector is not None:
            args += [vector] if other is None else [vector, other]
            outs.append(held(vector.shape, F32))
        outs = call(
            "halve", functools.partial(step_kernel, self.settled, places, groups, vec_in, place), args, outs
        )
        self.settled = [False] * count
        self.sends, self.keeps = list(outs[: len(groups)]), list(outs[len(groups) :][:count])
        self.vector_at = place
        if start:
            self.start()
        return self.keeps[0] if vector is None else outs[-1]

    def arrived(self):
        return [got for _, got in self.gots]


def two_axes(bits, turned):
    a, b, z, top = bits
    if turned:
        a, b = b, a
    orders = [[a, b, z, top], [b, a, z, top], [z, a, b, top]]
    plan = [
        [([0], a), ([1], b), ([2], z)],
        [([0], b), ([1, 2], a)],
        [([0, 1], z), ([2], b)],
        [([0, 1, 2], top)],
    ]
    return Halving(orders, plan)


def weight_section(name, terms, state, section, order, start=True):
    size = lax.axis_size("dp")
    model = terms[0][0][0].shape[0]
    chunk = model // size
    tokens = sum(left.shape[1] for left in terms[0][0])
    shape = [(len(left), len(right), columns, beside) for left, right, columns, beside in terms]
    width = sum((at.stop - at.start) * (many if beside else 1) for _, many, at, beside in shape)
    flat = [piece for left, right, _, _ in terms for piece in [*left, *right]]
    flops = 2 * model * tokens * width * {'grad_down': LONG_GD, 'grad_up': LONG_GU, 'grad_heads': LONG_GH}[name]
    if state is None:
        whole = call(
            name, functools.partial(whole_weight_kernel, shape), flat,
            [held((model, width), F32)], flops=flops,
        )[0]
        return halve(whole, order)
    keep, send = call(
        name, functools.partial(weight_kernel, chunk, size, shape),
        [chunk_sources(state.orders[section]), *flat], [held((model // 2, width), F32)] * 2,
        flops=flops, scalars=(0,),
    )
    state.keeps[section], state.sends[section] = keep, send
    if start:
        state.start([section])
    return send


def local(
    inputs,
    time_embed,
    targets,
    timesteps,
    ln1_gain,
    ln1_bias,
    qkv_weight,
    qv_bias,
    out_weight,
    out_bias,
    ln2_gain,
    ln2_bias,
    up_weight,
    up_bias,
    down_weight,
    down_bias,
):
    seq_count, length, model = inputs.shape
    width = qkv_weight.shape[2]
    hidden = up_weight.shape[1]
    size = lax.axis_size("dp")
    bits = axis_bits(size)
    halves = 2
    part_rows = length // halves
    pairs = width // PAIR
    x = inputs.reshape(length, model)
    goal = targets.reshape(length, model)
    w_qkv = jnp.transpose(qkv_weight, (1, 0, 2))
    g1, b1, g2, b2 = ln1_gain, ln1_bias, ln2_gain, ln2_bias
    ob, ub, db = out_bias, up_bias, down_bias

    buckets = (
        (timesteps >= NSTEPS // 64).astype(jnp.int32)
        + (timesteps >= NSTEPS // 16).astype(jnp.int32)
        + (timesteps >= NSTEPS // 4).astype(jnp.int32)
    )
    one_hot = buckets[:, None] == jnp.arange(NB, dtype=jnp.int32)[None, :]
    bucket_counts = jnp.sum(one_hot.astype(jnp.int32), axis=0)

    def count_hop(counts, bits):
        for bit in bits:
            counts = counts + hop(counts, bit)
        return counts

    vec = held((1, model), F32)

    def square(rows, dtype):
        return held((rows, model), dtype)

    v, attn_in, attn_t = call(
        "norm", functools.partial(norm_kernel, 256),
        [x, time_embed, g1, b1, w_qkv, qv_bias],
        [held((length, width), BF16), held((length, model), BF16), held((model, length), BF16)],
        flops=2 * length * model * width, plain=range(6),
    )
    attn_in, bucket_counts = lax.optimization_barrier((attn_in, bucket_counts))
    bucket_counts = count_hop(bucket_counts, bits[:1])
    q, k, lengths = call(
        "project", functools.partial(project_kernel, 256),
        [attn_in, w_qkv, qv_bias],
        [held((length, width), BF16)] * 2 + [held((16, 128), F32)],
        flops=4 * length * model * width,
    )

    q, bucket_counts = lax.optimization_barrier((q, bucket_counts))
    bucket_counts = count_hop(bucket_counts, bits[1:2])
    mixed, lse = call(
        "attend", functools.partial(attend_kernel, part_rows),
        [q, k, v, lengths],
        [held((length, width), BF16), held((8, length), F32)],
        scratch=[pltpu.VMEM((2 * width, length), BF16)],
        flops=16 * length * length * width,
    )
    mixed, bucket_counts = lax.optimization_barrier((mixed, bucket_counts))
    bucket_counts = count_hop(bucket_counts, bits[2:])
    own_attn, got_attn = [], []
    for half in range(halves):
        own_attn.append(call(
            "join_heads", functools.partial(join_heads_kernel, half * part_rows), [mixed, out_weight],
            [square(part_rows, F32)], flops=2 * part_rows * width * model,
        )[0])
        got_attn.append(swap(own_attn[half]))
        if half == 0:
            mixed = after(mixed, own_attn[0])
    own_attn[0], bucket_counts = lax.optimization_barrier((own_attn[0], bucket_counts))

    own_feed, mid, feed_t, activated, slope, got_feed = [], [], [], [], [], []
    for half in range(halves):
        outs = call(
            "feed", functools.partial(feed_kernel, half * part_rows, part_rows, hidden),
            [x, time_embed, own_attn[half], got_attn[half], ob, g2, b2, up_weight, ub, down_weight, db],
            [square(part_rows, F32), square(part_rows, F32), held((model, part_rows), BF16),
             held((part_rows, hidden), BF16), held((part_rows, hidden), BF16)],
            flops=4 * length * model * hidden // halves,
            pins=[*mid, *feed_t, *activated, *slope] + [goal] * half,
        )
        for kept, value in zip((own_feed, mid, feed_t, activated, slope), outs):
            kept.append(value)
        got_feed.append(swap(outs[0]))
        if half == 0:
            own_attn[1] = after(own_attn[1], outs[0])

    floors = jnp.maximum(bucket_counts, 1).astype(F32)
    total_seqs = seq_count * size
    seq_weight = total_seqs / (NB * jnp.sum(jnp.where(one_hot, floors[None, :], 0.0), axis=1))
    weight = seq_weight.reshape(1, 1)

    out_act, out_grad, out_low, out_t, down_sums = [], [], [], [], []
    for half in range(halves):
        outs = call(
            "loss", functools.partial(loss_kernel, half * part_rows, 256),
            [own_feed[half], got_feed[half], goal, weight],
            [square(part_rows, BF16), square(part_rows, F32), square(part_rows, BF16),
             held((model, part_rows), BF16), vec],
            scalars=(3,),
        )
        for kept, value in zip((out_act, out_grad, out_low, out_t, down_sums), outs):
            kept.append(value)

    staged = size == 16 and (model // size) % 16 == 0
    down, up, heads = [two_axes(bits, turned) if staged else None for turned in (False, True, True)]
    third = hidden // 3
    thirds = [slice(at * third, (at + 1) * third) for at in range(3)]
    down_parts, up_parts, head_parts = [], [], []
    for section, columns in enumerate(thirds):
        down_parts.append(weight_section("grad_down", [(out_t, activated, columns, False)], down, section, bits))
        activated = after(activated, down_parts[-1])

    out_low = after(out_low, *down_parts)
    pre_low, own_pre, up_sum = call(
        "back_feed", functools.partial(back_feed_kernel, 256, 512),
        [*out_low, *slope, up_weight, down_weight],
        [held((length, hidden), BF16), square(length, F32), held((1, hidden), F32)],
        flops=4 * length * model * hidden * LONG_BF,
    )
    got_pre = swap(own_pre)
    for section, columns in enumerate(thirds):
        up_parts.append(weight_section("grad_up", [(feed_t, [pre_low], columns, False)], up, section, bits))

    got_pre = after(got_pre, *up_parts)
    mid_grad, mid_t, mixed_grad, gain2_sum, bias2_sum, out_sum = call(
        "back_mid", functools.partial(back_mid_kernel, 256),
        [*mid, *out_grad, own_pre, got_pre, g2, out_weight],
        [square(length, F32), held((model, length), BF16), held((length, width), BF16)] + [vec] * 3,
        flops=2 * length * model * width * LONG_BM,
    )
    token = down.advance(out_sum) if staged else out_sum

    grads, sums = [], []
    section_of = [2, 0, 1]

    def head_gradient(pair, others, start=True):
        terms = [
            ([after(attn_t, *others)], grads[3 * pair :], slice(0, PAIR), True),
            ([mid_t], [mixed], slice(pair * PAIR, (pair + 1) * PAIR), False),
        ]
        head_parts.append(weight_section("grad_heads", terms, heads, section_of[pair], bits, start))
        return head_parts[-1]

    for pair in range(pairs):
        one = held((length, PAIR), BF16)
        one_sum = held((1, PAIR), F32)
        mixed_grad = after(mixed_grad, token)
        dq, dk, dv, dq_sum, dv_sum = call(
            "back_attend", functools.partial(back_attend_kernel, pair, halves),
            [q, k, v, mixed_grad, mixed, lse], [one, one, one, one_sum, one_sum],
            flops=40 * length * length * PAIR * LONG_AT,
        )
        grads += [dq, dk, dv]
        sums += [dq_sum, dv_sum]
        token = dq_sum
        if pair < pairs - 1:
            token = head_gradient(pair, [token])
        if staged:
            token = (up, down, up)[pair].advance(token)
            if pair == 1:
                token = heads.settle(section_of[0], token)
            if pair == 2:
                token = down.advance(token)
    grads[0] = after(grads[0], token)
    own_proj = call(
        "back_project", back_project_kernel, [*grads, w_qkv], [square(length, F32)],
        flops=6 * length * model * width * LONG_BP,
    )[0]
    got_proj = swap(own_proj)
    token = head_gradient(pairs - 1, [own_proj])
    got_proj = after(got_proj, token)
    input_grad, grad_time, gain1_sum, bias1_sum = call(
        "back_input", functools.partial(back_input_kernel, 256),
        [x, time_embed, own_proj, got_proj, mid_grad, g1],
        [square(length, F32), vec, vec, vec],
        flops=2 * length * model * width * LONG_BI,
    )
    packed = call(
        "pack", pack_kernel,
        [*down_sums, up_sum, gain2_sum, bias2_sum, out_sum, gain1_sum, bias1_sum,
         *sums[0::2], *sums[1::2]],
        [held((24, model // 2), F32)],
    )[0]

    rows = model // size
    vector = jax.ShapeDtypeStruct((model,), F32)
    small_outs = [vector] * 6
    small_outs += [jax.ShapeDtypeStruct((hidden,), F32), jax.ShapeDtypeStruct((2, width), F32)]
    to_store = [jax.ShapeDtypeStruct((length, model), F32), jax.ShapeDtypeStruct((1, model), F32)]
    if staged:
        packed = packed + hop(packed, bits[2])
        wide = [jax.ShapeDtypeStruct((rows, hidden), F32)]
        finish = functools.partial(finish_kernel, 3)
        down_part = call("finish", finish, [*down.keeps, *after(down.arrived(), packed)], wide)[0]
        token = up.advance(down_part)
        packed = heads.advance(token, vector=packed, place=1)
        stored = list(call("store", store_kernel, [after(input_grad, packed), grad_time], to_store))
        stored[0], packed = lax.optimization_barrier((stored[0], packed))
        up_part = call("finish", finish, [*up.keeps, *after(up.arrived(), packed)], wide)[0]
        packed = heads.advance(up_part, vector=packed, place=1)
        packed = heads.advance(packed, vector=packed, place=0)
        qkv_part, out_part, *small = call(
            "finish_heads",
            functools.partial(finish_heads_kernel, [section_of.index(at) for at in range(3)]),
            [*heads.keeps, *heads.arrived(), packed],
            [jax.ShapeDtypeStruct((3, rows, width), F32), jax.ShapeDtypeStruct((rows, width), F32)]
            + small_outs,
        )
        qkv_part = jnp.transpose(qkv_part, (1, 0, 2))
    else:
        stored = call("store", store_kernel, [input_grad, grad_time], to_store)
        for bit in bits[:-1]:
            packed = packed + hop(packed, bit)
        small = call("unpack", unpack_kernel, [packed, hop(packed, bits[-1])], small_outs)
        down_part = jnp.concatenate(down_parts, axis=1)
        up_part = jnp.concatenate(up_parts, axis=1)
        split = 3 * PAIR
        qkv_part = jnp.concatenate([p[:, :split].reshape(rows, 3, PAIR) for p in head_parts], axis=2)
        out_part = jnp.concatenate([p[:, split:] for p in head_parts], axis=1)
    out_sum, gain2_sum, bias2_sum, down_sum, gain1_sum, bias1_sum, up_sum, qv_sum = small
    input_grad, grad_time = stored

    return (
        jnp.concatenate(out_act, axis=0).reshape(inputs.shape),
        input_grad.reshape(inputs.shape),
        grad_time,
        gain1_sum,
        bias1_sum,
        qkv_part,
        qv_sum,
        out_part.T,
        out_sum,
        gain2_sum,
        bias2_sum,
        up_part,
        up_sum,
        down_part.T,
        down_sum,
        bucket_counts,
    )


def solution(mesh):
    in_specs = (
        P("dp", None, None),
        P("dp", None),
        P("dp", None, None),
        P("dp"),
        P(),
        P(),
        P(None, None, "mp"),
        P(None, "mp"),
        P("mp", None),
        P(),
        P(),
        P(),
        P(None, "mp"),
        P("mp"),
        P("mp", None),
        P(),
    )
    out_specs = (
        P("dp", None, None),
        P("dp", None, None),
        P("dp", None),
        P(),
        P(),
        P("dp", None, "mp"),
        P(None, "mp"),
        P("mp", "dp"),
        P(),
        P(),
        P(),
        P("dp", "mp"),
        P("mp"),
        P("mp", "dp"),
        P(),
        P(),
    )
    return jax.shard_map(local, mesh=mesh, in_specs=in_specs, out_specs=out_specs, check_vma=False)
```

```python
import functools
import math

import jax
import jax.numpy as jnp
from jax import lax
from jax.experimental import pallas as pl
from jax.experimental.pallas import tpu as pltpu
from jax.sharding import PartitionSpec as P

HD = 64
NSTEPS = 2000
NB = 4
PAIR = 2 * HD
VMEM_BYTES = 14 * 2**20
LONG_BF = LONG_BM = LONG_BP = LONG_BI = LONG_GD = 1
LONG_AT = LONG_GU = LONG_GH = 20
LONG_LAST = 20

epsilon = 1e-05
F32 = jnp.float32
BF16 = jnp.bfloat16
NT = (((1,), (1,)), ((), ()))
EXP_SCALE = math.log2(math.e) / math.sqrt(HD)
SCORE_LIMIT = 60.0


def dot(left, right):
    return jnp.dot(left, right, preferred_element_type=F32)


def dot_nt(left, right):
    return lax.dot_general(left, right, NT, preferred_element_type=F32)


def line(ref):
    return ref[...].reshape(1, -1)


def row_mean(value):
    return jnp.mean(value, axis=-1, keepdims=True)


def column_sum(value):
    return jnp.sum(value, axis=0, keepdims=True)


def normed_of(source):
    centred = source - row_mean(source)
    inv_std = lax.rsqrt(row_mean(centred * centred) + epsilon)
    return centred * inv_std, inv_std


def norm_grad(upstream, gain, normed, inv_std):
    scaled = upstream * gain
    inner = scaled - row_mean(scaled) - normed * row_mean(scaled * normed)
    return inv_std * inner


def head_mask(shape, head):
    lane = lax.broadcasted_iota(jnp.int32, shape, 1)
    return (lane >= HD) if head else (lane < HD)


def keep_head(value, head):
    return jnp.where(head_mask(value.shape, head), value, jnp.zeros_like(value))


def blocks_of(count, size):
    return [pl.ds(start, size) for start in range(0, count, size)]


def norm_kernel(rows, x_ref, time_ref, gain_ref, bias_ref, w_ref, qvb_ref, v_ref, in_ref, at_ref):
    for at in blocks_of(x_ref.shape[0], rows):
        residual = x_ref[at, :].astype(F32) + time_ref[...]
        normed, _ = normed_of(residual)
        attn_in = (normed * line(gain_ref) + line(bias_ref)).astype(BF16)
        in_ref[at, :] = attn_in
        at_ref[:, at] = attn_in.T
        v_ref[at, :] = (dot(attn_in, w_ref[2]) + qvb_ref[1:2]).astype(BF16)


def project_kernel(rows, in_ref, w_ref, qvb_ref, q_ref, k_ref, norm_ref):
    width = q_ref.shape[1]
    lane = lax.broadcasted_iota(jnp.int32, (width, 128), 0)
    column = lax.broadcasted_iota(jnp.int32, (width, 128), 1)
    pick = jnp.where(lane // HD == column, 1.0, 0.0).astype(BF16)
    longest = [None, None]
    for at in blocks_of(in_ref.shape[0], rows):
        attn_in = in_ref[at, :]
        queries = dot(attn_in, w_ref[0]) + qvb_ref[0:1]
        keys = dot(attn_in, w_ref[1])
        q_ref[at, :] = queries.astype(BF16)
        k_ref[at, :] = keys.astype(BF16)
        for place, value in enumerate((queries, keys)):
            top = jnp.max(dot((value * value).astype(BF16), pick), axis=0, keepdims=True)
            longest[place] = top if longest[place] is None else jnp.maximum(longest[place], top)
    norm_ref[...] = jnp.concatenate([jnp.broadcast_to(each, (8, 128)) for each in longest], axis=0)


def attend_kernel(rows, q_ref, k_ref, v_ref, norm_ref, mixed_ref, lse_ref, vt_ref):
    length, width = k_ref.shape
    pairs = width // PAIR
    for pair in range(pairs):
        turned = v_ref[:, pair * PAIR : (pair + 1) * PAIR].T
        for head in range(2):
            at = (2 * pair + head) * PAIR
            vt_ref[at : at + HD, :] = turned[head * HD : (head + 1) * HD]
            vt_ref[at + HD : at + PAIR, :] = jnp.ones((HD, length), BF16)

    def attend(place, count, shift):
        at_own = pl.ds(pl.multiple_of(place * count, count), count)
        pieces, stats = [], []
        for pair in range(pairs):
            lanes = slice(pair * PAIR, (pair + 1) * PAIR)
            keys = k_ref[:, lanes]
            queries = q_ref[at_own, lanes]
            for head in range(2):
                scores = dot_nt(keys, keep_head(queries, head))
                if shift:
                    top = jnp.max(scores, axis=0, keepdims=True)
                    expo = jnp.exp2((scores - top) * EXP_SCALE)
                else:
                    expo = jnp.exp2(scores * EXP_SCALE)
                at = (2 * pair + head) * PAIR
                both = dot(vt_ref[at : at + PAIR, :], expo.astype(BF16))
                total = both[HD : HD + 1]
                pieces.append(both[:HD] * (1.0 / total))
                stat = jnp.log2(total)
                stats.append(stat + top * EXP_SCALE if shift else stat)
        while len(stats) < lse_ref.shape[0]:
            stats.append(jnp.zeros_like(stats[0]))
        lse_ref[:, at_own] = jnp.concatenate(stats, axis=0)
        mixed_ref[at_own, :] = jnp.concatenate(pieces, axis=0).T.astype(BF16)

    bound = jnp.max(norm_ref[0:8, :] * norm_ref[8:16, :]) * (1.1 / HD)
    small = bound < SCORE_LIMIT * SCORE_LIMIT

    @pl.when(small)
    def _():
        @pl.loop(0, length // rows)
        def _(place):
            attend(place, rows, False)

    @pl.when(jnp.logical_not(small))
    def _():
        @pl.loop(0, length // 128)
        def _(place):
            attend(place, 128, True)


def join_heads_kernel(start, mixed_ref, ow_ref, part_ref):
    part_ref[...] = dot(mixed_ref[start : start + part_ref.shape[0], :], ow_ref[...])


def normal_parts(v):
    size = jnp.abs(v)
    t = 1.0 / (1.0 + 0.2316419 * size)
    poly = t * (
        0.319381530
        + t * (-0.356563782 + t * (1.781477937 + t * (-1.821255978 + t * 1.330274429)))
    )
    density = jnp.exp2(v * v * (-0.5 * math.log2(math.e))) * (1.0 / math.sqrt(2.0 * math.pi))
    tail = poly * density
    return jnp.where(v < 0.0, tail, 1.0 - tail), density


def feed_kernel(
    start, rows, columns, x_ref, time_ref, own_ref, got_ref, ob_ref, gain_ref, bias_ref, uw_ref,
    ub_ref, dw_ref, db_ref, part_ref, mid_ref, ft_ref, act_ref, slope_ref,
):
    count = own_ref.shape[0]
    hidden = uw_ref.shape[1]
    for at, at_all in zip(blocks_of(count, rows), range(start, start + count, rows)):
        mid = (
            x_ref[at_all : at_all + rows, :].astype(F32)
            + time_ref[...]
            + (own_ref[at, :] + got_ref[at, :])
            + line(ob_ref)
        )
        mid_ref[at, :] = mid
        normed, _ = normed_of(mid)
        ffn_in = (normed * line(gain_ref) + line(bias_ref)).astype(BF16)
        ft_ref[:, at] = ffn_in.T
        total = None
        for left in range(0, hidden, columns):
            span = slice(left, left + columns)
            preact = dot(ffn_in, uw_ref[:, span]) + line(ub_ref)[:, span]
            phi, density = normal_parts(preact)
            activated = (preact * phi).astype(BF16)
            act_ref[at, span] = activated
            slope_ref[at, span] = (phi + preact * density).astype(BF16)
            term = dot(activated, dw_ref[span, :])
            total = term if total is None else total + term
        part_ref[at, :] = total + 0.5 * (mid + line(db_ref))


def loss_kernel(
    start, rows, own_ref, got_ref, goal_ref, weight_ref,
    out_ref, og_ref, low_ref, lt_ref, sum_ref,
):
    total = None
    count = own_ref.shape[0]
    for at, at_all in zip(blocks_of(count, rows), range(start, start + count, rows)):
        final = own_ref[at, :] + got_ref[at, :]
        out_ref[at, :] = final.astype(BF16)
        goal = goal_ref[at_all : at_all + rows, :].astype(F32)
        out_grad = (final - goal) * weight_ref[0, 0]
        og_ref[at, :] = out_grad
        low = out_grad.astype(BF16)
        low_ref[at, :] = low
        lt_ref[:, at] = low.T
        term = column_sum(out_grad)
        total = term if total is None else total + term
    sum_ref[...] = total


def back_feed_kernel(
    rows, columns, low_a, low_b, slope_a, slope_b, uw_ref, dw_ref, pre_ref, part_ref, sum_ref
):
    half = low_a.shape[0]
    hidden = uw_ref.shape[1]
    sums = [None] * (hidden // columns)
    for place, (low_ref, slope_ref) in enumerate(((low_a, slope_a), (low_b, slope_b))):
        for at, at_all in zip(blocks_of(half, rows), range(place * half, (place + 1) * half, rows)):
            out_low = low_ref[at, :]
            total = None
            for part in range(hidden // columns):
                span = slice(part * columns, (part + 1) * columns)
                pre_grad = slope_ref[at, span].astype(F32) * dot_nt(out_low, dw_ref[span, :])
                term = column_sum(pre_grad)
                sums[part] = term if sums[part] is None else sums[part] + term
                low = pre_grad.astype(BF16)
                pre_ref[at_all : at_all + rows, span] = low
                term = dot_nt(low, uw_ref[:, span])
                total = term if total is None else total + term
            part_ref[at_all : at_all + rows, :] = total
    sum_ref[...] = jnp.concatenate(sums, axis=1)


def back_mid_kernel(
    rows, mid_a, mid_b, og_a, og_b, own_ref, got_ref, gain_ref, ow_ref,
    mg_ref, mt_ref, mixed_ref, gain_sum_ref, bias_sum_ref, out_sum_ref,
):
    half = mid_a.shape[0]
    sums = [0.0, 0.0, 0.0]
    for place, (mid_ref, og_ref) in enumerate(((mid_a, og_a), (mid_b, og_b))):
        for at, at_all in zip(blocks_of(half, rows), range(place * half, (place + 1) * half, rows)):
            span = slice(at_all, at_all + rows)
            normed, inv_std = normed_of(mid_ref[at, :])
            upstream = own_ref[span, :] + got_ref[span, :]
            mid_grad = og_ref[at, :] + norm_grad(upstream, line(gain_ref), normed, inv_std)
            mg_ref[span, :] = mid_grad
            low = mid_grad.astype(BF16)
            mt_ref[:, span] = low.T
            mixed_ref[span, :] = dot_nt(low, ow_ref[...]).astype(BF16)
            for which, value in enumerate((upstream * normed, upstream, mid_grad)):
                sums[which] = sums[which] + column_sum(value)
    gain_sum_ref[...], bias_sum_ref[...], out_sum_ref[...] = sums


def back_attend_kernel(
    pair, blocks, q_ref, k_ref, v_ref, do_ref, o_ref, lse_ref,
    dq_ref, dk_ref, dv_ref, dq_sum_ref, dv_sum_ref,
):
    scale = 1.0 / math.sqrt(HD)
    lanes = slice(pair * PAIR, (pair + 1) * PAIR)
    half = o_ref.shape[0] // blocks
    keys, values = k_ref[:, lanes], v_ref[:, lanes]
    keys_t = keys.T
    dk, dv, dq_sum = None, None, None
    for place in range(blocks):
        span = slice(place * half, (place + 1) * half)
        queries, upstream = q_ref[span, lanes], do_ref[span, lanes]
        both = (upstream.astype(F32) * o_ref[span, lanes].astype(F32)).T
        pieces = []
        for head in range(2):
            own_queries = keep_head(queries, head)
            own_upstream = keep_head(upstream, head)
            row_dot = column_sum(both[head * HD : (head + 1) * HD])
            log_total = lse_ref[2 * pair + head : 2 * pair + head + 1, span]
            scores = dot_nt(keys, own_queries)
            probs = jnp.exp2(scores * EXP_SCALE - log_total)
            prob_grad = dot_nt(values, own_upstream)
            score_grad = (probs * (prob_grad - row_dot)).astype(BF16)
            dv_term = dot(probs.astype(BF16), own_upstream)
            dk_term = dot(score_grad, own_queries)
            dv = dv_term if dv is None else dv + dv_term
            dk = dk_term if dk is None else dk + dk_term
            pieces.append(dot(keys_t[head * HD : (head + 1) * HD, :], score_grad))
        query_grad = jnp.concatenate(pieces, axis=0).T * scale
        dq_ref[span, :] = query_grad.astype(BF16)
        term = column_sum(query_grad)
        dq_sum = term if dq_sum is None else dq_sum + term
    dk_ref[...] = (dk * scale).astype(BF16)
    dv_ref[...] = dv.astype(BF16)
    dq_sum_ref[...] = dq_sum
    dv_sum_ref[...] = column_sum(dv)


def back_project_kernel(*refs):
    w_ref, part_ref = refs[-2:]
    pairs = (len(refs) - 2) // 3
    total = None
    for kind in range(3):
        grad = jnp.concatenate([refs[3 * pair + kind][...] for pair in range(pairs)], axis=1)
        term = dot_nt(grad, w_ref[kind])
        total = term if total is None else total + term
    part_ref[...] = total


def back_input_kernel(
    rows, x_ref, time_ref, own_ref, got_ref, mg_ref, gain_ref,
    out_ref, time_sum_ref, gain_sum_ref, bias_sum_ref,
):
    sums = [0.0, 0.0, 0.0]
    for at in blocks_of(x_ref.shape[0], rows):
        normed, inv_std = normed_of(x_ref[at, :].astype(F32) + time_ref[...])
        upstream = own_ref[at, :] + got_ref[at, :]
        grad = mg_ref[at, :] + norm_grad(upstream, line(gain_ref), normed, inv_std)
        out_ref[at, :] = grad
        for which, value in enumerate((grad, upstream * normed, upstream)):
            sums[which] = sums[which] + column_sum(value)
    time_sum_ref[...], gain_sum_ref[...], bias_sum_ref[...] = sums


def gathered(refs, start, count):
    return jnp.concatenate([ref[pl.ds(start, count), :] for ref in refs], axis=1)


def stacked(refs, columns, beside):
    return jnp.concatenate([ref[:, columns] for ref in refs], axis=1 if beside else 0)


def weight_kernel(chunk, count, terms, from_ref, *refs):
    keep_ref, send_ref = refs[-2:]
    half = count // 2
    for target, first in ((send_ref, half), (keep_ref, 0)):
        starts = [pl.multiple_of(from_ref[first + place] * chunk, 16) for place in range(half)]
        at, out_at = 0, 0
        for lefts, rights, columns, beside in terms:
            left_refs = refs[at : at + lefts]
            right_refs = refs[at + lefts : at + lefts + rights]
            at += lefts + rights
            left = jnp.concatenate([gathered(left_refs, start, chunk) for start in starts], axis=0)
            right = stacked(right_refs, columns, beside)
            target[:, out_at : out_at + right.shape[1]] = dot(left, right)
            out_at += right.shape[1]


def whole_weight_kernel(terms, *refs):
    at, out_at = 0, 0
    for lefts, rights, columns, beside in terms:
        left = jnp.concatenate([ref[...] for ref in refs[at : at + lefts]], axis=1)
        right = stacked(refs[at + lefts : at + lefts + rights], columns, beside)
        at += lefts + rights
        refs[-1][:, out_at : out_at + right.shape[1]] = dot(left, right)
        out_at += right.shape[1]


def step_kernel(settled, got_places, send_groups, vec_in, vec_out, *refs):
    count = len(settled)
    keeps, refs = refs[:count], refs[count:]
    total_gots = 1 + max(which for which, _ in got_places if which is not None)
    gots, refs = refs[:total_gots], refs[total_gots:]
    vector = None
    if vec_out is not None:
        vector, refs = refs[0][...], refs[1:]
        if vec_in == "other":
            other, refs = refs[0], refs[1:]
            vector = vector + get_vector(other, other.shape[0] - vector_rows(vector.shape, other.shape[1]), vector.shape)
            vec_in = None
    sends, news, refs = refs[: len(send_groups)], refs[len(send_groups) :][:count], refs[len(send_groups) + count :]
    rows, width = keeps[0].shape
    half = rows // 2
    for section, (which, at) in enumerate(got_places):
        total = keeps[section][...]
        if not settled[section]:
            total = total + gots[which][:rows, at * width : (at + 1) * width]
        news[section][...] = total[:half]
        for target, group in zip(sends, send_groups):
            if section in group:
                to = group.index(section) * width
                target[:half, to : to + width] = total[half:]
    if vector is not None:
        if vec_in is not None:
            vector = vector + get_vector(gots[vec_in], rows, vector.shape)
        put_vector(sends[vec_out], half, vector)
        refs[0][...] = vector


def vector_rows(shape, width):
    return 8 * -(-(shape[0] // 8) // (width // shape[1]))


def vector_spots(shape, width):
    each = width // shape[1]
    for block in range(shape[0] // 8):
        row, column = 8 * (block // each), shape[1] * (block % each)
        yield slice(8 * block, 8 * block + 8), slice(row, row + 8), slice(column, column + shape[1])


def put_vector(target, first, vector):
    for own, at, columns in vector_spots(vector.shape, target.shape[1]):
        target[first + at.start : first + at.stop, columns] = vector[own]


def get_vector(source, first, shape):
    parts = []
    for _, at, columns in vector_spots(shape, source.shape[1]):
        parts.append(source[first + at.start : first + at.stop, columns])
    return jnp.concatenate(parts, axis=0)


def store_kernel(value_ref, row_ref, value_out, row_out):
    value_out[...] = value_ref[...]
    row_out[...] = row_ref[...]


def settle_kernel(keep_ref, got_ref, out_ref):
    out_ref[...] = keep_ref[...] + got_ref[...]


def finish_kernel(count, *refs):
    keeps, got_ref, outs = refs[:count], refs[count], refs[count + 1 :]
    width = keeps[0].shape[1]
    share = count // len(outs)
    for place, keep in enumerate(keeps):
        total = keep[...] + got_ref[:, place * width : (place + 1) * width]
        at = (place % share) * width
        outs[place // share][:, at : at + width] = total


def finish_heads_kernel(pair_of, keep_a, keep_b, keep_c, got_ref, vector_ref, qkv_ref, out_ref, *smalls):
    rows, width = keep_a.shape
    for place, keep in enumerate((keep_a, keep_b, keep_c)):
        total = keep[...] + got_ref[:rows, place * width : (place + 1) * width]
        lanes = slice(pair_of[place] * PAIR, (pair_of[place] + 1) * PAIR)
        for kind in range(3):
            qkv_ref[kind, :, lanes] = total[:, kind * PAIR : (kind + 1) * PAIR]
        out_ref[:, lanes] = total[:, 3 * PAIR :]
    unpack(vector_ref[...] + get_vector(got_ref, rows, vector_ref.shape), *smalls)


def pack_kernel(*refs):
    out_ref = refs[-1]
    down_a, down_b, up, gain2, bias2, out, gain1, bias1 = refs[:8]
    model = 2 * out_ref.shape[1]
    wide = up.shape[1] // model
    rows = [out[...], gain2[...], bias2[...], down_a[...] + down_b[...], gain1[...], bias1[...]]
    rows += [up[:, at * model : (at + 1) * model] for at in range(wide)]
    rows.append(jnp.concatenate([ref[...] for ref in refs[8:-1]], axis=1))
    height, half = out_ref.shape[0] // 2, out_ref.shape[1]
    rows.append(jnp.zeros((height - len(rows), 2 * half), F32))
    whole = jnp.concatenate(rows, axis=0)
    out_ref[...] = jnp.concatenate([whole[:, :half], whole[:, half:]], axis=0)


def unpack_kernel(own_ref, got_ref, *outs):
    unpack(own_ref[...] + got_ref[...], *outs)


def unpack(halves, *outs):
    height = halves.shape[0] // 2
    total = jnp.concatenate([halves[:height], halves[height:]], axis=1)
    model = total.shape[1]
    for place in range(6):
        outs[place][...] = total[place]
    wide = outs[6].shape[0] // model
    for at in range(wide):
        outs[6][at * model : (at + 1) * model] = total[6 + at]
    width = outs[7].shape[1]
    last = total[6 + wide : 7 + wide]
    outs[7][...] = jnp.concatenate([last[:, :width], last[:, width : 2 * width]], axis=0)


def held(shape, dtype):
    return pltpu.VMEM(shape, dtype)


def call(name, kernel, args, outs, scratch=(), flops=0, scalars=(), pins=(), plain=()):
    if pins:
        count, inner = len(args), kernel
        kernel = lambda *refs: inner(*refs[:count], *refs[count + len(pins) :])
        args = [*args, *pins]
    whole = pl.BlockSpec(memory_space=pltpu.VMEM)
    specs = [
        pl.BlockSpec(memory_space=pltpu.SMEM) if place in scalars else whole
        for place in range(len(args))
    ]
    args = [
        arg if place in scalars
        else pltpu.with_memory_space_constraint(arg, pltpu.HBM if place in plain else pltpu.VMEM)
        for place, arg in enumerate(args)
    ]
    moved = sum(math.prod(a.shape) * a.dtype.itemsize for a in outs)
    return pl.pallas_call(
        kernel,
        name=name,
        in_specs=specs,
        out_specs=[whole] * len(outs),
        out_shape=outs,
        scratch_shapes=list(scratch),
        compiler_params=pltpu.CompilerParams(vmem_limit_bytes=VMEM_BYTES),
        cost_estimate=pl.CostEstimate(flops=int(flops), bytes_accessed=int(moved), transcendentals=0),
    )(*args)


def after(values, *others):
    return lax.optimization_barrier((values, others))[0]


def swap(value):
    return lax.ppermute(value, "mp", [(0, 1), (1, 0)])


def xor_pairs(size, bit):
    return [(index, index ^ bit) for index in range(size)]


def axis_bits(size):
    return [1 << place for place in range(size.bit_length() - 1)]


def hop(value, bit):
    return lax.ppermute(value, "dp", xor_pairs(lax.axis_size("dp"), bit))


def halve(section, order):
    size = lax.axis_size("dp")
    me = lax.axis_index("dp")
    left = sorted(order, reverse=True)
    rows, columns = section.shape
    section = section.reshape((2,) * len(left) + (rows // size, columns))
    for bit in order:
        at = left.index(bit)
        mine = (me // bit) % 2
        send = lax.dynamic_index_in_dim(section, 1 - mine, at, keepdims=False)
        keep = lax.dynamic_index_in_dim(section, mine, at, keepdims=False)
        section = keep + hop(send, bit)
        left.remove(bit)
    return section


def chunk_sources(order):
    me = lax.axis_index("dp")
    places = []
    for place in range(1 << len(order)):
        relative = 0
        for step, bit in enumerate(order):
            if (place >> (len(order) - 1 - step)) & 1:
                relative |= bit
        places.append(relative)
    return jnp.array(places, jnp.int32) ^ me


class Halving:
    def __init__(self, orders, plan):
        self.orders = orders
        self.plan = list(plan)
        self.keeps = [None] * len(orders)
        self.sends = [None] * len(orders)
        self.gots = []
        self.settled = [False] * len(orders)
        self.vector_at = None

    def start(self, places=None):
        for place, (_, bit) in enumerate(self.plan[0]):
            if places is None or place in places:
                self.gots.append((place, hop(self.sends[place], bit)))

    def settle(self, section, *others):
        which = [place for place, (group, _) in enumerate(self.plan[0]) if group == [section]][0]
        got = dict(self.gots)[which]
        self.gots = [each for each in self.gots if each[0] != which]
        keep, got = after((self.keeps[section], got), *others)
        self.keeps[section] = call("settle", settle_kernel, [keep, got], [held(keep.shape, F32)])[0]
        self.settled[section] = True
        return self.keeps[section]

    def advance(self, *others, vector=None, place=None, other=None, start=True):
        order = sorted(self.gots, key=lambda pair: pair[0])
        gots = after([got for _, got in order], *others)
        count = len(self.keeps)
        places = [(None, None)] * count
        for which, (slot, _) in enumerate(order):
            for at, section in enumerate(self.plan[0][slot][0]):
                places[section] = (which, at)
        vec_in = None
        if self.vector_at is not None:
            vec_in = [slot for slot, _ in order].index(self.vector_at)
        if other is not None:
            vec_in = "other"
        self.plan = self.plan[1:]
        self.gots = []
        groups = [group for group, _ in self.plan[0]]
        rows, width = self.keeps[0].shape
        half = rows // 2
        extra = [0] * len(groups)
        if vector is not None:
            extra[place] = vector_rows(vector.shape, width * len(groups[place]))
        outs = [held((half + more, width * len(group)), F32) for group, more in zip(groups, extra)]
        outs += [held((half, width), F32)] * count
        args = [*self.keeps, *gots]
        if vector is not None:
            args += [vector] if other is None else [vector, other]
            outs.append(held(vector.shape, F32))
        outs = call(
            "halve", functools.partial(step_kernel, self.settled, places, groups, vec_in, place), args, outs
        )
        self.settled = [False] * count
        self.sends, self.keeps = list(outs[: len(groups)]), list(outs[len(groups) :][:count])
        self.vector_at = place
        if start:
            self.start()
        return self.keeps[0] if vector is None else outs[-1]

    def arrived(self):
        return [got for _, got in self.gots]


def two_axes(bits, turned):
    a, b, z, top = bits
    if turned:
        a, b = b, a
    orders = [[a, b, z, top], [b, a, z, top], [z, a, b, top]]
    plan = [
        [([0], a), ([1], b), ([2], z)],
        [([0], b), ([1, 2], a)],
        [([0, 1], z), ([2], b)],
        [([0, 1, 2], top)],
    ]
    return Halving(orders, plan)


def weight_section(name, terms, state, section, order, start=True):
    size = lax.axis_size("dp")
    model = terms[0][0][0].shape[0]
    chunk = model // size
    tokens = sum(left.shape[1] for left in terms[0][0])
    shape = [(len(left), len(right), columns, beside) for left, right, columns, beside in terms]
    width = sum((at.stop - at.start) * (many if beside else 1) for _, many, at, beside in shape)
    flat = [piece for left, right, _, _ in terms for piece in [*left, *right]]
    flops = 2 * model * tokens * width * {'grad_down': LONG_GD, 'grad_up': LONG_GU, 'grad_heads': LONG_GH}[name]
    if state is None:
        whole = call(
            name, functools.partial(whole_weight_kernel, shape), flat,
            [held((model, width), F32)], flops=flops,
        )[0]
        return halve(whole, order)
    keep, send = call(
        name, functools.partial(weight_kernel, chunk, size, shape),
        [chunk_sources(state.orders[section]), *flat], [held((model // 2, width), F32)] * 2,
        flops=flops, scalars=(0,),
    )
    state.keeps[section], state.sends[section] = keep, send
    if start:
        state.start([section])
    return send


def local(
    inputs,
    time_embed,
    targets,
    timesteps,
    ln1_gain,
    ln1_bias,
    qkv_weight,
    qv_bias,
    out_weight,
    out_bias,
    ln2_gain,
    ln2_bias,
    up_weight,
    up_bias,
    down_weight,
    down_bias,
):
    seq_count, length, model = inputs.shape
    width = qkv_weight.shape[2]
    hidden = up_weight.shape[1]
    size = lax.axis_size("dp")
    bits = axis_bits(size)
    halves = 2
    part_rows = length // halves
    pairs = width // PAIR
    x = inputs.reshape(length, model)
    goal = targets.reshape(length, model)
    w_qkv = jnp.transpose(qkv_weight, (1, 0, 2))
    g1, b1, g2, b2 = ln1_gain, ln1_bias, ln2_gain, ln2_bias
    ob, ub, db = out_bias, up_bias, down_bias

    buckets = (
        (timesteps >= NSTEPS // 64).astype(jnp.int32)
        + (timesteps >= NSTEPS // 16).astype(jnp.int32)
        + (timesteps >= NSTEPS // 4).astype(jnp.int32)
    )
    one_hot = buckets[:, None] == jnp.arange(NB, dtype=jnp.int32)[None, :]
    bucket_counts = jnp.sum(one_hot.astype(jnp.int32), axis=0)

    def count_hop(counts, bits):
        for bit in bits:
            counts = counts + hop(counts, bit)
        return counts

    vec = held((1, model), F32)

    def square(rows, dtype):
        return held((rows, model), dtype)

    v, attn_in, attn_t = call(
        "norm", functools.partial(norm_kernel, part_rows),
        [x, time_embed, g1, b1, w_qkv, qv_bias],
        [held((length, width), BF16), held((length, model), BF16), held((model, length), BF16)],
        flops=2 * length * model * width, plain=range(6),
    )
    attn_in, bucket_counts = lax.optimization_barrier((attn_in, bucket_counts))
    bucket_counts = count_hop(bucket_counts, bits[:1])
    q, k, lengths = call(
        "project", functools.partial(project_kernel, part_rows),
        [attn_in, w_qkv, qv_bias],
        [held((length, width), BF16)] * 2 + [held((16, 128), F32)],
        flops=4 * length * model * width,
    )

    q, bucket_counts = lax.optimization_barrier((q, bucket_counts))
    bucket_counts = count_hop(bucket_counts, bits[1:2])
    mixed, lse = call(
        "attend", functools.partial(attend_kernel, part_rows),
        [q, k, v, lengths],
        [held((length, width), BF16), held((8, length), F32)],
        scratch=[pltpu.VMEM((2 * width, length), BF16)],
        flops=16 * length * length * width,
    )
    mixed, bucket_counts = lax.optimization_barrier((mixed, bucket_counts))
    bucket_counts = count_hop(bucket_counts, bits[2:])
    own_attn, got_attn = [], []
    for half in range(halves):
        own_attn.append(call(
            "join_heads", functools.partial(join_heads_kernel, half * part_rows), [mixed, out_weight],
            [square(part_rows, F32)], flops=2 * part_rows * width * model,
        )[0])
        got_attn.append(swap(own_attn[half]))
        if half == 0:
            mixed = after(mixed, own_attn[0])
    own_attn[0], bucket_counts = lax.optimization_barrier((own_attn[0], bucket_counts))

    own_feed, mid, feed_t, activated, slope, got_feed = [], [], [], [], [], []
    for half in range(halves):
        outs = call(
            "feed", functools.partial(feed_kernel, half * part_rows, part_rows, hidden),
            [x, time_embed, own_attn[half], got_attn[half], ob, g2, b2, up_weight, ub, down_weight, db],
            [square(part_rows, F32), square(part_rows, F32), held((model, part_rows), BF16),
             held((part_rows, hidden), BF16), held((part_rows, hidden), BF16)],
            flops=4 * length * model * hidden // halves,
            pins=[*mid, *feed_t, *activated, *slope] + [goal] * half,
        )
        for kept, value in zip((own_feed, mid, feed_t, activated, slope), outs):
            kept.append(value)
        got_feed.append(swap(outs[0]))
        if half == 0:
            own_attn[1] = after(own_attn[1], outs[0])

    floors = jnp.maximum(bucket_counts, 1).astype(F32)
    total_seqs = seq_count * size
    seq_weight = total_seqs / (NB * jnp.sum(jnp.where(one_hot, floors[None, :], 0.0), axis=1))
    weight = seq_weight.reshape(1, 1)

    out_act, out_grad, out_low, out_t, down_sums = [], [], [], [], []
    for half in range(halves):
        outs = call(
            "loss", functools.partial(loss_kernel, half * part_rows, part_rows),
            [own_feed[half], got_feed[half], goal, weight],
            [square(part_rows, BF16), square(part_rows, F32), square(part_rows, BF16),
             held((model, part_rows), BF16), vec],
            scalars=(3,),
        )
        for kept, value in zip((out_act, out_grad, out_low, out_t, down_sums), outs):
            kept.append(value)

    staged = size == 16 and (model // size) % 16 == 0
    down, up, heads = [two_axes(bits, turned) if staged else None for turned in (False, True, True)]
    third = hidden // 3
    thirds = [slice(at * third, (at + 1) * third) for at in range(3)]
    down_parts, up_parts, head_parts = [], [], []
    for section, columns in enumerate(thirds):
        down_parts.append(weight_section("grad_down", [(out_t, activated, columns, False)], down, section, bits))
        activated = after(activated, down_parts[-1])

    out_low = after(out_low, *down_parts)
    pre_low, own_pre, up_sum = call(
        "back_feed", functools.partial(back_feed_kernel, part_rows, hidden),
        [*out_low, *slope, up_weight, down_weight],
        [held((length, hidden), BF16), square(length, F32), held((1, hidden), F32)],
        flops=4 * length * model * hidden * LONG_BF,
    )
    got_pre = swap(own_pre)
    for section, columns in enumerate(thirds):
        up_parts.append(weight_section("grad_up", [(feed_t, [pre_low], columns, False)], up, section, bits))

    got_pre = after(got_pre, *up_parts)
    mid_grad, mid_t, mixed_grad, gain2_sum, bias2_sum, out_sum = call(
        "back_mid", functools.partial(back_mid_kernel, part_rows),
        [*mid, *out_grad, own_pre, got_pre, g2, out_weight],
        [square(length, F32), held((model, length), BF16), held((length, width), BF16)] + [vec] * 3,
        flops=2 * length * model * width * LONG_BM,
    )
    token = down.advance(out_sum) if staged else out_sum

    grads, sums = [], []
    section_of = [2, 0, 1]

    def head_gradient(pair, others, start=True):
        terms = [
            ([after(attn_t, *others)], grads[3 * pair :], slice(0, PAIR), True),
            ([mid_t], [mixed], slice(pair * PAIR, (pair + 1) * PAIR), False),
        ]
        head_parts.append(weight_section("grad_heads", terms, heads, section_of[pair], bits, start))
        return head_parts[-1]

    for pair in range(pairs):
        one = held((length, PAIR), BF16)
        one_sum = held((1, PAIR), F32)
        mixed_grad = after(mixed_grad, token)
        dq, dk, dv, dq_sum, dv_sum = call(
            "back_attend", functools.partial(back_attend_kernel, pair, halves),
            [q, k, v, mixed_grad, mixed, lse], [one, one, one, one_sum, one_sum],
            flops=40 * length * length * PAIR * LONG_AT,
        )
        grads += [dq, dk, dv]
        sums += [dq_sum, dv_sum]
        token = dq_sum
        if pair < pairs - 1:
            token = head_gradient(pair, [token])
        if staged:
            token = (up, down, up)[pair].advance(token)
            if pair == 1:
                token = heads.settle(section_of[0], token)
            if pair == 2:
                token = down.advance(token)
    grads[0] = after(grads[0], token)
    own_proj = call(
        "back_project", back_project_kernel, [*grads, w_qkv], [square(length, F32)],
        flops=6 * length * model * width * LONG_BP,
    )[0]
    got_proj = swap(own_proj)
    token = head_gradient(pairs - 1, [own_proj])
    got_proj = after(got_proj, token)
    input_grad, grad_time, gain1_sum, bias1_sum = call(
        "back_input", functools.partial(back_input_kernel, part_rows),
        [x, time_embed, own_proj, got_proj, mid_grad, g1],
        [square(length, F32), vec, vec, vec],
        flops=2 * length * model * width * LONG_BI,
    )
    packed = call(
        "pack", pack_kernel,
        [*down_sums, up_sum, gain2_sum, bias2_sum, out_sum, gain1_sum, bias1_sum,
         *sums[0::2], *sums[1::2]],
        [held((24, model // 2), F32)],
    )[0]

    rows = model // size
    vector = jax.ShapeDtypeStruct((model,), F32)
    small_outs = [vector] * 6
    small_outs += [jax.ShapeDtypeStruct((hidden,), F32), jax.ShapeDtypeStruct((2, width), F32)]
    to_store = [jax.ShapeDtypeStruct((length, model), F32), jax.ShapeDtypeStruct((1, model), F32)]
    if staged:
        packed = packed + hop(packed, bits[2])
        wide = [jax.ShapeDtypeStruct((rows, hidden), F32)]
        finish = functools.partial(finish_kernel, 3)
        down_part = call("finish", finish, [*down.keeps, *after(down.arrived(), packed)], wide)[0]
        token = up.advance(down_part)
        packed = heads.advance(token, vector=packed, place=1)
        stored = list(call("store", store_kernel, [after(input_grad, packed), grad_time], to_store))
        stored[0], packed = lax.optimization_barrier((stored[0], packed))
        up_part = call("finish", finish, [*up.keeps, *after(up.arrived(), packed)], wide)[0]
        packed = heads.advance(up_part, vector=packed, place=1)
        packed = heads.advance(packed, vector=packed, place=0)
        qkv_part, out_part, *small = call(
            "finish_heads",
            functools.partial(finish_heads_kernel, [section_of.index(at) for at in range(3)]),
            [*heads.keeps, *heads.arrived(), packed],
            [jax.ShapeDtypeStruct((3, rows, width), F32), jax.ShapeDtypeStruct((rows, width), F32)]
            + small_outs,
        )
        qkv_part = jnp.transpose(qkv_part, (1, 0, 2))
    else:
        stored = call("store", store_kernel, [input_grad, grad_time], to_store)
        for bit in bits[:-1]:
            packed = packed + hop(packed, bit)
        small = call("unpack", unpack_kernel, [packed, hop(packed, bits[-1])], small_outs)
        down_part = jnp.concatenate(down_parts, axis=1)
        up_part = jnp.concatenate(up_parts, axis=1)
        split = 3 * PAIR
        qkv_part = jnp.concatenate([p[:, :split].reshape(rows, 3, PAIR) for p in head_parts], axis=2)
        out_part = jnp.concatenate([p[:, split:] for p in head_parts], axis=1)
    out_sum, gain2_sum, bias2_sum, down_sum, gain1_sum, bias1_sum, up_sum, qv_sum = small
    input_grad, grad_time = stored

    return (
        jnp.concatenate(out_act, axis=0).reshape(inputs.shape),
        input_grad.reshape(inputs.shape),
        grad_time,
        gain1_sum,
        bias1_sum,
        qkv_part,
        qv_sum,
        out_part.T,
        out_sum,
        gain2_sum,
        bias2_sum,
        up_part,
        up_sum,
        down_part.T,
        down_sum,
        bucket_counts,
    )


def solution(mesh):
    in_specs = (
        P("dp", None, None),
        P("dp", None),
        P("dp", None, None),
        P("dp"),
        P(),
        P(),
        P(None, None, "mp"),
        P(None, "mp"),
        P("mp", None),
        P(),
        P(),
        P(),
        P(None, "mp"),
        P("mp"),
        P("mp", None),
        P(),
    )
    out_specs = (
        P("dp", None, None),
        P("dp", None, None),
        P("dp", None),
        P(),
        P(),
        P("dp", None, "mp"),
        P(None, "mp"),
        P("mp", "dp"),
        P(),
        P(),
        P(),
        P("dp", "mp"),
        P("mp"),
        P("mp", "dp"),
        P(),
        P(),
    )
    return jax.shard_map(local, mesh=mesh, in_specs=in_specs, out_specs=out_specs, check_vma=False)
```
